128 devices in a mesh: row: 4 (over y_hi, core), col: 32 (over x, z, y_lo).
Axes of the slice: x: 4, y: 4 (y_hi: 2, y_lo: 2; y = y_hi * 2 + y_lo), z: 4, core: 2. Of those that a mesh axis runs over, the one named last changes fastest.
Arguments:
- inputs: bfloat16 [1024, 8192], P(('row', 'col')), may hold values from -6 to 6
- layer_norm_gain: float32 [8192], replicated, may hold values from 0.1 to 1.9
- w_in: bfloat16 [8192, 16384], P('row', 'col'), may hold values from -0.09375 to 0.09375
- w_out: bfloat16 [16384, 8192], P('col', 'row'), may hold values from -0.0625 to 0.0625
- pattern_in: int32 [64, 16], replicated, may hold values from 0 to 31, as said below
- pattern_out: int32 [32, 32], replicated, may hold values from 0 to 63, as said below
- out_grad: bfloat16 [1024, 8192], P(('row', 'col')), may hold values from -6 to 6
Outputs:
- output: bfloat16 [1024, 8192], P(('row', 'col'))
- grad_inputs: bfloat16 [1024, 8192], P(('row', 'col'))
- grad_w_in: bfloat16 [8192, 16384], P('row', 'col')
- grad_w_out: bfloat16 [16384, 8192], P('col', 'row')
- norm_gain_gradient: float32 [8192], replicated
The draws below stay inside these ranges and needn't reach their ends.
Inputs may be any that keep to these rules, and one draw needn't show every extreme that they name: `pattern_in`: each row lists 8192 / 512 different tile rows in increasing order. `pattern_out`: each row lists 16384 / 512 different tile rows in increasing order.
All inputs are finite; a program needn't handle non-finite values.
Results may differ from the reference program's by a relative error of at most 0.022.
Values may be sent and summed in bfloat16 or wider, within the bound.
A program may use at most 128 MiB of HBM per device.

```python
import jax
import jax.numpy as jnp
from jax import lax

D = 8192
FF = 16384
BLOCK = 256
TOKENS = 1024
N_ROW = 4
N_COL = 32


def kept_rows(key, columns, tile_rows):
    keys = jax.random.split(key, columns)
    orders = jax.vmap(lambda k: jax.random.permutation(k, tile_rows))(keys)
    return jnp.sort(orders[:, :tile_rows // 2], axis=1).astype(jnp.int32)


def draw_pattern_in(key, part):
    return kept_rows(jax.random.fold_in(key, 11), FF // BLOCK, D // BLOCK)


def draw_pattern_out(key, part):
    return kept_rows(jax.random.fold_in(key, 23), D // BLOCK, FF // BLOCK)


def block_scale(own_key, shape, shards, low, high):
    loudness = 1.0
    for position, shards_of in shards:
        heights = jax.random.uniform(jax.random.fold_in(jax.random.fold_in(own_key, 6), position), (shards_of,), jnp.float32, low / len(shards), high / len(shards))
        loudness = loudness * jnp.repeat(jnp.exp(heights), shape[position] // shards_of).reshape((-1,) + (1,) * (len(shape) - 1 - position))
    return loudness


def gaussian(rng, extent, scale, most, cuts=(), held_as=jnp.bfloat16):
    loudness = block_scale(rng, extent, cuts, -0.22, 0.18) if cuts else 1.0
    array = jax.random.normal(rng, extent, jnp.float32) * scale * loudness
    return jnp.minimum(jnp.maximum(array, -most), most).astype(held_as)


def setup_inputs(seed: int = 0) -> dict:
    key_list = jax.random.split(jax.random.key(seed), 8)
    inputs = gaussian(key_list[0], (TOKENS, D), 1.0, 6.0, ((0, 128),))
    layer_norm_gain = jnp.clip(1.0 + 0.18 * jax.random.normal(key_list[1], (D,), jnp.float32), 0.1, 1.9)
    w_in = gaussian(key_list[2], (D, FF), (D // 2) ** -0.5, 0.09375, ((0, 4), (1, 32)))
    w_out = gaussian(key_list[3], (FF, D), (FF // 2) ** -0.5, 0.0625, ((0, 32), (1, 4)))
    pattern_in = draw_pattern_in(jax.random.fold_in(key_list[7], 71), 0)
    pattern_out = draw_pattern_out(jax.random.fold_in(key_list[7], 71), 0)
    out_grad = gaussian(key_list[6], (TOKENS, D), 1.0, 6.0, ((0, 128),))
    return dict(inputs=inputs, layer_norm_gain=layer_norm_gain, w_in=w_in, w_out=w_out, pattern_in=pattern_in, pattern_out=pattern_out, out_grad=out_grad)


def block_mask(pattern, tile_rows):
    iota = jnp.arange(tile_rows, dtype=jnp.int32)
    return jnp.any(pattern[None, :, :] == iota[:, None, None], axis=2)

def apply_mask(weight, mask):
    rows_t, cols_t = mask.shape
    shaped = weight.reshape(rows_t, BLOCK, cols_t, BLOCK)
    kept = jnp.where(mask[:, None, :, None], shaped, jnp.zeros((), weight.dtype))
    return kept.reshape(weight.shape)

def gelu_value(h):
    inner = 0.7978845608 * (h + 0.044715 * h * h * h)
    return 0.5 * h * (1.0 + jnp.tanh(inner))

def gelu_slope(h):
    tanh_v = jnp.tanh(0.7978845608 * (h + 0.044715 * h * h * h))
    return 0.5 * (1.0 + tanh_v) + 0.5 * h * (1.0 - tanh_v * tanh_v) * 0.7978845608 * (1.0 + 0.134145 * h * h)

def rounded(value):
    return lax.optimization_barrier(value.astype(jnp.bfloat16)).astype(jnp.float32)

def reference(inputs, layer_norm_gain, w_in, w_out, pattern_in, pattern_out, out_grad):
    xfloat = inputs.astype(jnp.float32)
    centered_input = xfloat - lax.optimization_barrier(jnp.mean(xfloat, axis=1, keepdims=True))
    inverse_deviation = lax.rsqrt(lax.optimization_barrier(jnp.mean(centered_input * centered_input, axis=1, keepdims=True)) + 1e-05)
    standardized_input = centered_input * inverse_deviation
    normalized_input = (standardized_input * layer_norm_gain[None, :]).astype(jnp.bfloat16)
    w_in_e = apply_mask(w_in, block_mask(pattern_in, D // BLOCK))
    mask_out = block_mask(pattern_out, FF // BLOCK)
    w_out_e = apply_mask(w_out, mask_out)
    mask_in = block_mask(pattern_in, D // BLOCK)
    pre = jnp.dot(normalized_input, w_in_e, preferred_element_type=jnp.float32)
    activation = gelu_value(pre).astype(jnp.bfloat16)
    hidden_group = FF // N_COL

    def out_step(running, group):
        part_a = lax.dynamic_slice_in_dim(activation, group * hidden_group, hidden_group, 1)
        part_w = lax.dynamic_slice_in_dim(w_out_e, group * hidden_group, hidden_group, 0)
        return (running + rounded(jnp.dot(part_a, part_w, preferred_element_type=jnp.float32)), None)
    summed, _ = lax.scan(out_step, jnp.zeros((TOKENS, D), jnp.float32), jnp.arange(N_COL, dtype=jnp.int32))
    output = (xfloat + summed).astype(jnp.bfloat16)
    d_act = jnp.dot(out_grad, w_out_e.T, preferred_element_type=jnp.float32)
    d_pre = (d_act * gelu_slope(pre)).astype(jnp.bfloat16)
    panel_size = TOKENS // N_ROW

    def w2_step(running, group):
        part_a = lax.dynamic_slice_in_dim(activation, group * panel_size, panel_size, 0)
        part_g = lax.dynamic_slice_in_dim(out_grad, group * panel_size, panel_size, 0)
        return (running + rounded(jnp.dot(part_a.T, part_g, preferred_element_type=jnp.float32)), None)
    w2_sum, _ = lax.scan(w2_step, jnp.zeros((FF, D), jnp.float32), jnp.arange(N_ROW, dtype=jnp.int32))
    grad_w_out = apply_mask(w2_sum.astype(jnp.bfloat16), mask_out)

    def w1_step(running, group):
        part_x = lax.dynamic_slice_in_dim(normalized_input, group * panel_size, panel_size, 0)
        part_d = lax.dynamic_slice_in_dim(d_pre, group * panel_size, panel_size, 0)
        return (running + rounded(jnp.dot(part_x.T, part_d, preferred_element_type=jnp.float32)), None)
    w1_sum, _ = lax.scan(w1_step, jnp.zeros((D, FF), jnp.float32), jnp.arange(N_ROW, dtype=jnp.int32))
    grad_w_in = apply_mask(w1_sum.astype(jnp.bfloat16), mask_in)

    def dx_step(running, group):
        part_d = lax.dynamic_slice_in_dim(d_pre, group * hidden_group, hidden_group, 1)
        part_w = lax.dynamic_slice_in_dim(w_in_e, group * hidden_group, hidden_group, 1)
        return (running + rounded(jnp.dot(part_d, part_w.T, preferred_element_type=jnp.float32)), None)
    normed_gradient, _ = lax.scan(dx_step, jnp.zeros((TOKENS, D), jnp.float32), jnp.arange(N_COL, dtype=jnp.int32))
    norm_gain_gradient = lax.optimization_barrier(jnp.sum(normed_gradient * standardized_input, axis=0))
    gain_scaled = normed_gradient * layer_norm_gain[None, :]
    backward_result = inverse_deviation * (gain_scaled - lax.optimization_barrier(jnp.mean(gain_scaled, axis=1, keepdims=True)) - standardized_input * lax.optimization_barrier(jnp.mean(gain_scaled * standardized_input, axis=1, keepdims=True)))
    grad_inputs = (out_grad.astype(jnp.float32) + backward_result).astype(jnp.bfloat16)
    return (output, grad_inputs, grad_w_in, grad_w_out, norm_gain_gradient)
```

```python
import functools

import jax
import jax.numpy as jnp
from jax import lax
from jax.experimental import pallas as pl
from jax.experimental.pallas import tpu as pltpu
from jax.sharding import PartitionSpec as P

BLOCK = 256
BF = jnp.bfloat16
F32 = jnp.float32
N_COPIES = 192


def gelu_value(h):
    inner = 0.7978845608 * (h + 0.044715 * h * h * h)
    return 0.5 * h * (1.0 + jnp.tanh(inner))


def gelu_slope(h):
    tanh_v = jnp.tanh(0.7978845608 * (h + 0.044715 * h * h * h))
    return 0.5 * (1.0 + tanh_v) + 0.5 * h * (1.0 - tanh_v * tanh_v) * 0.7978845608 * (
        1.0 + 0.134145 * h * h
    )


def dot_nn(a, b):
    return lax.dot_general(a, b, (((1,), (0,)), ((), ())), preferred_element_type=F32)


def dot_nt(a, b):
    return lax.dot_general(a, b, (((1,), (1,)), ((), ())), preferred_element_type=F32)


def dot_tn(a, b):
    return lax.dot_general(a, b, (((0,), (0,)), ((), ())), preferred_element_type=F32)


def kernel(
    x_ref, gain_ref, gain64_ref, og_ref, win_hbm, wout_hbm, min_ref, mout_ref,
    out_ref, gin_ref, gwin_ref, gwout_ref, gg_ref,
    win, wout, normed, s0x, s0g, gx, gg,
    ar_send, ar_recv, ay_send, ay_recv, acc, act, dpre,
    rs_far, rs_half, rs_full, rs_in, rs_own,
    ru_far, ru_half, ru_full, ru_in,
    rfin, e_buf, gw1, gw2, s_x, s_z, s_c,
    send_sem, recv_sem, w_sem,
):
    row = lax.axis_index("row")
    col = lax.axis_index("col")
    xi, zi, yl = col // 8, (col // 2) % 4, col % 2
    yh, core = row // 2, row % 2
    q = row * 2 + yl

    def dev(x, z, qq):
        return (qq // 2, (x * 4 + z) * 2 + qq % 2)

    used = [0]

    def copy(src, dst, to):
        i = used[0]
        used[0] += 1
        c = pltpu.make_async_remote_copy(
            src_ref=src, dst_ref=dst, send_sem=send_sem.at[i], recv_sem=recv_sem.at[i],
            device_id=to, device_id_type=pl.DeviceIdType.MESH,
        )
        sent.append(c)
        return c

    sent = []

    def go(src, dst, to):
        c = copy(src, dst, to)
        c.start()
        return c

    def step(i, n):
        return (i + n + 4) % 4

    sibling = (yh * 2 + (1 - core), col)
    partner = ((1 - yh) * 2 + core, col)

    w_in_copy = pltpu.make_async_copy(win_hbm, win, w_sem.at[0])
    w_out_copy = pltpu.make_async_copy(wout_hbm, wout, w_sem.at[1])
    w_in_copy.start()
    w_out_copy.start()

    barrier = pltpu.get_barrier_semaphore()
    peers = [dev(step(xi, n), zi, q) for n in (1, 2, 3)]
    peers += [dev(xi, step(zi, n), q) for n in (1, 2, 3)]
    peers += [dev(xi, zi, (q + n) % 8) for n in range(1, 8)]
    for p in peers:
        pl.semaphore_signal(barrier, inc=1, device_id=p, device_id_type=pl.DeviceIdType.MESH)

    xf = x_ref[...].astype(F32)
    cen = xf - jnp.mean(xf, axis=1, keepdims=True)
    inv = lax.rsqrt(jnp.mean(cen * cen, axis=1, keepdims=True) + 1e-05)
    nrm = (cen * inv * gain_ref[...]).astype(BF)
    for r in range(4):
        normed[r] = nrm[:, r * 2048 : (r + 1) * 2048]
    pl.semaphore_wait(barrier, len(peers))

    def column_in(src_of, dst):
        cs = []
        for n in range(1, 8):
            qq = (q + n) % 8
            cs.append(go(src_of(qq), dst.at[q], dev(xi, zi, qq)))
        return cs

    c0x = column_in(lambda qq: normed.at[qq // 2], s0x)
    c0g = column_in(
        lambda qq: og_ref.at[:, pl.ds(pl.multiple_of((qq // 2) * 2048, 2048), 2048)], s0g
    )
    s0x[q] = normed[row]
    s0g[q] = og_ref[:, pl.ds(pl.multiple_of(row * 2048, 2048), 2048)]

    w_in_copy.wait()
    for t in range(8):
        win[t * 256 : (t + 1) * 256] = win[t * 256 : (t + 1) * 256] * min_ref[t : t + 1].astype(BF)
    w_out_copy.wait()
    for t in range(2):
        wout[t * 256 : (t + 1) * 256] = wout[t * 256 : (t + 1) * 256] * mout_ref[t : t + 1].astype(BF)

    def blk(g, k, u, v):
        return g.at[0, v, u] if k == 0 else g.at[1, u, v]

    def gather(s0, g, arrived):
        for c in arrived:
            c.wait_recv()
        block = s0[...].reshape(64, 2048)
        g[0, xi, zi] = block[:, :1024]
        g[1, xi, zi] = block[:, 1024:]
        st = []
        for k in range(2):
            u0, v0 = (zi, xi) if k == 0 else (xi, zi)

            def to_u(n, k=k):
                return dev(xi, step(zi, n), q) if k == 0 else dev(step(xi, n), zi, q)

            def to_v(n, k=k):
                return dev(step(xi, n), zi, q) if k == 0 else dev(xi, step(zi, n), q)

            st.append(dict(k=k, u0=u0, v0=v0, to_u=to_u, to_v=to_v))

        def both(s, u, v, to):
            b = blk(g, s["k"], u, v)
            return {n: go(b, b, to(n)) for n in (1, -1)}

        for s in st:
            s["f"] = both(s, s["u0"], s["v0"], s["to_u"])
            s["s"] = {0: both(s, s["u0"], s["v0"], s["to_v"])}
            s["f2"], s["s2"] = {}, []
        yield
        for n in (1, -1):
            for s in st:
                s["f"][n].wait_recv()
                u = step(s["u0"], -n)
                b = blk(g, s["k"], u, s["v0"])
                part = b.at[pl.ds(0, 32)] if n == 1 else b.at[pl.ds(32, 32)]
                s["f2"][n] = go(part, part, s["to_u"](n))
                s["s"][-n] = both(s, u, s["v0"], s["to_v"])
            yield
        for n in (1, -1):
            for s in st:
                s["s"][0][n].wait_recv()
                if n == 1:
                    b = blk(g, s["k"], s["u0"], step(s["v0"], -n))
                    s["s2"].append(go(b, b, s["to_v"](n)))
        for s in st:
            s["f2"][1].wait_recv()
            s["f2"][-1].wait_recv()
            s["s"][2] = both(s, step(s["u0"], 2), s["v0"], s["to_v"])
        yield
        for off in (-1, 1):
            for n in (1, -1):
                for s in st:
                    s["s"][off][n].wait_recv()
                    if n == off:
                        b = blk(g, s["k"], step(s["u0"], off), step(s["v0"], -n))
                        s["s2"].append(go(b, b, s["to_v"](n)))
            yield
        for n in (1, -1):
            for s in st:
                s["s"][2][n].wait_recv()
                if n == -1:
                    b = blk(g, s["k"], step(s["u0"], 2), step(s["v0"], -n))
                    s["s2"].append(go(b, b, s["to_v"](n)))
        yield
        for s in st:
            for c in s["s2"]:
                c.wait_recv()

    def drain(g, n=None):
        for i, _ in enumerate(g):
            if n is not None and i + 1 >= n:
                return

    gen_x = gather(s0x, gx, c0x)
    gen_g = gather(s0g, gg, c0g)
    drain(gen_x, 1)
    drain(gen_g, 1)
    for _ in range(3):
        drain(gen_x, 1)
        drain(gen_g, 1)
    drain(gen_x)

    def partial(g, w, nt, xx):
        a = g[0, xx].reshape(256, 1024)
        b = g[1, xx].reshape(256, 1024)
        if nt:
            return dot_nt(a, w[:, :1024]) + dot_nt(b, w[:, 1024:])
        return dot_nn(a, w[:1024]) + dot_nn(b, w[1024:])

    def row_sum_a(i, g, w, nt):
        def other(j, _):
            ar_send[i, j] = partial(g, w, nt, 2 * (1 - core) + j).astype(BF)
            return 0

        lax.fori_loop(0, 2, other, 0)
        return go(ar_send.at[i], ar_recv.at[i], sibling)

    def row_sum_b(i, g, w, nt, c):
        def mine(j, _):
            acc[i, j] = partial(g, w, nt, 2 * core + j)
            return 0

        lax.fori_loop(0, 2, mine, 0)
        c.wait_recv()

        def add(j, _):
            v = acc[i, j] + ar_recv[i, j].astype(F32)
            acc[i, j] = v
            ay_send[i, j] = v.astype(BF)
            return 0

        lax.fori_loop(0, 2, add, 0)
        return go(ay_send.at[i], ay_recv.at[i], partner)

    def rows_loop(f):
        def body(j, _):
            h, m = j // 4, j % 4
            f(h, m, pl.ds(pl.multiple_of(m * 64, 64), 64))
            return 0

        lax.fori_loop(0, 8, body, 0)

    ca = row_sum_a(0, gx, win, False)
    drain(gen_g, 1)
    cb = row_sum_b(0, gx, win, False, ca)
    drain(gen_g)
    ca1 = row_sum_a(1, gg, wout, True)
    cb.wait_recv()

    def act_rows(h, m, rows):
        pre = acc[0, h, rows] + ay_recv[0, h, rows].astype(F32)
        acc[0, h, rows] = pre
        act[2 * core + h, m] = gelu_value(pre).astype(BF)

    rows_loop(act_rows)
    mine2 = pl.ds(2 * core, 2)
    cc = go(act.at[mine2], act.at[mine2], sibling)
    cb1 = row_sum_b(1, gg, wout, True, ca1)

    def term(t, k, v):
        if t == 0:
            a = act[v] if k == 0 else act[:, v]
            return dot_nn(a.reshape(256, 512), wout[:, k * 1024 : (k + 1) * 1024])
        a = dpre[v] if k == 0 else dpre[:, v]
        return dot_nt(a.reshape(256, 512), win[k * 1024 : (k + 1) * 1024, :])

    def scatter(t):
        st = []
        for k in range(2):
            u0, v0 = (zi, xi) if k == 0 else (xi, zi)

            def to_u(n, k=k):
                return dev(xi, step(zi, n), q) if k == 0 else dev(step(xi, n), zi, q)

            def to_v(n, k=k):
                return dev(step(xi, n), zi, q) if k == 0 else dev(xi, step(zi, n), q)

            st.append(dict(k=k, u0=u0, v0=v0, to_u=to_u, to_v=to_v))
        for s in st:
            k = s["k"]
            rs_far[t, k] = term(t, k, step(s["v0"], 2)).astype(BF).reshape(4, 64, 1024)
            s["h"] = {
                n: go(
                    rs_far.at[t, k, pl.ds(0 if n == 1 else 2, 2)],
                    rs_half.at[t, k, 0 if n == 1 else 1],
                    s["to_v"](n),
                )
                for n in (1, -1)
            }
        yield
        for n in (1, -1):
            for s in st:
                k = s["k"]
                j = 0 if n == 1 else 1
                p = term(t, k, step(s["v0"], n)).reshape(4, 64, 1024)
                s["h"][n].wait_recv()
                lo, hi = p[0:2], p[2:4]
                extra = rs_half[t, k, j].astype(F32)
                if n == 1:
                    lo = lo + extra
                else:
                    hi = hi + extra
                rs_full[t, k, j, 0:2] = lo.astype(BF)
                rs_full[t, k, j, 2:4] = hi.astype(BF)
                s.setdefault("w", {})[n] = go(
                    rs_full.at[t, k, j], rs_in.at[t, k, j], s["to_v"](n)
                )
            yield
        for s in st:
            k = s["k"]
            rs_own[k] = term(t, k, s["v0"]).reshape(4, 64, 1024)
        yield
        for s in st:
            k = s["k"]
            s["w"][1].wait_recv()
            s["w"][-1].wait_recv()

            def summed(u, k=k):
                return (
                    rs_own[k, u]
                    + rs_in[t, k, 0, u].astype(F32)
                    + rs_in[t, k, 1, u].astype(F32)
                )

            s["sum"] = summed
            ru_far[t, k] = summed(step(s["u0"], 2)).astype(BF)
            s["uh"] = {
                n: go(
                    ru_far.at[t, k, pl.ds(0 if n == 1 else 32, 32)],
                    ru_half.at[t, k, 0 if n == 1 else 1],
                    s["to_u"](n),
                )
                for n in (1, -1)
            }
        yield
        for n in (1, -1):
            for s in st:
                k = s["k"]
                j = 0 if n == 1 else 1
                p = s["sum"](step(s["u0"], n))
                s["uh"][n].wait_recv()
                extra = ru_half[t, k, j].astype(F32)
                lo, hi = p[0:32], p[32:64]
                if n == 1:
                    lo = lo + extra
                else:
                    hi = hi + extra
                ru_full[t, k, j, 0:32] = lo.astype(BF)
                ru_full[t, k, j, 32:64] = hi.astype(BF)
                s.setdefault("uw", {})[n] = go(
                    ru_full.at[t, k, j], ru_in.at[t, k, j], s["to_u"](n)
                )
        yield
        for s in st:
            k = s["k"]
            s["uw"][1].wait_recv()
            s["uw"][-1].wait_recv()
            r = s["sum"](s["u0"]) + ru_in[t, k, 0].astype(F32) + ru_in[t, k, 1].astype(F32)
            rfin[t, :, :, k * 1024 : (k + 1) * 1024] = r.astype(BF).reshape(8, 8, 1024)
        cs = []
        for n in range(1, 8):
            qq = (q + n) % 8
            cs.append(go(rfin.at[t, qq], e_buf.at[t, q], dev(xi, zi, qq)))
        e_buf[t, q] = rfin[t, q]
        last[t] = cs

    last = {}
    cc.wait_recv()
    gen_o = scatter(0)
    drain(gen_o, 1)
    drain(gen_o, 2)
    cb1.wait_recv()

    def dpre_rows(h, m, rows):
        d = acc[1, h, rows] + ay_recv[1, h, rows].astype(F32)
        dpre[2 * core + h, m] = (d * gelu_slope(acc[0, h, rows])).astype(BF)

    rows_loop(dpre_rows)
    cd = go(dpre.at[mine2], dpre.at[mine2], sibling)
    drain(gen_o, 1)
    cd.wait_recv()
    drain(gen_o)
    gen_d = scatter(1)
    drain(gen_d, 1)
    drain(gen_d, 2)

    ones = jnp.ones((8, 512), BF)
    for k in range(2):

        def win_tile(j, _, k=k):
            lanes = pl.ds(pl.multiple_of(j * 256, 256), 256)
            ft = k * 4 + j
            a = gx[k, :, :, :, lanes].reshape(1024, 256)
            raw = dot_tn(a, dpre[...].reshape(1024, 512))
            rows = pl.ds(pl.multiple_of(ft * 256, 256), 256)
            gw1[rows] = (raw * min_ref[pl.ds(ft, 1)]).astype(BF)
            p = raw * win[rows].astype(F32)
            hi = p.astype(BF)
            lo = (p - hi.astype(F32)).astype(BF)
            s = dot_nt(ones, hi) + dot_nt(ones, lo)
            s_x[xi, pl.ds(2 * ft, 1)] = s[0:1, :128]
            s_x[xi, pl.ds(2 * ft + 1, 1)] = s[0:1, 128:]
            return 0

        lax.fori_loop(0, 4, win_tile, 0)
    o1 = pltpu.make_async_copy(gw1, gwin_ref, w_sem.at[0])
    o1.start()
    sx = [go(s_x.at[xi], s_x.at[xi], dev(step(xi, n), zi, q)) for n in (1, 2, 3)]
    drain(gen_d, 1)
    for k in range(2):

        def wout_tile(j, _, k=k):
            lanes = pl.ds(pl.multiple_of(j * 256, 256), 256)
            b = gg[k, :, :, :, lanes].reshape(1024, 256)
            raw = dot_tn(act[...].reshape(1024, 512), b)
            cols = pl.ds(pl.multiple_of(k * 1024 + j * 256, 256), 256)
            for h in range(2):
                gw2[h * 256 : (h + 1) * 256, cols] = (
                    raw[h * 256 : (h + 1) * 256] * mout_ref[h : h + 1, cols]
                ).astype(BF)
            return 0

        lax.fori_loop(0, 4, wout_tile, 0)
    o2 = pltpu.make_async_copy(gw2, gwout_ref, w_sem.at[1])
    o2.start()
    for c in sx:
        c.wait_recv()
    s_z[zi] = (s_x[0] + s_x[1]) + (s_x[2] + s_x[3])
    sz = [go(s_z.at[zi], s_z.at[zi], dev(xi, step(zi, n), q)) for n in (1, 2, 3)]
    drain(gen_d, 1)
    for c in sz:
        c.wait_recv()
    s_c[q] = (s_z[0] + s_z[1]) + (s_z[2] + s_z[3])
    sc = [go(s_c.at[q], s_c.at[q], dev(xi, zi, (q + n) % 8)) for n in range(1, 8)]
    drain(gen_d)

    for c in last[0]:
        c.wait_recv()
    for r in range(4):
        f = slice(r * 2048, (r + 1) * 2048)
        o = e_buf[0, 2 * r].astype(F32) + e_buf[0, 2 * r + 1].astype(F32)
        out_ref[:, f] = (x_ref[:, f].astype(F32) + o).astype(BF)
    for c in sc:
        c.wait_recv()
    for r in range(4):
        gg_ref[r * 16 : (r + 1) * 16] = (s_c[2 * r] + s_c[2 * r + 1]) / gain64_ref[r * 16 : (r + 1) * 16]

    for c in last[1]:
        c.wait_recv()
    parts = [
        e_buf[1, 2 * r].astype(F32) + e_buf[1, 2 * r + 1].astype(F32) for r in range(4)
    ]
    d = jnp.concatenate(parts, axis=1)
    xf = x_ref[...].astype(F32)
    cen = xf - jnp.mean(xf, axis=1, keepdims=True)
    inv = lax.rsqrt(jnp.mean(cen * cen, axis=1, keepdims=True) + 1e-05)
    hat = cen * inv
    g = d * gain_ref[...]
    back = inv * (
        g - jnp.mean(g, axis=1, keepdims=True) - hat * jnp.mean(g * hat, axis=1, keepdims=True)
    )
    gin_ref[...] = (og_ref[...].astype(F32) + back).astype(BF)
    for c in sent:
        c.wait_send()
    o1.wait()
    o2.wait()


def tile_mask(pattern, tile_rows):
    iota = jnp.arange(tile_rows, dtype=jnp.int32)
    return jnp.any(pattern[None, :, :] == iota[:, None, None], axis=2)


def shards(inputs, layer_norm_gain, w_in, w_out, pattern_in, pattern_out, out_grad):
    row = lax.axis_index("row")
    col = lax.axis_index("col")
    m_in = lax.dynamic_slice(tile_mask(pattern_in, 32), (row * 8, col * 2), (8, 2))
    m_out = lax.dynamic_slice(tile_mask(pattern_out, 64), (col * 2, row * 8), (2, 8))
    m_in = jnp.repeat(m_in.astype(F32), BLOCK, axis=1)
    m_out = jnp.repeat(m_out.astype(F32), BLOCK, axis=1)
    vm = functools.partial(pl.BlockSpec, memory_space=pltpu.VMEM)
    hbm = functools.partial(pl.BlockSpec, memory_space=pl.ANY)
    V = pltpu.VMEM
    out = pl.pallas_call(
        kernel,
        out_shape=(
            jax.ShapeDtypeStruct((8, 8192), BF),
            jax.ShapeDtypeStruct((8, 8192), BF),
            jax.ShapeDtypeStruct((2048, 512), BF),
            jax.ShapeDtypeStruct((512, 2048), BF),
            jax.ShapeDtypeStruct((64, 128), F32),
        ),
        in_specs=[vm(), vm(), vm(), vm(), hbm(), hbm(), vm(), vm()],
        out_specs=(vm(), vm(), hbm(), hbm(), vm()),
        scratch_shapes=[
            V((2048, 512), BF),
            V((512, 2048), BF),
            V((4, 8, 2048), BF),
            V((8, 8, 2048), BF),
            V((8, 8, 2048), BF),
            V((2, 4, 4, 64, 1024), BF),
            V((2, 4, 4, 64, 1024), BF),
            V((2, 2, 256, 512), BF),
            V((2, 2, 256, 512), BF),
            V((2, 2, 256, 512), BF),
            V((2, 2, 256, 512), BF),
            V((2, 2, 256, 512), F32),
            V((4, 4, 64, 512), BF),
            V((4, 4, 64, 512), BF),
            V((2, 2, 4, 64, 1024), BF),
            V((2, 2, 2, 2, 64, 1024), BF),
            V((2, 2, 2, 4, 64, 1024), BF),
            V((2, 2, 2, 4, 64, 1024), BF),
            V((2, 4, 64, 1024), F32),
            V((2, 2, 64, 1024), BF),
            V((2, 2, 2, 32, 1024), BF),
            V((2, 2, 2, 64, 1024), BF),
            V((2, 2, 2, 64, 1024), BF),
            V((2, 8, 8, 2048), BF),
            V((2, 8, 8, 2048), BF),
            V((2048, 512), BF),
            V((512, 2048), BF),
            V((4, 16, 128), F32),
            V((4, 16, 128), F32),
            V((8, 16, 128), F32),
            pltpu.SemaphoreType.DMA((N_COPIES,)),
            pltpu.SemaphoreType.DMA((N_COPIES,)),
            pltpu.SemaphoreType.DMA((2,)),
        ],
        compiler_params=pltpu.CompilerParams(
            collective_id=0, has_side_effects=True, vmem_limit_bytes=67_043_328
        ),
        name="ffn",
    )(
        inputs, layer_norm_gain.reshape(1, 8192), layer_norm_gain.reshape(64, 128), out_grad,
        w_in, w_out, m_in, m_out,
    )
    output, grad_inputs, g_in, g_out, g_gain = out
    return output, grad_inputs, g_in, g_out, g_gain.reshape(8192)


def solution(mesh):
    in_specs = (
        P(("row", "col"), None),
        P(),
        P("row", "col"),
        P("col", "row"),
        P(),
        P(),
        P(("row", "col"), None),
    )
    out_specs = (
        P(("row", "col"), None),
        P(("row", "col"), None),
        P("row", "col"),
        P("col", "row"),
        P(),
    )
    return jax.shard_map(shards, mesh=mesh, in_specs=in_specs, out_specs=out_specs, check_vma=False)
```

```python
import functools

import jax
import jax.numpy as jnp
from jax import lax
from jax.experimental import pallas as pl
from jax.experimental.pallas import tpu as pltpu
from jax.sharding import PartitionSpec as P

BF = jnp.bfloat16
F32 = jnp.float32
N_COPIES = 256


def gelu_value(h):
    inner = 0.7978845608 * (h + 0.044715 * h * h * h)
    return 0.5 * h * (1.0 + jnp.tanh(inner))


def gelu_slope(h):
    tanh_v = jnp.tanh(0.7978845608 * (h + 0.044715 * h * h * h))
    return 0.5 * (1.0 + tanh_v) + 0.5 * h * (1.0 - tanh_v * tanh_v) * 0.7978845608 * (
        1.0 + 0.134145 * h * h
    )


def dot_nn(a, b):
    return lax.dot_general(a, b, (((1,), (0,)), ((), ())), preferred_element_type=F32)


def dot_nt(a, b):
    return lax.dot_general(a, b, (((1,), (1,)), ((), ())), preferred_element_type=F32)


def dot_tn(a, b):
    return lax.dot_general(a, b, (((0,), (0,)), ((), ())), preferred_element_type=F32)


class Sent:
    def __init__(self, c):
        self.c, self.got = c, False
        c.start()

    def wait_recv(self):
        self.got = True
        self.c.wait_recv()


def kernel(
    x_ref, gain_ref, gain64_ref, og_ref, win_hbm, wout_hbm, pin_ref, pout_ref,
    out_ref, gin_ref, gwin_ref, gwout_ref, gg_ref,
    win, wout, min_ref, mout_ref, normed, s0x, s0g, gx, gg,
    ar_send, ar_recv, ay_send, ay_recv, acc, act, dpre,
    rs_far, rs_half, rs_full, rs_in, rs_p,
    ru_far, ru_half, ru_full, ru_in,
    rfin, e_buf, gw1, gw2, s_x, s_z, s_c,
    send_sem, recv_sem, w_sem,
):
    row = lax.axis_index("row")
    col = lax.axis_index("col")
    xi, zi, yl = col // 8, (col // 2) % 4, col % 2
    yh, core = row // 2, row % 2
    q = row * 2 + yl

    def dev(x, z, qq):
        return (qq // 2, (x * 4 + z) * 2 + qq % 2)

    sent = []
    outs = []

    def go(src, dst, to):
        i = len(sent)
        c = Sent(
            pltpu.make_async_remote_copy(
                src_ref=src, dst_ref=dst, send_sem=send_sem.at[i], recv_sem=recv_sem.at[i],
                device_id=to, device_id_type=pl.DeviceIdType.MESH,
            )
        )
        sent.append(c)
        return c

    def finish():
        for c in sent:
            if not c.got:
                c.wait_recv()
        for c in sent:
            c.c.wait_send()
        for o in outs:
            o.wait()

    def step(i, n):
        return (i + n + 4) % 4

    sibling = (yh * 2 + (1 - core), col)
    partner = ((1 - yh) * 2 + core, col)

    barrier = pltpu.get_barrier_semaphore()
    peers = [dev(xi, zi, (q + n) % 8) for n in range(1, 8)]
    peers += [dev(step(xi, n), zi, q) for n in (1, 2, 3)]
    peers += [dev(xi, step(zi, n), q) for n in (1, 2, 3)]
    for p in peers:
        pl.semaphore_signal(barrier, inc=1, device_id=p, device_id_type=pl.DeviceIdType.MESH)

    w_in_copy = pltpu.make_async_copy(win_hbm, win, w_sem.at[0])
    w_out_copy = pltpu.make_async_copy(wout_hbm, wout, w_sem.at[1])
    w_in_copy.start()
    w_out_copy.start()

    xf = x_ref[...].astype(F32)
    cen = xf - jnp.mean(xf, axis=1, keepdims=True)
    inv = lax.rsqrt(jnp.mean(cen * cen, axis=1, keepdims=True) + 1e-05)
    nrm = (cen * inv * gain_ref[...]).astype(BF)
    for r in range(4):
        normed[r] = nrm[:, r * 2048 : (r + 1) * 2048]
    pl.semaphore_wait(barrier, len(peers))

    def column_in(src_of, dst):
        cs = []
        for n in range(1, 8):
            qq = (q + n) % 8
            cs.append(go(src_of(qq), dst.at[q], dev(xi, zi, qq)))
        return cs

    c0x = column_in(lambda qq: normed.at[qq // 2], s0x)
    c0g = column_in(
        lambda qq: og_ref.at[:, pl.ds(pl.multiple_of((qq // 2) * 2048, 2048), 2048)], s0g
    )
    s0x[q] = normed[row]
    s0g[q] = og_ref[:, pl.ds(pl.multiple_of(row * 2048, 2048), 2048)]

    pin = pin_ref[pl.ds(col * 2, 2), :]
    tile = lax.broadcasted_iota(jnp.int32, (8, 16), 0) + row * 8
    for h in range(2):
        kept = jnp.max(jnp.where(pin[h : h + 1] == tile, 1.0, 0.0), axis=1, keepdims=True)
        min_ref[:, h * 256 : (h + 1) * 256] = jnp.broadcast_to(kept, (8, 256))
    pout = pout_ref[pl.ds(pl.multiple_of(row * 8, 8), 8), :]
    for h in range(2):
        kept = jnp.max(jnp.where(pout == col * 2 + h, 1.0, 0.0), axis=1, keepdims=True)
        for t in range(8):
            mout_ref[h : h + 1, t * 256 : (t + 1) * 256] = jnp.broadcast_to(
                kept[t : t + 1], (1, 256)
            )

    def blk(g, k, u, v):
        return g.at[0, v, u] if k == 0 else g.at[1, u, v]

    def colours():
        st = []
        for k in range(2):
            u0, v0 = (zi, xi) if k == 0 else (xi, zi)

            def to_z(n):
                return dev(xi, step(zi, n), q)

            def to_x(n):
                return dev(step(xi, n), zi, q)

            st.append(
                dict(
                    k=k, u0=u0, v0=v0, to_u=to_z if k == 0 else to_x, to_v=to_x if k == 0 else to_z
                )
            )
        return st

    def gather(s0, g, arrived):
        for c in arrived:
            c.wait_recv()
        block = s0[...].reshape(64, 2048)
        g[0, xi, zi] = block[:, :1024]
        g[1, xi, zi] = block[:, 1024:]
        st = colours()

        def one(s, off, n, v=None):
            b = blk(g, s["k"], step(s["u0"], off), s["v0"] if v is None else v)
            return go(b, b, s["to_v"](n))

        def both(s, off):
            s["s", off] = {n: one(s, off, n) for n in (1, -1)}

        for s in st:
            b = blk(g, s["k"], s["u0"], s["v0"])
            s["f"] = {n: go(b, b, s["to_u"](n)) for n in (1, -1)}
            both(s, 0)
            s["f2"], s["s2"] = {}, {}
        yield
        for n in (1, -1):
            for s in st:
                s["f"][n].wait_recv()
                b = blk(g, s["k"], step(s["u0"], -n), s["v0"])
                part = b.at[pl.ds(0, 32)] if n == 1 else b.at[pl.ds(32, 32)]
                s["f2"][n] = go(part, part, s["to_u"](n))
                both(s, -n)
            yield

        def relay(s, off, n):
            s["s", off][n].wait_recv()
            s["s2"][off] = one(s, off, n, step(s["v0"], -n))

        for s in st:
            relay(s, 0, 1)
        yield
        for s in st:
            s["f2"][1].wait_recv()
            s["f2"][-1].wait_recv()
            both(s, 2)
        for s in st:
            s["s", 0][-1].wait_recv()
        yield
        for off in (-1, 1, 2):
            n = 1 if off == 1 else -1
            for s in st:
                relay(s, off, n)
            for s in st:
                s["s", off][-n].wait_recv()
            yield
        for off in (0, -1, 1, 2):
            for s in st:
                s["s2"][off].wait_recv()
            yield

    def drain(g, n):
        for _ in range(n):
            next(g, None)

    gen_x = gather(s0x, gx, c0x)
    gen_g = gather(s0g, gg, c0g)

    def partial(g, w, nt, xx):
        a = g[0, xx].reshape(256, 1024)
        b = g[1, xx].reshape(256, 1024)
        if nt:
            return dot_nt(a, w[:, :1024]) + dot_nt(b, w[:, 1024:])
        return dot_nn(a, w[:1024]) + dot_nn(b, w[1024:])

    def x_of(p, mine):
        c = core if mine else 1 - core
        return (xi + (4 - c if p == 0 else 1 + c)) % 4

    side = ((gx, win, False), (gg, wout, True))

    def row_other(i, p):
        ar_send[i, p] = partial(*side[i], x_of(p, False)).astype(BF)
        return go(ar_send.at[i, p], ar_recv.at[i, p], sibling)

    def row_mine(i, p):
        acc[i, p] = partial(*side[i], x_of(p, True))

    def row_add(i, p, c):
        c.wait_recv()
        v = acc[i, p] + ar_recv[i, p].astype(F32)
        acc[i, p] = v
        ay_send[i, p] = v.astype(BF)
        return go(ay_send.at[i, p], ay_recv.at[i, p], partner)

    def rows_loop(f):
        def body(m, _):
            f(m, pl.ds(pl.multiple_of(m * 64, 64), 64))
            return 0

        lax.fori_loop(0, 4, body, 0)

    def row_act(p, c):
        c.wait_recv()
        xx = x_of(p, True)

        def rows_of(m, rows):
            pre = acc[0, p, rows] + ay_recv[0, p, rows].astype(F32)
            acc[0, p, rows] = pre
            act[xx, m] = gelu_value(pre).astype(BF)

        rows_loop(rows_of)
        return go(act.at[xx], act.at[xx], sibling)

    def row_dpre(p, c):
        c.wait_recv()
        xx = x_of(p, True)

        def rows_of(m, rows):
            d = acc[1, p, rows] + ay_recv[1, p, rows].astype(F32)
            dpre[xx, m] = (d * gelu_slope(acc[0, p, rows])).astype(BF)

        rows_loop(rows_of)
        return go(dpre.at[xx], dpre.at[xx], sibling)

    def term(t, k, v):
        if t == 0:
            a = act[v] if k == 0 else act[:, v]
            r = dot_nn(a.reshape(256, 512), wout[:, k * 1024 : (k + 1) * 1024])
        else:
            a = dpre[v] if k == 0 else dpre[:, v]
            r = dot_nt(a.reshape(256, 512), win[k * 1024 : (k + 1) * 1024, :])
        return r.reshape(4, 64, 1024)

    last = {}

    def scatter(t):
        st = colours()
        with_half = {1: (2, -1), -1: (1, 0)}
        for s in st:
            k = s["k"]
            rs_far[t, k] = term(t, k, step(s["v0"], 2)).astype(BF)
            s["h"], s["w"], s["uw"] = {}, {}, {}
            for i in range(2):
                for n in (1, -1):
                    off = with_half[n][i]
                    u = step(s["u0"], off)
                    s["h"][off] = go(rs_far.at[t, k, u], rs_half.at[t, k, u], s["to_v"](n))
        yield

        def piece(s, n, off):
            k, u, j = s["k"], step(s["u0"], off), 0 if n == 1 else 1
            p = rs_p[k, j, u]
            if off in with_half[n]:
                s["h"][off].wait_recv()
                p = p + rs_half[t, k, u].astype(F32)
            rs_full[t, k, j, u] = p.astype(BF)
            s["w"][n, off] = go(rs_full.at[t, k, j, u], rs_in.at[t, k, j, u], s["to_v"](n))

        for n in (-1, 1):
            for s in st:
                rs_p[s["k"], 0 if n == 1 else 1] = term(t, s["k"], step(s["v0"], n))
                for off in with_half[-n]:
                    piece(s, n, off)
        yield
        for i in range(2):
            for n in (1, -1):
                for s in st:
                    piece(s, n, with_half[n][i])
        yield
        for s in st:
            rs_p[s["k"], 2] = term(t, s["k"], s["v0"])
        yield

        def summed(s, off):
            k, u = s["k"], step(s["u0"], off)
            s["w"][1, off].wait_recv()
            s["w"][-1, off].wait_recv()
            return rs_p[k, 2, u] + rs_in[t, k, 0, u].astype(F32) + rs_in[t, k, 1, u].astype(F32)

        for s in st:
            k = s["k"]
            ru_far[t, k] = summed(s, 2).astype(BF)
            s["uh"] = {
                n: go(
                    ru_far.at[t, k, pl.ds(0 if n == 1 else 32, 32)],
                    ru_half.at[t, k, 0 if n == 1 else 1],
                    s["to_u"](n),
                )
                for n in (1, -1)
            }
        yield
        for n in (-1, 1):
            for s in st:
                k, j = s["k"], 0 if n == 1 else 1
                p = summed(s, n)
                s["uh"][n].wait_recv()
                extra = ru_half[t, k, j].astype(F32)
                lo, hi = p[0:32], p[32:64]
                if n == 1:
                    lo = lo + extra
                else:
                    hi = hi + extra
                ru_full[t, k, j, 0:32] = lo.astype(BF)
                ru_full[t, k, j, 32:64] = hi.astype(BF)
                s["uw"][n] = go(ru_full.at[t, k, j], ru_in.at[t, k, j], s["to_u"](n))
        yield
        for s in st:
            k = s["k"]
            r = summed(s, 0)
            s["uw"][1].wait_recv()
            s["uw"][-1].wait_recv()
            r = r + ru_in[t, k, 0].astype(F32) + ru_in[t, k, 1].astype(F32)
            rfin[t, :, :, k * 1024 : (k + 1) * 1024] = r.astype(BF).reshape(8, 8, 1024)
        last[t] = [
            go(rfin.at[t, (q + n) % 8], e_buf.at[t, q], dev(xi, zi, (q + n) % 8))
            for n in range(1, 8)
        ]
        e_buf[t, q] = rfin[t, q]
        yield

    ones = jnp.ones((8, 512), BF)

    def grad_in_tiles(k, lo, hi):
        def win_tile(j, _):
            lanes = pl.ds(pl.multiple_of(j * 256, 256), 256)
            ft = k * 4 + j
            a = gx[k, :, :, :, lanes].reshape(1024, 256)
            raw = dot_tn(a, dpre[...].reshape(1024, 512))
            rows = pl.ds(pl.multiple_of(ft * 256, 256), 256)
            gw1[rows] = (raw * min_ref[pl.ds(ft, 1)]).astype(BF)
            p = raw * win[rows].astype(F32)
            hi = p.astype(BF)
            lo = (p - hi.astype(F32)).astype(BF)
            s = dot_nt(ones, hi) + dot_nt(ones, lo)
            s_x[xi, pl.ds(2 * ft, 1)] = s[0:1, :128]
            s_x[xi, pl.ds(2 * ft + 1, 1)] = s[0:1, 128:]
            return 0

        lax.fori_loop(lo, hi, win_tile, 0)

    def grad_out_tiles(k, lo, hi):
        def wout_tile(j, _):
            lanes = pl.ds(pl.multiple_of(j * 256, 256), 256)
            b = gg[k, :, :, :, lanes].reshape(1024, 256)
            raw = dot_tn(act[...].reshape(1024, 512), b)
            cols = pl.ds(pl.multiple_of(k * 1024 + j * 256, 256), 256)
            for h in range(2):
                gw2[h * 256 : (h + 1) * 256, cols] = (
                    raw[h * 256 : (h + 1) * 256] * mout_ref[h : h + 1, cols]
                ).astype(BF)
            return 0

        lax.fori_loop(lo, hi, wout_tile, 0)

    def put(src, dst, i):
        o = pltpu.make_async_copy(src, dst, w_sem.at[i])
        o.start()
        outs.append(o)

    drain(gen_x, 1)
    w_in_copy.wait()
    for t in range(8):
        win[t * 256 : (t + 1) * 256] = win[t * 256 : (t + 1) * 256] * min_ref[t : t + 1].astype(BF)
    w_out_copy.wait()
    drain(gen_x, 4)
    drain(gen_g, 1)
    for t in range(2):
        wout[t * 256 : (t + 1) * 256] = wout[t * 256 : (t + 1) * 256] * mout_ref[t : t + 1].astype(BF)
    drain(gen_x, 2)
    drain(gen_g, 1)
    drain(gen_x, 1)
    drain(gen_g, 1)
    drain(gen_x, 2)
    ca0 = row_other(0, 0)
    row_mine(0, 0)
    drain(gen_g, 1)
    cb0 = row_add(0, 0, ca0)
    drain(gen_x, 2)
    ca1 = row_other(0, 1)
    row_mine(0, 1)
    cb1 = row_add(0, 1, ca1)
    drain(gen_g, 3)
    cc0 = row_act(0, cb0)
    drain(gen_g, 1)
    cc1 = row_act(1, cb1)
    cc0.wait_recv()
    cc1.wait_recv()
    gen_o = scatter(0)
    drain(gen_o, 1)
    drain(gen_g, 2)
    da0 = row_other(1, 0)
    drain(gen_o, 1)
    row_mine(1, 0)
    db0 = row_add(1, 0, da0)
    drain(gen_g, 2)
    da1 = row_other(1, 1)
    row_mine(1, 1)
    db1 = row_add(1, 1, da1)
    drain(gen_o, 2)
    grad_out_tiles(0, 0, 4)
    dc0 = row_dpre(0, db0)
    drain(gen_o, 1)
    grad_out_tiles(1, 0, 4)
    put(gw2, gwout_ref, 1)
    dc1 = row_dpre(1, db1)
    drain(gen_o, 1)
    dc0.wait_recv()
    dc1.wait_recv()
    gen_d = scatter(1)
    drain(gen_d, 2)
    drain(gen_o, 1)
    grad_in_tiles(0, 0, 2)
    drain(gen_d, 1)
    grad_in_tiles(0, 2, 4)
    drain(gen_d, 1)
    grad_in_tiles(1, 0, 4)
    put(gw1, gwin_ref, 0)
    sx = [go(s_x.at[xi], s_x.at[xi], dev(step(xi, n), zi, q)) for n in (1, 2, 3)]
    drain(gen_d, 1)
    for c in last[0]:
        c.wait_recv()
    for r in range(4):
        f = slice(r * 2048, (r + 1) * 2048)
        o = e_buf[0, 2 * r].astype(F32) + e_buf[0, 2 * r + 1].astype(F32)
        out_ref[:, f] = (x_ref[:, f].astype(F32) + o).astype(BF)
    for c in sx:
        c.wait_recv()
    s_z[zi] = (s_x[0] + s_x[1]) + (s_x[2] + s_x[3])
    sz = [go(s_z.at[zi], s_z.at[zi], dev(xi, step(zi, n), q)) for n in (1, 2, 3)]
    drain(gen_d, 1)
    for c in sz:
        c.wait_recv()
    s_c[q] = (s_z[0] + s_z[1]) + (s_z[2] + s_z[3])
    sc = [go(s_c.at[q], s_c.at[q], dev(xi, zi, (q + n) % 8)) for n in range(1, 8)]
    drain(gen_d, 1)
    for c in sc:
        c.wait_recv()
    for r in range(4):
        gg_ref[r * 16 : (r + 1) * 16] = (s_c[2 * r] + s_c[2 * r + 1]) / gain64_ref[r * 16 : (r + 1) * 16]
    xf = x_ref[...].astype(F32)
    cen = xf - jnp.mean(xf, axis=1, keepdims=True)
    inv = lax.rsqrt(jnp.mean(cen * cen, axis=1, keepdims=True) + 1e-05)
    hat = cen * inv
    for c in last[1]:
        c.wait_recv()
    parts = [
        e_buf[1, 2 * r].astype(F32) + e_buf[1, 2 * r + 1].astype(F32) for r in range(4)
    ]
    d = jnp.concatenate(parts, axis=1)
    g = d * gain_ref[...]
    back = inv * (
        g - jnp.mean(g, axis=1, keepdims=True) - hat * jnp.mean(g * hat, axis=1, keepdims=True)
    )
    gin_ref[...] = (og_ref[...].astype(F32) + back).astype(BF)
    finish()


def hand_over(n, *refs):
    ins, outs, bufs = refs[:n], refs[n : 2 * n], refs[2 * n : 3 * n]
    sem_in, sem_out = refs[3 * n :]
    moves, i = [], 0
    for a, o, b in zip(ins, outs, bufs):
        parts = 4 if a.shape[0] > 64 else 1
        rows = a.shape[0] // parts
        for p in range(parts):
            r = pl.ds(p * rows, rows)
            moves.append(
                (
                    pltpu.make_async_copy(a.at[r], b.at[r], sem_in.at[i]),
                    pltpu.make_async_copy(b.at[r], o.at[r], sem_out.at[i]),
                )
            )
            i += 1
    for get, _ in moves:
        get.start()
    for get, give in moves:
        get.wait()
        give.start()
    for _, give in moves:
        give.wait()


def shards(inputs, layer_norm_gain, w_in, w_out, pattern_in, pattern_out, out_grad):
    vm = functools.partial(pl.BlockSpec, memory_space=pltpu.VMEM)
    hbm = functools.partial(pl.BlockSpec, memory_space=pl.ANY)
    V = pltpu.VMEM
    out = pl.pallas_call(
        kernel,
        out_shape=(
            jax.ShapeDtypeStruct((8, 8192), BF),
            jax.ShapeDtypeStruct((8, 8192), BF),
            jax.ShapeDtypeStruct((2048, 512), BF),
            jax.ShapeDtypeStruct((512, 2048), BF),
            jax.ShapeDtypeStruct((64, 128), F32),
        ),
        in_specs=[vm(), vm(), vm(), vm(), hbm(), hbm(), vm(), vm()],
        out_specs=(vm(), vm(), hbm(), hbm(), vm()),
        scratch_shapes=[
            V((2048, 512), BF),
            V((512, 2048), BF),
            V((8, 512), F32),
            V((2, 2048), F32),
            V((4, 8, 2048), BF),
            V((8, 8, 2048), BF),
            V((8, 8, 2048), BF),
            V((2, 4, 4, 64, 1024), BF),
            V((2, 4, 4, 64, 1024), BF),
            V((2, 2, 256, 512), BF),
            V((2, 2, 256, 512), BF),
            V((2, 2, 256, 512), BF),
            V((2, 2, 256, 512), BF),
            V((2, 2, 256, 512), F32),
            V((4, 4, 64, 512), BF),
            V((4, 4, 64, 512), BF),
            V((2, 2, 4, 64, 1024), BF),
            V((2, 2, 4, 64, 1024), BF),
            V((2, 2, 2, 4, 64, 1024), BF),
            V((2, 2, 2, 4, 64, 1024), BF),
            V((2, 3, 4, 64, 1024), F32),
            V((2, 2, 64, 1024), BF),
            V((2, 2, 2, 32, 1024), BF),
            V((2, 2, 2, 64, 1024), BF),
            V((2, 2, 2, 64, 1024), BF),
            V((2, 8, 8, 2048), BF),
            V((2, 8, 8, 2048), BF),
            V((2048, 512), BF),
            V((512, 2048), BF),
            V((4, 16, 128), F32),
            V((4, 16, 128), F32),
            V((8, 16, 128), F32),
            pltpu.SemaphoreType.DMA((N_COPIES,)),
            pltpu.SemaphoreType.DMA((N_COPIES,)),
            pltpu.SemaphoreType.DMA((2,)),
        ],
        compiler_params=pltpu.CompilerParams(
            collective_id=0, has_side_effects=True, vmem_limit_bytes=67_043_328
        ),
        name="ffn",
    )(
        inputs, layer_norm_gain.reshape(1, 8192), layer_norm_gain.reshape(64, 128), out_grad,
        w_in, w_out, pattern_in, pattern_out,
    )
    output, grad_inputs, g_in, g_out, g_gain = pl.pallas_call(
        functools.partial(hand_over, len(out)),
        out_shape=tuple(jax.ShapeDtypeStruct(o.shape, o.dtype) for o in out),
        in_specs=[hbm()] * len(out),
        out_specs=(hbm(),) * len(out),
        scratch_shapes=[V(o.shape, o.dtype) for o in out]
        + [pltpu.SemaphoreType.DMA((16,)), pltpu.SemaphoreType.DMA((16,))],
        name="hand_over",
    )(*out)
    return output, grad_inputs, g_in, g_out, g_gain.reshape(8192)


def solution(mesh):
    in_specs = (
        P(("row", "col"), None),
        P(),
        P("row", "col"),
        P("col", "row"),
        P(),
        P(),
        P(("row", "col"), None),
    )
    out_specs = (
        P(("row", "col"), None),
        P(("row", "col"), None),
        P("row", "col"),
        P("col", "row"),
        P(),
    )
    return jax.shard_map(shards, mesh=mesh, in_specs=in_specs, out_specs=out_specs, check_vma=False)
```

```python
import functools

import jax
import jax.numpy as jnp
from jax import lax
from jax.experimental import pallas as pl
from jax.experimental.pallas import tpu as pltpu
from jax.sharding import PartitionSpec as P

BF = jnp.bfloat16
F32 = jnp.float32
N_COPIES = 256


def gelu_value(h):
    inner = 0.7978845608 * (h + 0.044715 * h * h * h)
    return 0.5 * h * (1.0 + jnp.tanh(inner))


def gelu_slope(h):
    tanh_v = jnp.tanh(0.7978845608 * (h + 0.044715 * h * h * h))
    return 0.5 * (1.0 + tanh_v) + 0.5 * h * (1.0 - tanh_v * tanh_v) * 0.7978845608 * (
        1.0 + 0.134145 * h * h
    )


def dot_nn(a, b):
    return lax.dot_general(a, b, (((1,), (0,)), ((), ())), preferred_element_type=F32)


def dot_nt(a, b):
    return lax.dot_general(a, b, (((1,), (1,)), ((), ())), preferred_element_type=F32)


def dot_tn(a, b):
    return lax.dot_general(a, b, (((0,), (0,)), ((), ())), preferred_element_type=F32)


class Sent:
    def __init__(self, c):
        self.c, self.got = c, False
        c.start()

    def wait_recv(self):
        self.got = True
        self.c.wait_recv()


def kernel(
    x_ref, gain_ref, gain64_ref, og_ref, win_hbm, wout_hbm, pin_ref, pout_ref,
    out_ref, gin_ref, gwin_ref, gwout_ref, gg_ref,
    win, wout, min_ref, mout_ref, normed, s0x, s0g, gx, gg,
    ar_send, ar_recv, ay_send, ay_recv, acc, act, dpre,
    rs_far, rs_half, rs_full, rs_in, rs_p,
    ru_far, ru_half, ru_full, ru_in,
    rfin, e_buf, gw1, gw2, s_x, s_z, s_c,
    send_sem, recv_sem, w_sem,
):
    row = lax.axis_index("row")
    col = lax.axis_index("col")
    xi, zi, yl = col // 8, (col // 2) % 4, col % 2
    yh, core = row // 2, row % 2
    q = row * 2 + yl

    def dev(x, z, qq):
        return (qq // 2, (x * 4 + z) * 2 + qq % 2)

    sent = []
    outs = []

    def go(src, dst, to):
        i = len(sent)
        c = Sent(
            pltpu.make_async_remote_copy(
                src_ref=src, dst_ref=dst, send_sem=send_sem.at[i], recv_sem=recv_sem.at[i],
                device_id=to, device_id_type=pl.DeviceIdType.MESH,
            )
        )
        sent.append(c)
        return c

    def finish():
        for c in sent:
            if not c.got:
                c.wait_recv()
        for c in sent:
            c.c.wait_send()
        for o in outs:
            o.wait()

    def step(i, n):
        return (i + n + 4) % 4

    sibling = (yh * 2 + (1 - core), col)
    partner = ((1 - yh) * 2 + core, col)

    barrier = pltpu.get_barrier_semaphore()
    peers = [dev(xi, zi, (q + n) % 8) for n in range(1, 8)]
    peers += [dev(step(xi, n), zi, q) for n in (1, 2, 3)]
    peers += [dev(xi, step(zi, n), q) for n in (1, 2, 3)]
    for p in peers:
        pl.semaphore_signal(barrier, inc=1, device_id=p, device_id_type=pl.DeviceIdType.MESH)

    w_in_copy = pltpu.make_async_copy(win_hbm, win, w_sem.at[0])
    w_out_copy = pltpu.make_async_copy(wout_hbm, wout, w_sem.at[1])
    w_in_copy.start()
    w_out_copy.start()

    xf = x_ref[...].astype(F32)
    cen = xf - jnp.mean(xf, axis=1, keepdims=True)
    inv = lax.rsqrt(jnp.mean(cen * cen, axis=1, keepdims=True) + 1e-05)
    nrm = (cen * inv * gain_ref[...]).astype(BF)
    for r in range(4):
        normed[r] = nrm[:, r * 2048 : (r + 1) * 2048]
    pl.semaphore_wait(barrier, len(peers))

    def column_in(src_of, dst):
        cs = []
        for n in range(1, 8):
            qq = (q + n) % 8
            cs.append(go(src_of(qq), dst.at[q], dev(xi, zi, qq)))
        return cs

    c0x = column_in(lambda qq: normed.at[qq // 2], s0x)
    s0x[q] = normed[row]
    s0g[q] = og_ref[:, pl.ds(pl.multiple_of(row * 2048, 2048), 2048)]

    lane = lax.broadcasted_iota(jnp.int32, (16, 64), 1)
    tile = lax.broadcasted_iota(jnp.int32, (16, 128), 1) + row * 8
    for h in range(2):
        rows = jnp.max(jnp.where(lane == col * 2 + h, pin_ref[...], -1), axis=1, keepdims=True)
        kept = jnp.max(jnp.where(rows == tile, 1.0, 0.0), axis=0, keepdims=True)
        for t in range(8):
            min_ref[t : t + 1, h * 256 : (h + 1) * 256] = jnp.broadcast_to(
                kept[:, t : t + 1], (1, 256)
            )
    pout = pout_ref[pl.ds(pl.multiple_of(row * 8, 8), 8), :]
    for h in range(2):
        kept = jnp.max(jnp.where(pout == col * 2 + h, 1.0, 0.0), axis=1, keepdims=True)
        for t in range(8):
            mout_ref[h : h + 1, t * 256 : (t + 1) * 256] = jnp.broadcast_to(
                kept[t : t + 1], (1, 256)
            )

    def blk(g, k, u, v):
        return g.at[0, v, u] if k == 0 else g.at[1, u, v]

    def colours():
        st = []
        for k in range(2):
            u0, v0 = (zi, xi) if k == 0 else (xi, zi)

            def to_z(n):
                return dev(xi, step(zi, n), q)

            def to_x(n):
                return dev(step(xi, n), zi, q)

            st.append(
                dict(
                    k=k, u0=u0, v0=v0, to_u=to_z if k == 0 else to_x, to_v=to_x if k == 0 else to_z
                )
            )
        return st

    def gather(s0, g, arrived):
        for c in arrived:
            c.wait_recv()
        block = s0[...].reshape(64, 2048)
        g[0, xi, zi] = block[:, :1024]
        g[1, xi, zi] = block[:, 1024:]
        st = colours()

        def one(s, off, n, v=None):
            b = blk(g, s["k"], step(s["u0"], off), s["v0"] if v is None else v)
            return go(b, b, s["to_v"](n))

        def both(s, off):
            s["s", off] = {n: one(s, off, n) for n in (1, -1)}

        for s in st:
            b = blk(g, s["k"], s["u0"], s["v0"])
            s["f"] = {n: go(b, b, s["to_u"](n)) for n in (1, -1)}
            both(s, 0)
            s["f2"], s["s2"] = {}, {}
        yield
        for n in (1, -1):
            for s in st:
                s["f"][n].wait_recv()
                b = blk(g, s["k"], step(s["u0"], -n), s["v0"])
                part = b.at[pl.ds(0, 32)] if n == 1 else b.at[pl.ds(32, 32)]
                s["f2"][n] = go(part, part, s["to_u"](n))
                both(s, -n)
            yield

        def relay(s, off, n):
            s["s", off][n].wait_recv()
            s["s2"][off] = one(s, off, n, step(s["v0"], -n))

        for s in st:
            relay(s, 0, 1)
        yield
        for s in st:
            s["f2"][1].wait_recv()
            s["f2"][-1].wait_recv()
            both(s, 2)
        for s in st:
            s["s", 0][-1].wait_recv()
        yield
        for off in (-1, 1, 2):
            n = 1 if off == 1 else -1
            for s in st:
                relay(s, off, n)
            for s in st:
                s["s", off][-n].wait_recv()
            yield
        for off in (0, -1, 1, 2):
            for s in st:
                s["s2"][off].wait_recv()
            yield

    def drain(g, n):
        for _ in range(n):
            next(g, None)

    gen_x = gather(s0x, gx, c0x)
    c0g = []
    gen_g = gather(s0g, gg, c0g)

    def partial(g, w, nt, xx):
        a = g[0, xx].reshape(256, 1024)
        b = g[1, xx].reshape(256, 1024)
        if nt:
            return dot_nt(a, w[:, :1024]) + dot_nt(b, w[:, 1024:])
        return dot_nn(a, w[:1024]) + dot_nn(b, w[1024:])

    def x_of(p, mine):
        c = core if mine else 1 - core
        return (xi + (4 - c if p == 0 else 1 + c)) % 4

    side = ((gx, win, False), (gg, wout, True))

    def row_other(i, p):
        ar_send[i, p] = partial(*side[i], x_of(p, False)).astype(BF)
        return go(ar_send.at[i, p], ar_recv.at[i, p], sibling)

    def row_mine(i, p):
        acc[i, p] = partial(*side[i], x_of(p, True))

    def row_add(i, p, c):
        c.wait_recv()
        v = acc[i, p] + ar_recv[i, p].astype(F32)
        acc[i, p] = v
        ay_send[i, p] = v.astype(BF)
        return go(ay_send.at[i, p], ay_recv.at[i, p], partner)

    def rows_loop(f):
        def body(m, _):
            f(m, pl.ds(pl.multiple_of(m * 64, 64), 64))
            return 0

        lax.fori_loop(0, 4, body, 0)

    def row_act(p, c):
        c.wait_recv()
        xx = x_of(p, True)

        def rows_of(m, rows):
            pre = acc[0, p, rows] + ay_recv[0, p, rows].astype(F32)
            acc[0, p, rows] = pre
            act[xx, m] = gelu_value(pre).astype(BF)

        rows_loop(rows_of)
        return go(act.at[xx], act.at[xx], sibling)

    def row_dpre(p, c):
        c.wait_recv()
        xx = x_of(p, True)

        def rows_of(m, rows):
            d = acc[1, p, rows] + ay_recv[1, p, rows].astype(F32)
            dpre[xx, m] = (d * gelu_slope(acc[0, p, rows])).astype(BF)

        rows_loop(rows_of)
        return go(dpre.at[xx], dpre.at[xx], sibling)

    def term(t, k, v):
        if t == 0:
            a = act[v] if k == 0 else act[:, v]
            r = dot_nn(a.reshape(256, 512), wout[:, k * 1024 : (k + 1) * 1024])
        else:
            a = dpre[v] if k == 0 else dpre[:, v]
            r = dot_nt(a.reshape(256, 512), win[k * 1024 : (k + 1) * 1024, :])
        return r.reshape(4, 64, 1024)

    last = {}

    def scatter(t):
        st = colours()
        with_half = {1: (2, -1), -1: (1, 0)}
        for s in st:
            k = s["k"]
            rs_far[t, k] = term(t, k, step(s["v0"], 2)).astype(BF)
            s["h"], s["w"], s["uw"] = {}, {}, {}
            for i in range(2):
                for n in (1, -1):
                    off = with_half[n][i]
                    u = step(s["u0"], off)
                    s["h"][off] = go(rs_far.at[t, k, u], rs_half.at[t, k, u], s["to_v"](n))
        yield

        def piece(s, n, off):
            k, u, j = s["k"], step(s["u0"], off), 0 if n == 1 else 1
            p = rs_p[k, j, u]
            if off in with_half[n]:
                s["h"][off].wait_recv()
                p = p + rs_half[t, k, u].astype(F32)
            rs_full[t, k, j, u] = p.astype(BF)
            s["w"][n, off] = go(rs_full.at[t, k, j, u], rs_in.at[t, k, j, u], s["to_v"](n))

        for n, off in ((-1, 2), (1, 1)):
            for s in st:
                rs_p[s["k"], 0 if n == 1 else 1] = term(t, s["k"], step(s["v0"], n))
                piece(s, n, off)
        yield
        for n, off in ((-1, -1), (1, 2)):
            for s in st:
                piece(s, n, off)
        yield
        for n, off in ((-1, 1), (1, -1)):
            for s in st:
                piece(s, n, off)
        for s in st:
            rs_p[s["k"], 2] = term(t, s["k"], s["v0"])
        yield

        def summed(s, off):
            k, u = s["k"], step(s["u0"], off)
            s["w"][1, off].wait_recv()
            s["w"][-1, off].wait_recv()
            return rs_p[k, 2, u] + rs_in[t, k, 0, u].astype(F32) + rs_in[t, k, 1, u].astype(F32)

        for s in st:
            k = s["k"]
            ru_far[t, k] = summed(s, 2).astype(BF)
            s["uh"] = {
                n: go(
                    ru_far.at[t, k, pl.ds(0 if n == 1 else 32, 32)],
                    ru_half.at[t, k, 0 if n == 1 else 1],
                    s["to_u"](n),
                )
                for n in (1, -1)
            }
        for s in st:
            for n in (1, -1):
                piece(s, n, 0)
        yield
        for n in (-1, 1):
            for s in st:
                k, j = s["k"], 0 if n == 1 else 1
                p = summed(s, n)
                s["uh"][n].wait_recv()
                extra = ru_half[t, k, j].astype(F32)
                lo, hi = p[0:32], p[32:64]
                if n == 1:
                    lo = lo + extra
                else:
                    hi = hi + extra
                ru_full[t, k, j, 0:32] = lo.astype(BF)
                ru_full[t, k, j, 32:64] = hi.astype(BF)
                s["uw"][n] = go(ru_full.at[t, k, j], ru_in.at[t, k, j], s["to_u"](n))
        yield
        for s in st:
            k = s["k"]
            r = summed(s, 0)
            s["uw"][1].wait_recv()
            s["uw"][-1].wait_recv()
            r = r + ru_in[t, k, 0].astype(F32) + ru_in[t, k, 1].astype(F32)
            rfin[t, :, :, k * 1024 : (k + 1) * 1024] = r.astype(BF).reshape(8, 8, 1024)
        last[t] = [
            go(rfin.at[t, (q + n) % 8], e_buf.at[t, q], dev(xi, zi, (q + n) % 8))
            for n in range(1, 8)
        ]
        e_buf[t, q] = rfin[t, q]
        yield

    ones = jnp.ones((8, 512), BF)

    def grad_in_tiles(k, lo, hi):
        def win_tile(j, _):
            lanes = pl.ds(pl.multiple_of(j * 256, 256), 256)
            ft = k * 4 + j
            a = gx[k, :, :, :, lanes].reshape(1024, 256)
            raw = dot_tn(a, dpre[...].reshape(1024, 512))
            rows = pl.ds(pl.multiple_of(ft * 256, 256), 256)
            gw1[rows] = (raw * min_ref[pl.ds(ft, 1)]).astype(BF)
            p = raw * win[rows].astype(F32)
            hi = p.astype(BF)
            lo = (p - hi.astype(F32)).astype(BF)
            s = dot_nt(ones, hi) + dot_nt(ones, lo)
            s_x[xi, pl.ds(2 * ft, 1)] = s[0:1, :128]
            s_x[xi, pl.ds(2 * ft + 1, 1)] = s[0:1, 128:]
            return 0

        lax.fori_loop(lo, hi, win_tile, 0)

    def grad_out_tiles(k, lo, hi):
        def wout_tile(j, _):
            lanes = pl.ds(pl.multiple_of(j * 256, 256), 256)
            b = gg[k, :, :, :, lanes].reshape(1024, 256)
            raw = dot_tn(act[...].reshape(1024, 512), b)
            cols = pl.ds(pl.multiple_of(k * 1024 + j * 256, 256), 256)
            for h in range(2):
                gw2[h * 256 : (h + 1) * 256, cols] = (
                    raw[h * 256 : (h + 1) * 256] * mout_ref[h : h + 1, cols]
                ).astype(BF)
            return 0

        lax.fori_loop(lo, hi, wout_tile, 0)

    def put(src, dst, i):
        o = pltpu.make_async_copy(src, dst, w_sem.at[i])
        o.start()
        outs.append(o)

    drain(gen_x, 1)
    c0g += column_in(
        lambda qq: og_ref.at[:, pl.ds(pl.multiple_of((qq // 2) * 2048, 2048), 2048)], s0g
    )
    w_in_copy.wait()
    for t in range(8):
        win[t * 256 : (t + 1) * 256] = win[t * 256 : (t + 1) * 256] * min_ref[t : t + 1].astype(BF)
    w_out_copy.wait()
    drain(gen_x, 4)
    drain(gen_g, 1)
    for t in range(2):
        wout[t * 256 : (t + 1) * 256] = wout[t * 256 : (t + 1) * 256] * mout_ref[t : t + 1].astype(BF)
    drain(gen_x, 2)
    drain(gen_g, 1)
    drain(gen_x, 1)
    drain(gen_g, 1)
    drain(gen_x, 2)
    drain(gen_g, 2)
    ca0 = row_other(0, 0)
    row_mine(0, 0)
    cb0 = row_add(0, 0, ca0)
    drain(gen_x, 2)
    drain(gen_g, 1)
    ca1 = row_other(0, 1)
    row_mine(0, 1)
    cb1 = row_add(0, 1, ca1)
    drain(gen_g, 2)
    cc0 = row_act(0, cb0)
    cc1 = row_act(1, cb1)
    cc0.wait_recv()
    cc1.wait_recv()
    gen_o = scatter(0)
    drain(gen_o, 1)
    drain(gen_g, 2)
    da0 = row_other(1, 0)
    drain(gen_o, 1)
    row_mine(1, 0)
    db0 = row_add(1, 0, da0)
    drain(gen_g, 2)
    da1 = row_other(1, 1)
    drain(gen_o, 1)
    row_mine(1, 1)
    db1 = row_add(1, 1, da1)
    drain(gen_o, 1)
    grad_out_tiles(0, 0, 4)
    dc0 = row_dpre(0, db0)
    drain(gen_o, 1)
    dc1 = row_dpre(1, db1)
    dc0.wait_recv()
    dc1.wait_recv()
    gen_d = scatter(1)
    drain(gen_d, 1)
    drain(gen_o, 1)
    drain(gen_d, 1)
    drain(gen_o, 1)
    drain(gen_d, 1)
    grad_out_tiles(1, 0, 4)
    put(gw2, gwout_ref, 1)
    drain(gen_d, 1)
    grad_in_tiles(0, 0, 4)
    drain(gen_d, 1)
    grad_in_tiles(1, 0, 4)
    put(gw1, gwin_ref, 0)
    sx = [go(s_x.at[xi], s_x.at[xi], dev(step(xi, n), zi, q)) for n in (1, 2, 3)]
    for c in last[0]:
        c.wait_recv()
    for r in range(4):
        f = slice(r * 2048, (r + 1) * 2048)
        o = e_buf[0, 2 * r].astype(F32) + e_buf[0, 2 * r + 1].astype(F32)
        out_ref[:, f] = (x_ref[:, f].astype(F32) + o).astype(BF)
    drain(gen_d, 1)
    for c in sx:
        c.wait_recv()
    s_z[zi] = (s_x[0] + s_x[1]) + (s_x[2] + s_x[3])
    sz = [go(s_z.at[zi], s_z.at[zi], dev(xi, step(zi, n), q)) for n in (1, 2, 3)]
    drain(gen_d, 1)
    for c in sz:
        c.wait_recv()
    s_c[q] = (s_z[0] + s_z[1]) + (s_z[2] + s_z[3])
    sc = [go(s_c.at[q], s_c.at[q], dev(xi, zi, (q + n) % 8)) for n in range(1, 8)]
    for c in sc:
        c.wait_recv()
    for r in range(4):
        gg_ref[r * 16 : (r + 1) * 16] = (s_c[2 * r] + s_c[2 * r + 1]) / gain64_ref[r * 16 : (r + 1) * 16]
    xf = x_ref[...].astype(F32)
    cen = xf - jnp.mean(xf, axis=1, keepdims=True)
    inv = lax.rsqrt(jnp.mean(cen * cen, axis=1, keepdims=True) + 1e-05)
    hat = cen * inv
    for c in last[1]:
        c.wait_recv()
    parts = [
        e_buf[1, 2 * r].astype(F32) + e_buf[1, 2 * r + 1].astype(F32) for r in range(4)
    ]
    d = jnp.concatenate(parts, axis=1)
    g = d * gain_ref[...]
    back = inv * (
        g - jnp.mean(g, axis=1, keepdims=True) - hat * jnp.mean(g * hat, axis=1, keepdims=True)
    )
    gin_ref[...] = (og_ref[...].astype(F32) + back).astype(BF)
    finish()


def hand_over(n, *refs):
    ins, outs, bufs = refs[:n], refs[n : 2 * n], refs[2 * n : 3 * n]
    sem_in, sem_out = refs[3 * n :]
    moves, i = [], 0
    for a, o, b in zip(ins, outs, bufs):
        parts = 4 if a.shape[0] > 64 else 1
        rows = a.shape[0] // parts
        for p in range(parts):
            r = pl.ds(p * rows, rows)
            moves.append(
                (
                    pltpu.make_async_copy(a.at[r], b.at[r], sem_in.at[i]),
                    pltpu.make_async_copy(b.at[r], o.at[r], sem_out.at[i]),
                )
            )
            i += 1
    for get, _ in moves:
        get.start()
    for get, give in moves:
        get.wait()
        give.start()
    for _, give in moves:
        give.wait()


def shards(inputs, layer_norm_gain, w_in, w_out, pattern_in, pattern_out, out_grad):
    vm = functools.partial(pl.BlockSpec, memory_space=pltpu.VMEM)
    hbm = functools.partial(pl.BlockSpec, memory_space=pl.ANY)
    V = pltpu.VMEM
    out = pl.pallas_call(
        kernel,
        out_shape=(
            jax.ShapeDtypeStruct((8, 8192), BF),
            jax.ShapeDtypeStruct((8, 8192), BF),
            jax.ShapeDtypeStruct((2048, 512), BF),
            jax.ShapeDtypeStruct((512, 2048), BF),
            jax.ShapeDtypeStruct((64, 128), F32),
        ),
        in_specs=[vm(), vm(), vm(), vm(), hbm(), hbm(), vm(), vm()],
        out_specs=(vm(), vm(), hbm(), hbm(), vm()),
        scratch_shapes=[
            V((2048, 512), BF),
            V((512, 2048), BF),
            V((8, 512), F32),
            V((2, 2048), F32),
            V((4, 8, 2048), BF),
            V((8, 8, 2048), BF),
            V((8, 8, 2048), BF),
            V((2, 4, 4, 64, 1024), BF),
            V((2, 4, 4, 64, 1024), BF),
            V((2, 2, 256, 512), BF),
            V((2, 2, 256, 512), BF),
            V((2, 2, 256, 512), BF),
            V((2, 2, 256, 512), BF),
            V((2, 2, 256, 512), F32),
            V((4, 4, 64, 512), BF),
            V((4, 4, 64, 512), BF),
            V((2, 2, 4, 64, 1024), BF),
            V((2, 2, 4, 64, 1024), BF),
            V((2, 2, 2, 4, 64, 1024), BF),
            V((2, 2, 2, 4, 64, 1024), BF),
            V((2, 3, 4, 64, 1024), F32),
            V((2, 2, 64, 1024), BF),
            V((2, 2, 2, 32, 1024), BF),
            V((2, 2, 2, 64, 1024), BF),
            V((2, 2, 2, 64, 1024), BF),
            V((2, 8, 8, 2048), BF),
            V((2, 8, 8, 2048), BF),
            V((2048, 512), BF),
            V((512, 2048), BF),
            V((4, 16, 128), F32),
            V((4, 16, 128), F32),
            V((8, 16, 128), F32),
            pltpu.SemaphoreType.DMA((N_COPIES,)),
            pltpu.SemaphoreType.DMA((N_COPIES,)),
            pltpu.SemaphoreType.DMA((2,)),
        ],
        compiler_params=pltpu.CompilerParams(
            collective_id=0, has_side_effects=True, vmem_limit_bytes=67_043_328
        ),
        name="ffn",
    )(
        inputs, layer_norm_gain.reshape(1, 8192), layer_norm_gain.reshape(64, 128), out_grad,
        w_in, w_out, pattern_in.T, pattern_out,
    )
    output, grad_inputs, g_in, g_out, g_gain = pl.pallas_call(
        functools.partial(hand_over, len(out)),
        out_shape=tuple(jax.ShapeDtypeStruct(o.shape, o.dtype) for o in out),
        in_specs=[hbm()] * len(out),
        out_specs=(hbm(),) * len(out),
        scratch_shapes=[V(o.shape, o.dtype) for o in out]
        + [pltpu.SemaphoreType.DMA((16,)), pltpu.SemaphoreType.DMA((16,))],
        name="hand_over",
    )(*out)
    return output, grad_inputs, g_in, g_out, g_gain.reshape(8192)


def solution(mesh):
    in_specs = (
        P(("row", "col"), None),
        P(),
        P("row", "col"),
        P("col", "row"),
        P(),
        P(),
        P(("row", "col"), None),
    )
    out_specs = (
        P(("row", "col"), None),
        P(("row", "col"), None),
        P("row", "col"),
        P("col", "row"),
        P(),
    )
    return jax.shard_map(shards, mesh=mesh, in_specs=in_specs, out_specs=out_specs, check_vma=False)
```

```python
import functools

import jax
import jax.numpy as jnp
from jax import lax
from jax.experimental import pallas as pl
from jax.experimental.pallas import tpu as pltpu
from jax.sharding import PartitionSpec as P

BF = jnp.bfloat16
F32 = jnp.float32
N_COPIES = 256


def gelu_value(h):
    inner = 0.7978845608 * (h + 0.044715 * h * h * h)
    return 0.5 * h * (1.0 + jnp.tanh(inner))


def gelu_slope(h):
    tanh_v = jnp.tanh(0.7978845608 * (h + 0.044715 * h * h * h))
    return 0.5 * (1.0 + tanh_v) + 0.5 * h * (1.0 - tanh_v * tanh_v) * 0.7978845608 * (
        1.0 + 0.134145 * h * h
    )


def dot_nn(a, b):
    return lax.dot_general(a, b, (((1,), (0,)), ((), ())), preferred_element_type=F32)


def dot_nt(a, b):
    return lax.dot_general(a, b, (((1,), (1,)), ((), ())), preferred_element_type=F32)


def dot_tn(a, b):
    return lax.dot_general(a, b, (((0,), (0,)), ((), ())), preferred_element_type=F32)


class Sent:
    def __init__(self, c):
        self.c, self.got = c, False
        c.start()

    def wait_recv(self):
        self.got = True
        self.c.wait_recv()


def kernel(
    x_ref, gain_ref, gain64_ref, og_ref, win_hbm, wout_hbm, pin_ref, pout_ref,
    out_ref, gin_ref, gwin_ref, gwout_ref, gg_ref,
    win, wout, min_ref, mout_ref, normed, s0x, s0g, gx, gg,
    ar_send, ar_recv, ay_send, ay_recv, acc, act, dpre,
    rs_far, rs_half, rs_full, rs_in, rs_p,
    ru_far, ru_half, ru_full, ru_in,
    rfin, e_buf, gw1, gw2, s_x, s_z, s_c,
    send_sem, recv_sem, w_sem,
):
    row = lax.axis_index("row")
    col = lax.axis_index("col")
    xi, zi, yl = col // 8, (col // 2) % 4, col % 2
    yh, core = row // 2, row % 2
    q = row * 2 + yl

    def dev(x, z, qq):
        return (qq // 2, (x * 4 + z) * 2 + qq % 2)

    sent = []
    outs = []

    def go(src, dst, to):
        i = len(sent)
        c = Sent(
            pltpu.make_async_remote_copy(
                src_ref=src, dst_ref=dst, send_sem=send_sem.at[i], recv_sem=recv_sem.at[i],
                device_id=to, device_id_type=pl.DeviceIdType.MESH,
            )
        )
        sent.append(c)
        return c

    def finish():
        for c in sent:
            if not c.got:
                c.wait_recv()
        for c in sent:
            c.c.wait_send()
        for o in outs:
            o.wait()

    def step(i, n):
        return (i + n + 4) % 4

    sibling = (yh * 2 + (1 - core), col)
    partner = ((1 - yh) * 2 + core, col)

    barrier = pltpu.get_barrier_semaphore()
    peers = [dev(xi, zi, (q + n) % 8) for n in range(1, 8)]
    peers += [dev(step(xi, n), zi, q) for n in (1, 2, 3)]
    peers += [dev(xi, step(zi, n), q) for n in (1, 2, 3)]
    for p in peers:
        pl.semaphore_signal(barrier, inc=1, device_id=p, device_id_type=pl.DeviceIdType.MESH)

    w_in_copy = pltpu.make_async_copy(win_hbm, win, w_sem.at[0])
    w_out_copy = pltpu.make_async_copy(wout_hbm, wout, w_sem.at[1])
    w_in_copy.start()
    w_out_copy.start()

    xf = x_ref[...].astype(F32)
    cen = xf - jnp.mean(xf, axis=1, keepdims=True)
    inv = lax.rsqrt(jnp.mean(cen * cen, axis=1, keepdims=True) + 1e-05)
    nrm = (cen * inv * gain_ref[...]).astype(BF)
    for r in range(4):
        normed[r] = nrm[:, r * 2048 : (r + 1) * 2048]
    pl.semaphore_wait(barrier, len(peers))

    def column_in(src_of, dst):
        cs = []
        for n in range(1, 8):
            qq = (q + n) % 8
            cs.append(go(src_of(qq), dst.at[q], dev(xi, zi, qq)))
        return cs

    c0x = column_in(lambda qq: normed.at[qq // 2], s0x)
    s0x[q] = normed[row]
    s0g[q] = og_ref[:, pl.ds(pl.multiple_of(row * 2048, 2048), 2048)]

    lane = lax.broadcasted_iota(jnp.int32, (16, 64), 1)
    tile = lax.broadcasted_iota(jnp.int32, (16, 128), 1) + row * 8
    for h in range(2):
        rows = jnp.max(jnp.where(lane == col * 2 + h, pin_ref[...], -1), axis=1, keepdims=True)
        kept = jnp.max(jnp.where(rows == tile, 1.0, 0.0), axis=0, keepdims=True)
        for t in range(8):
            min_ref[t : t + 1, h * 256 : (h + 1) * 256] = jnp.broadcast_to(
                kept[:, t : t + 1], (1, 256)
            )
    pout = pout_ref[pl.ds(pl.multiple_of(row * 8, 8), 8), :]
    for h in range(2):
        kept = jnp.max(jnp.where(pout == col * 2 + h, 1.0, 0.0), axis=1, keepdims=True)
        for t in range(8):
            mout_ref[h : h + 1, t * 256 : (t + 1) * 256] = jnp.broadcast_to(
                kept[t : t + 1], (1, 256)
            )

    def blk(g, k, u, v):
        return g.at[0, v, u] if k == 0 else g.at[1, u, v]

    def colours():
        st = []
        for k in range(2):
            u0, v0 = (zi, xi) if k == 0 else (xi, zi)

            def to_z(n):
                return dev(xi, step(zi, n), q)

            def to_x(n):
                return dev(step(xi, n), zi, q)

            st.append(
                dict(
                    k=k, u0=u0, v0=v0, to_u=to_z if k == 0 else to_x, to_v=to_x if k == 0 else to_z
                )
            )
        return st

    def gather(s0, g, arrived):
        for c in arrived:
            c.wait_recv()
        block = s0[...].reshape(64, 2048)
        g[0, xi, zi] = block[:, :1024]
        g[1, xi, zi] = block[:, 1024:]
        st = colours()

        def one(s, off, n, v=None):
            b = blk(g, s["k"], step(s["u0"], off), s["v0"] if v is None else v)
            return go(b, b, s["to_v"](n))

        def both(s, off):
            s["s", off] = {n: one(s, off, n) for n in (1, -1)}

        for s in st:
            b = blk(g, s["k"], s["u0"], s["v0"])
            s["f"] = {n: go(b, b, s["to_u"](n)) for n in (1, -1)}
            both(s, 0)
            s["f2"], s["s2"] = {}, {}
        yield
        for n in (1, -1):
            for s in st:
                s["f"][n].wait_recv()
                b = blk(g, s["k"], step(s["u0"], -n), s["v0"])
                part = b.at[pl.ds(0, 32)] if n == 1 else b.at[pl.ds(32, 32)]
                s["f2"][n] = go(part, part, s["to_u"](n))
                both(s, -n)
            yield

        def relay(s, off, n):
            s["s", off][n].wait_recv()
            s["s2"][off] = one(s, off, n, step(s["v0"], -n))

        for s in st:
            relay(s, 0, 1)
        yield
        for s in st:
            s["f2"][1].wait_recv()
            s["f2"][-1].wait_recv()
            both(s, 2)
        for s in st:
            s["s", 0][-1].wait_recv()
        yield
        for off in (-1, 1, 2):
            n = 1 if off == 1 else -1
            for s in st:
                relay(s, off, n)
            for s in st:
                s["s", off][-n].wait_recv()
            yield
        for off in (0, -1, 1, 2):
            for s in st:
                s["s2"][off].wait_recv()
            yield

    def drain(g, n):
        for _ in range(n):
            next(g, None)

    gen_x = gather(s0x, gx, c0x)
    c0g = []
    gen_g = gather(s0g, gg, c0g)

    def partial(g, w, nt, xx):
        a = g[0, xx].reshape(256, 1024)
        b = g[1, xx].reshape(256, 1024)
        if nt:
            return dot_nt(a, w[:, :1024]) + dot_nt(b, w[:, 1024:])
        return dot_nn(a, w[:1024]) + dot_nn(b, w[1024:])

    def x_of(p, mine):
        c = core if mine else 1 - core
        return (xi + (4 - c if p == 0 else 1 + c)) % 4

    side = ((gx, win, False), (gg, wout, True))

    def row_other(i, p):
        ar_send[i, p] = partial(*side[i], x_of(p, False)).astype(BF)
        return go(ar_send.at[i, p], ar_recv.at[i, p], sibling)

    def row_mine(i, p):
        acc[i, p] = partial(*side[i], x_of(p, True))

    def row_add(i, p, c):
        c.wait_recv()
        v = acc[i, p] + ar_recv[i, p].astype(F32)
        acc[i, p] = v
        ay_send[i, p] = v.astype(BF)
        return go(ay_send.at[i, p], ay_recv.at[i, p], partner)

    def rows_loop(f):
        def body(m, _):
            f(m, pl.ds(pl.multiple_of(m * 64, 64), 64))
            return 0

        lax.fori_loop(0, 4, body, 0)

    def row_act(p, c):
        c.wait_recv()
        xx = x_of(p, True)

        def rows_of(m, rows):
            pre = acc[0, p, rows] + ay_recv[0, p, rows].astype(F32)
            acc[0, p, rows] = pre
            act[xx, m] = gelu_value(pre).astype(BF)

        rows_loop(rows_of)
        return go(act.at[xx], act.at[xx], sibling)

    def row_dpre(p, c):
        c.wait_recv()
        xx = x_of(p, True)

        def rows_of(m, rows):
            d = acc[1, p, rows] + ay_recv[1, p, rows].astype(F32)
            dpre[xx, m] = (d * gelu_slope(acc[0, p, rows])).astype(BF)

        rows_loop(rows_of)
        return go(dpre.at[xx], dpre.at[xx], sibling)

    def term(t, k, v):
        if t == 0:
            a = act[v] if k == 0 else act[:, v]
            r = dot_nn(a.reshape(256, 512), wout[:, k * 1024 : (k + 1) * 1024])
        else:
            a = dpre[v] if k == 0 else dpre[:, v]
            r = dot_nt(a.reshape(256, 512), win[k * 1024 : (k + 1) * 1024, :])
        return r.reshape(4, 64, 1024)

    last = {}

    def scatter(t):
        st = colours()
        with_half = {1: (2, -1), -1: (1, 0)}
        for s in st:
            k = s["k"]
            rs_far[t, k] = term(t, k, step(s["v0"], 2)).astype(BF)
            s["h"], s["w"], s["uw"] = {}, {}, {}
            for i in range(2):
                for n in (1, -1):
                    off = with_half[n][i]
                    u = step(s["u0"], off)
                    s["h"][off] = go(rs_far.at[t, k, u], rs_half.at[t, k, u], s["to_v"](n))
        yield

        def piece(s, n, off):
            k, u, j = s["k"], step(s["u0"], off), 0 if n == 1 else 1
            p = rs_p[k, j, u]
            if off in with_half[n]:
                s["h"][off].wait_recv()
                p = p + rs_half[t, k, u].astype(F32)
            rs_full[t, k, j, u] = p.astype(BF)
            s["w"][n, off] = go(rs_full.at[t, k, j, u], rs_in.at[t, k, j, u], s["to_v"](n))

        for n, off in ((-1, 2), (1, 1)):
            for s in st:
                rs_p[s["k"], 0 if n == 1 else 1] = term(t, s["k"], step(s["v0"], n))
                piece(s, n, off)
        yield
        for n, off in ((-1, -1), (1, 2)):
            for s in st:
                piece(s, n, off)
        yield
        for n, off in ((-1, 1), (1, -1)):
            for s in st:
                piece(s, n, off)
        for s in st:
            rs_p[s["k"], 2] = term(t, s["k"], s["v0"])
        yield

        def summed(s, off):
            k, u = s["k"], step(s["u0"], off)
            s["w"][1, off].wait_recv()
            s["w"][-1, off].wait_recv()
            return rs_p[k, 2, u] + rs_in[t, k, 0, u].astype(F32) + rs_in[t, k, 1, u].astype(F32)

        for s in st:
            k = s["k"]
            ru_far[t, k] = summed(s, 2).astype(BF)
            s["uh"] = {
                n: go(
                    ru_far.at[t, k, pl.ds(0 if n == 1 else 32, 32)],
                    ru_half.at[t, k, 0 if n == 1 else 1],
                    s["to_u"](n),
                )
                for n in (1, -1)
            }
        for s in st:
            for n in (1, -1):
                piece(s, n, 0)
        yield
        for n in (-1, 1):
            for s in st:
                k, j = s["k"], 0 if n == 1 else 1
                p = summed(s, n)
                s["uh"][n].wait_recv()
                extra = ru_half[t, k, j].astype(F32)
                lo, hi = p[0:32], p[32:64]
                if n == 1:
                    lo = lo + extra
                else:
                    hi = hi + extra
                ru_full[t, k, j, 0:32] = lo.astype(BF)
                ru_full[t, k, j, 32:64] = hi.astype(BF)
                s["uw"][n] = go(ru_full.at[t, k, j], ru_in.at[t, k, j], s["to_u"](n))
        yield
        for s in st:
            k = s["k"]
            r = summed(s, 0)
            s["uw"][1].wait_recv()
            s["uw"][-1].wait_recv()
            r = r + ru_in[t, k, 0].astype(F32) + ru_in[t, k, 1].astype(F32)
            rfin[t, :, :, k * 1024 : (k + 1) * 1024] = r.astype(BF).reshape(8, 8, 1024)
        last[t] = [
            go(rfin.at[t, (q + n) % 8], e_buf.at[t, q], dev(xi, zi, (q + n) % 8))
            for n in range(1, 8)
        ]
        e_buf[t, q] = rfin[t, q]
        yield

    ones = jnp.ones((8, 512), BF)

    def grad_in_tiles(k, lo, hi):
        def win_tile(j, _):
            lanes = pl.ds(pl.multiple_of(j * 256, 256), 256)
            ft = k * 4 + j
            a = gx[k, :, :, :, lanes].reshape(1024, 256)
            raw = dot_tn(a, dpre[...].reshape(1024, 512))
            rows = pl.ds(pl.multiple_of(ft * 256, 256), 256)
            gw1[rows] = (raw * min_ref[pl.ds(ft, 1)]).astype(BF)
            p = raw * win[rows].astype(F32)
            hi = p.astype(BF)
            lo = (p - hi.astype(F32)).astype(BF)
            s = dot_nt(ones, hi) + dot_nt(ones, lo)
            s_x[xi, pl.ds(2 * ft, 1)] = s[0:1, :128]
            s_x[xi, pl.ds(2 * ft + 1, 1)] = s[0:1, 128:]
            return 0

        lax.fori_loop(lo, hi, win_tile, 0)

    def grad_out_tiles(k, lo, hi):
        def wout_tile(j, _):
            lanes = pl.ds(pl.multiple_of(j * 256, 256), 256)
            b = gg[k, :, :, :, lanes].reshape(1024, 256)
            raw = dot_tn(act[...].reshape(1024, 512), b)
            cols = pl.ds(pl.multiple_of(k * 1024 + j * 256, 256), 256)
            for h in range(2):
                gw2[h * 256 : (h + 1) * 256, cols] = (
                    raw[h * 256 : (h + 1) * 256] * mout_ref[h : h + 1, cols]
                ).astype(BF)
            return 0

        lax.fori_loop(lo, hi, wout_tile, 0)

    def put(src, dst, i):
        o = pltpu.make_async_copy(src, dst, w_sem.at[i])
        o.start()
        outs.append(o)

    drain(gen_x, 1)
    c0g += column_in(
        lambda qq: og_ref.at[:, pl.ds(pl.multiple_of((qq // 2) * 2048, 2048), 2048)], s0g
    )
    w_in_copy.wait()
    for t in range(8):
        win[t * 256 : (t + 1) * 256] = win[t * 256 : (t + 1) * 256] * min_ref[t : t + 1].astype(BF)
    w_out_copy.wait()
    for t in range(2):
        wout[t * 256 : (t + 1) * 256] = wout[t * 256 : (t + 1) * 256] * mout_ref[t : t + 1].astype(BF)
    drain(gen_x, 7)
    drain(gen_g, 1)
    drain(gen_x, 2)
    ca0 = row_other(0, 0)
    row_mine(0, 0)
    drain(gen_g, 2)
    cb0 = row_add(0, 0, ca0)
    drain(gen_x, 2)
    ca1 = row_other(0, 1)
    drain(gen_g, 1)
    row_mine(0, 1)
    cb1 = row_add(0, 1, ca1)
    drain(gen_g, 2)
    cc0 = row_act(0, cb0)
    drain(gen_g, 1)
    cc1 = row_act(1, cb1)
    drain(gen_g, 1)
    cc0.wait_recv()
    cc1.wait_recv()
    gen_o = scatter(0)
    drain(gen_o, 1)
    drain(gen_g, 2)
    da0 = row_other(1, 0)
    drain(gen_o, 1)
    row_mine(1, 0)
    db0 = row_add(1, 0, da0)
    drain(gen_g, 2)
    da1 = row_other(1, 1)
    row_mine(1, 1)
    db1 = row_add(1, 1, da1)
    drain(gen_o, 2)
    grad_out_tiles(0, 0, 2)
    dc0 = row_dpre(0, db0)
    drain(gen_o, 1)
    grad_out_tiles(0, 2, 4)
    drain(gen_o, 1)
    dc1 = row_dpre(1, db1)
    dc0.wait_recv()
    dc1.wait_recv()
    gen_d = scatter(1)
    drain(gen_d, 1)
    drain(gen_o, 1)
    drain(gen_d, 1)
    grad_out_tiles(1, 0, 2)
    drain(gen_d, 1)
    grad_out_tiles(1, 2, 4)
    put(gw2, gwout_ref, 1)
    drain(gen_d, 1)
    grad_in_tiles(0, 0, 4)
    drain(gen_d, 1)
    grad_in_tiles(1, 0, 4)
    put(gw1, gwin_ref, 0)
    sx = [go(s_x.at[xi], s_x.at[xi], dev(step(xi, n), zi, q)) for n in (1, 2, 3)]
    for c in last[0]:
        c.wait_recv()
    for r in range(4):
        f = slice(r * 2048, (r + 1) * 2048)
        o = e_buf[0, 2 * r].astype(F32) + e_buf[0, 2 * r + 1].astype(F32)
        out_ref[:, f] = (x_ref[:, f].astype(F32) + o).astype(BF)
    drain(gen_d, 1)
    for c in sx:
        c.wait_recv()
    s_z[zi] = (s_x[0] + s_x[1]) + (s_x[2] + s_x[3])
    sz = [go(s_z.at[zi], s_z.at[zi], dev(xi, step(zi, n), q)) for n in (1, 2, 3)]
    drain(gen_d, 1)
    for c in sz:
        c.wait_recv()
    s_c[q] = (s_z[0] + s_z[1]) + (s_z[2] + s_z[3])
    sc = [go(s_c.at[q], s_c.at[q], dev(xi, zi, (q + n) % 8)) for n in range(1, 8)]
    for c in sc:
        c.wait_recv()
    for r in range(4):
        gg_ref[r * 16 : (r + 1) * 16] = (s_c[2 * r] + s_c[2 * r + 1]) / gain64_ref[r * 16 : (r + 1) * 16]
    xf = x_ref[...].astype(F32)
    cen = xf - jnp.mean(xf, axis=1, keepdims=True)
    inv = lax.rsqrt(jnp.mean(cen * cen, axis=1, keepdims=True) + 1e-05)
    hat = cen * inv
    for c in last[1]:
        c.wait_recv()
    parts = [
        e_buf[1, 2 * r].astype(F32) + e_buf[1, 2 * r + 1].astype(F32) for r in range(4)
    ]
    d = jnp.concatenate(parts, axis=1)
    g = d * gain_ref[...]
    back = inv * (
        g - jnp.mean(g, axis=1, keepdims=True) - hat * jnp.mean(g * hat, axis=1, keepdims=True)
    )
    gin_ref[...] = (og_ref[...].astype(F32) + back).astype(BF)
    finish()


def hand_over(n, *refs):
    ins, outs, bufs = refs[:n], refs[n : 2 * n], refs[2 * n : 3 * n]
    sem_in, sem_out = refs[3 * n :]
    moves, i = [], 0
    for a, o, b in zip(ins, outs, bufs):
        parts = 4 if a.shape[0] > 64 else 1
        rows = a.shape[0] // parts
        for p in range(parts):
            r = pl.ds(p * rows, rows)
            moves.append(
                (
                    pltpu.make_async_copy(a.at[r], b.at[r], sem_in.at[i]),
                    pltpu.make_async_copy(b.at[r], o.at[r], sem_out.at[i]),
                )
            )
            i += 1
    for get, _ in moves:
        get.start()
    for get, give in moves:
        get.wait()
        give.start()
    for _, give in moves:
        give.wait()


def shards(inputs, layer_norm_gain, w_in, w_out, pattern_in, pattern_out, out_grad):
    vm = functools.partial(pl.BlockSpec, memory_space=pltpu.VMEM)
    hbm = functools.partial(pl.BlockSpec, memory_space=pl.ANY)
    V = pltpu.VMEM
    out = pl.pallas_call(
        kernel,
        out_shape=(
            jax.ShapeDtypeStruct((8, 8192), BF),
            jax.ShapeDtypeStruct((8, 8192), BF),
            jax.ShapeDtypeStruct((2048, 512), BF),
            jax.ShapeDtypeStruct((512, 2048), BF),
            jax.ShapeDtypeStruct((64, 128), F32),
        ),
        in_specs=[vm(), vm(), vm(), vm(), hbm(), hbm(), vm(), vm()],
        out_specs=(vm(), vm(), hbm(), hbm(), vm()),
        scratch_shapes=[
            V((2048, 512), BF),
            V((512, 2048), BF),
            V((8, 512), F32),
            V((2, 2048), F32),
            V((4, 8, 2048), BF),
            V((8, 8, 2048), BF),
            V((8, 8, 2048), BF),
            V((2, 4, 4, 64, 1024), BF),
            V((2, 4, 4, 64, 1024), BF),
            V((2, 2, 256, 512), BF),
            V((2, 2, 256, 512), BF),
            V((2, 2, 256, 512), BF),
            V((2, 2, 256, 512), BF),
            V((2, 2, 256, 512), F32),
            V((4, 4, 64, 512), BF),
            V((4, 4, 64, 512), BF),
            V((2, 2, 4, 64, 1024), BF),
            V((2, 2, 4, 64, 1024), BF),
            V((2, 2, 2, 4, 64, 1024), BF),
            V((2, 2, 2, 4, 64, 1024), BF),
            V((2, 3, 4, 64, 1024), F32),
            V((2, 2, 64, 1024), BF),
            V((2, 2, 2, 32, 1024), BF),
            V((2, 2, 2, 64, 1024), BF),
            V((2, 2, 2, 64, 1024), BF),
            V((2, 8, 8, 2048), BF),
            V((2, 8, 8, 2048), BF),
            V((2048, 512), BF),
            V((512, 2048), BF),
            V((4, 16, 128), F32),
            V((4, 16, 128), F32),
            V((8, 16, 128), F32),
            pltpu.SemaphoreType.DMA((N_COPIES,)),
            pltpu.SemaphoreType.DMA((N_COPIES,)),
            pltpu.SemaphoreType.DMA((2,)),
        ],
        compiler_params=pltpu.CompilerParams(
            collective_id=0, has_side_effects=True, vmem_limit_bytes=67_043_328
        ),
        name="ffn",
    )(
        inputs, layer_norm_gain.reshape(1, 8192), layer_norm_gain.reshape(64, 128), out_grad,
        w_in, w_out, pattern_in.T, pattern_out,
    )
    output, grad_inputs, g_in, g_out, g_gain = pl.pallas_call(
        functools.partial(hand_over, len(out)),
        out_shape=tuple(jax.ShapeDtypeStruct(o.shape, o.dtype) for o in out),
        in_specs=[hbm()] * len(out),
        out_specs=(hbm(),) * len(out),
        scratch_shapes=[V(o.shape, o.dtype) for o in out]
        + [pltpu.SemaphoreType.DMA((16,)), pltpu.SemaphoreType.DMA((16,))],
        name="hand_over",
    )(*out)
    return output, grad_inputs, g_in, g_out, g_gain.reshape(8192)


def solution(mesh):
    in_specs = (
        P(("row", "col"), None),
        P(),
        P("row", "col"),
        P("col", "row"),
        P(),
        P(),
        P(("row", "col"), None),
    )
    out_specs = (
        P(("row", "col"), None),
        P(("row", "col"), None),
        P("row", "col"),
        P("col", "row"),
        P(),
    )
    return jax.shard_map(shards, mesh=mesh, in_specs=in_specs, out_specs=out_specs, check_vma=False)
```

```python
import functools

import jax
import jax.numpy as jnp
from jax import lax
from jax.experimental import pallas as pl
from jax.experimental.pallas import tpu as pltpu
from jax.sharding import PartitionSpec as P

BF = jnp.bfloat16
F32 = jnp.float32
N_COPIES = 256
FAR_FIRST = ((1, 0, 0), (1, 1, 0), (0, 0, 1), (0, 1, 1), (1, 0, 1), (1, 1, 1), (0, 1, 0))


def gelu_value(h):
    inner = 0.7978845608 * (h + 0.044715 * h * h * h)
    return 0.5 * h * (1.0 + jnp.tanh(inner))


def gelu_slope(h):
    tanh_v = jnp.tanh(0.7978845608 * (h + 0.044715 * h * h * h))
    return 0.5 * (1.0 + tanh_v) + 0.5 * h * (1.0 - tanh_v * tanh_v) * 0.7978845608 * (
        1.0 + 0.134145 * h * h
    )


def dot_nn(a, b):
    return lax.dot_general(a, b, (((1,), (0,)), ((), ())), preferred_element_type=F32)


def dot_nt(a, b):
    return lax.dot_general(a, b, (((1,), (1,)), ((), ())), preferred_element_type=F32)


def dot_tn(a, b):
    return lax.dot_general(a, b, (((0,), (0,)), ((), ())), preferred_element_type=F32)


class Sent:
    def __init__(self, c):
        self.c, self.got = c, False
        c.start()

    def wait_recv(self):
        self.got = True
        self.c.wait_recv()


def kernel(
    x_ref, gain_ref, gain64_ref, og_ref, win_hbm, wout_hbm, pin_ref, pout_ref,
    out_ref, gin_ref, gw1, gw2, gg_ref,
    win, wout, min_ref, mout_ref, normed, s0x, s0g, gx, gg,
    ar_send, ar_recv, ay_send, ay_recv, acc, act, dpre,
    rs_far, rs_half, rs_full, rs_in, rs_p,
    ru_far, ru_half, ru_full, ru_in,
    rfin, e_buf, s_x, s_z, s_c,
    send_sem, recv_sem, w_sem,
):
    row = lax.axis_index("row")
    col = lax.axis_index("col")
    xi, zi, yl = col // 8, (col // 2) % 4, col % 2
    yh, core = row // 2, row % 2
    q = row * 2 + yl

    def dev(x, z, qq):
        return (qq // 2, (x * 4 + z) * 2 + qq % 2)

    sent = []

    def go(src, dst, to):
        i = len(sent)
        c = Sent(
            pltpu.make_async_remote_copy(
                src_ref=src, dst_ref=dst, send_sem=send_sem.at[i], recv_sem=recv_sem.at[i],
                device_id=to, device_id_type=pl.DeviceIdType.MESH,
            )
        )
        sent.append(c)
        return c

    def finish():
        for c in sent:
            if not c.got:
                c.wait_recv()
        for c in sent:
            c.c.wait_send()

    def step(i, n):
        return (i + n + 4) % 4

    def flip(h, c, y):
        return (yh + h) % 2 * 4 + (core + c) % 2 * 2 + (yl + y) % 2

    sibling = (yh * 2 + (1 - core), col)
    partner = ((1 - yh) * 2 + core, col)

    far_first = [flip(h, c, y) for h, c, y in FAR_FIRST]

    barrier = pltpu.get_barrier_semaphore()
    peers = [dev(xi, zi, (q + n) % 8) for n in range(1, 8)]
    peers += [dev(step(xi, n), zi, q) for n in (1, 2, 3)]
    peers += [dev(xi, step(zi, n), q) for n in (1, 2, 3)]
    for p in peers:
        pl.semaphore_signal(barrier, inc=1, device_id=p, device_id_type=pl.DeviceIdType.MESH)

    w_in_copy = pltpu.make_async_copy(win_hbm, win, w_sem.at[0])
    w_out_copy = pltpu.make_async_copy(wout_hbm, wout, w_sem.at[1])
    w_in_copy.start()
    w_out_copy.start()

    xf = x_ref[...].astype(F32)
    cen = xf - jnp.mean(xf, axis=1, keepdims=True)
    inv = lax.rsqrt(jnp.mean(cen * cen, axis=1, keepdims=True) + 1e-05)
    nrm = (cen * inv * gain_ref[...]).astype(BF)
    for r in range(4):
        normed[r] = nrm[:, r * 2048 : (r + 1) * 2048]
    pl.semaphore_wait(barrier, len(peers))

    def column_in(src_of, dst):
        cs = []
        for qq in far_first:
            cs.append(go(src_of(qq), dst.at[q], dev(xi, zi, qq)))
        return cs

    c0x = column_in(lambda qq: normed.at[qq // 2], s0x)
    s0x[q] = normed[row]
    s0g[q] = og_ref[:, pl.ds(pl.multiple_of(row * 2048, 2048), 2048)]

    lane = lax.broadcasted_iota(jnp.int32, (16, 64), 1)
    tile = lax.broadcasted_iota(jnp.int32, (16, 128), 1) + row * 8
    for h in range(2):
        rows = jnp.max(jnp.where(lane == col * 2 + h, pin_ref[...], -1), axis=1, keepdims=True)
        kept = jnp.max(jnp.where(rows == tile, 1.0, 0.0), axis=0, keepdims=True)
        for t in range(8):
            min_ref[t : t + 1, h * 256 : (h + 1) * 256] = jnp.broadcast_to(
                kept[:, t : t + 1], (1, 256)
            )
    pout = pout_ref[pl.ds(pl.multiple_of(row * 8, 8), 8), :]
    for h in range(2):
        kept = jnp.max(jnp.where(pout == col * 2 + h, 1.0, 0.0), axis=1, keepdims=True)
        for t in range(8):
            mout_ref[h : h + 1, t * 256 : (t + 1) * 256] = jnp.broadcast_to(
                kept[t : t + 1], (1, 256)
            )

    def blk(g, k, u, v):
        return g.at[0, v, u] if k == 0 else g.at[1, u, v]

    def colours():
        st = []
        for k in range(2):
            u0, v0 = (zi, xi) if k == 0 else (xi, zi)

            def to_z(n):
                return dev(xi, step(zi, n), q)

            def to_x(n):
                return dev(step(xi, n), zi, q)

            st.append(
                dict(
                    k=k, u0=u0, v0=v0, to_u=to_z if k == 0 else to_x, to_v=to_x if k == 0 else to_z
                )
            )
        return st

    def gather(s0, g, arrived):
        for c in arrived:
            c.wait_recv()
        block = s0[...].reshape(64, 2048)
        g[0, xi, zi] = block[:, :1024]
        g[1, xi, zi] = block[:, 1024:]
        st = colours()

        def one(s, off, n, v=None):
            b = blk(g, s["k"], step(s["u0"], off), s["v0"] if v is None else v)
            return go(b, b, s["to_v"](n))

        def both(s, off):
            s["s", off] = {n: one(s, off, n) for n in (1, -1)}

        for s in st:
            b = blk(g, s["k"], s["u0"], s["v0"])
            s["f"] = {n: go(b, b, s["to_u"](n)) for n in (1, -1)}
            both(s, 0)
            s["f2"], s["s2"] = {}, {}
        yield
        for n in (1, -1):
            for s in st:
                s["f"][n].wait_recv()
                b = blk(g, s["k"], step(s["u0"], -n), s["v0"])
                part = b.at[pl.ds(0, 32)] if n == 1 else b.at[pl.ds(32, 32)]
                s["f2"][n] = go(part, part, s["to_u"](n))
                both(s, -n)
            yield

        def relay(s, off, n):
            s["s", off][n].wait_recv()
            s["s2"][off] = one(s, off, n, step(s["v0"], -n))

        for s in st:
            relay(s, 0, 1)
        yield
        for s in st:
            s["f2"][1].wait_recv()
            s["f2"][-1].wait_recv()
            both(s, 2)
        for s in st:
            s["s", 0][-1].wait_recv()
        yield
        for off in (-1, 1, 2):
            n = 1 if off == 1 else -1
            for s in st:
                relay(s, off, n)
            for s in st:
                s["s", off][-n].wait_recv()
            yield
        for off in (0, -1, 1, 2):
            for s in st:
                s["s2"][off].wait_recv()
            yield

    def drain(g, n):
        for _ in range(n):
            next(g, None)

    gen_x = gather(s0x, gx, c0x)
    c0g = []
    gen_g = gather(s0g, gg, c0g)

    def partial(g, w, nt, xx):
        a = g[0, xx].reshape(256, 1024)
        b = g[1, xx].reshape(256, 1024)
        if nt:
            return dot_nt(a, w[:, :1024]) + dot_nt(b, w[:, 1024:])
        return dot_nn(a, w[:1024]) + dot_nn(b, w[1024:])

    def x_of(p, mine):
        c = core if mine else 1 - core
        return (xi + (4 - c if p == 0 else 1 + c)) % 4

    side = ((gx, win, False), (gg, wout, True))

    def row_other(i, p):
        ar_send[i, p] = partial(*side[i], x_of(p, False)).astype(BF)
        return go(ar_send.at[i, p], ar_recv.at[i, p], sibling)

    def row_mine(i, p):
        acc[i, p] = partial(*side[i], x_of(p, True))

    def row_add(i, p, c):
        c.wait_recv()
        v = acc[i, p] + ar_recv[i, p].astype(F32)
        acc[i, p] = v
        ay_send[i, p] = v.astype(BF)
        return go(ay_send.at[i, p], ay_recv.at[i, p], partner)

    def rows_loop(f):
        def body(m, _):
            f(m, pl.ds(pl.multiple_of(m * 64, 64), 64))
            return 0

        lax.fori_loop(0, 4, body, 0)

    def row_act(p, c):
        c.wait_recv()
        xx = x_of(p, True)

        def rows_of(m, rows):
            pre = acc[0, p, rows] + ay_recv[0, p, rows].astype(F32)
            acc[0, p, rows] = pre
            act[xx, m] = gelu_value(pre).astype(BF)

        rows_loop(rows_of)
        return go(act.at[xx], act.at[xx], sibling)

    def row_dpre(p, c):
        c.wait_recv()
        xx = x_of(p, True)

        def rows_of(m, rows):
            d = acc[1, p, rows] + ay_recv[1, p, rows].astype(F32)
            dpre[xx, m] = (d * gelu_slope(acc[0, p, rows])).astype(BF)

        rows_loop(rows_of)
        return go(dpre.at[xx], dpre.at[xx], sibling)

    def term(t, k, v):
        if t == 0:
            a = act[v] if k == 0 else act[:, v]
            r = dot_nn(a.reshape(256, 512), wout[:, k * 1024 : (k + 1) * 1024])
        else:
            a = dpre[v] if k == 0 else dpre[:, v]
            r = dot_nt(a.reshape(256, 512), win[k * 1024 : (k + 1) * 1024, :])
        return r.reshape(4, 64, 1024)

    last = {}

    def scatter(t):
        st = colours()
        with_half = {1: (2, -1), -1: (1, 0)}
        for s in st:
            k = s["k"]
            rs_far[t, k] = term(t, k, step(s["v0"], 2)).astype(BF)
            s["h"], s["w"], s["uw"] = {}, {}, {}
            for i in range(2):
                for n in (1, -1):
                    off = with_half[n][i]
                    u = step(s["u0"], off)
                    s["h"][off] = go(rs_far.at[t, k, u], rs_half.at[t, k, u], s["to_v"](n))
        yield

        def piece(s, n, off):
            k, u, j = s["k"], step(s["u0"], off), 0 if n == 1 else 1
            p = rs_p[k, j, u]
            if off in with_half[n]:
                s["h"][off].wait_recv()
                p = p + rs_half[t, k, u].astype(F32)
            rs_full[t, k, j, u] = p.astype(BF)
            s["w"][n, off] = go(rs_full.at[t, k, j, u], rs_in.at[t, k, j, u], s["to_v"](n))

        for n, off in ((-1, 2), (1, 1)):
            for s in st:
                rs_p[s["k"], 0 if n == 1 else 1] = term(t, s["k"], step(s["v0"], n))
                piece(s, n, off)
        yield
        for n, off in ((-1, -1), (1, 2)):
            for s in st:
                piece(s, n, off)
        yield
        for n, off in ((-1, 1), (1, -1)):
            for s in st:
                piece(s, n, off)
        for s in st:
            rs_p[s["k"], 2] = term(t, s["k"], s["v0"])
        yield

        def summed(s, off):
            k, u = s["k"], step(s["u0"], off)
            s["w"][1, off].wait_recv()
            s["w"][-1, off].wait_recv()
            return rs_p[k, 2, u] + rs_in[t, k, 0, u].astype(F32) + rs_in[t, k, 1, u].astype(F32)

        for s in st:
            k = s["k"]
            ru_far[t, k] = summed(s, 2).astype(BF)
            s["uh"] = {
                n: go(
                    ru_far.at[t, k, pl.ds(0 if n == 1 else 32, 32)],
                    ru_half.at[t, k, 0 if n == 1 else 1],
                    s["to_u"](n),
                )
                for n in (1, -1)
            }
        for s in st:
            for n in (1, -1):
                piece(s, n, 0)
        yield
        for n in (-1, 1):
            for s in st:
                k, j = s["k"], 0 if n == 1 else 1
                p = summed(s, n)
                s["uh"][n].wait_recv()
                extra = ru_half[t, k, j].astype(F32)
                lo, hi = p[0:32], p[32:64]
                if n == 1:
                    lo = lo + extra
                else:
                    hi = hi + extra
                ru_full[t, k, j, 0:32] = lo.astype(BF)
                ru_full[t, k, j, 32:64] = hi.astype(BF)
                s["uw"][n] = go(ru_full.at[t, k, j], ru_in.at[t, k, j], s["to_u"](n))
        yield
        for s in st:
            k = s["k"]
            r = summed(s, 0)
            s["uw"][1].wait_recv()
            s["uw"][-1].wait_recv()
            r = r + ru_in[t, k, 0].astype(F32) + ru_in[t, k, 1].astype(F32)
            rfin[t, :, :, k * 1024 : (k + 1) * 1024] = r.astype(BF).reshape(8, 8, 1024)
        last[t] = [
            go(rfin.at[t, qq], e_buf.at[t, q], dev(xi, zi, qq)) for qq in far_first
        ]
        e_buf[t, q] = rfin[t, q]
        yield

    ones = jnp.ones((8, 512), BF)

    def grad_in_tiles(k, lo, hi):
        def win_tile(j, _):
            lanes = pl.ds(pl.multiple_of(j * 256, 256), 256)
            ft = k * 4 + j
            a = gx[k, :, :, :, lanes].reshape(1024, 256)
            raw = dot_tn(a, dpre[...].reshape(1024, 512))
            rows = pl.ds(pl.multiple_of(ft * 256, 256), 256)
            gw1[rows] = (raw * min_ref[pl.ds(ft, 1)]).astype(BF)
            p = raw * win[rows].astype(F32)
            hi = p.astype(BF)
            lo = (p - hi.astype(F32)).astype(BF)
            s = dot_nt(ones, hi) + dot_nt(ones, lo)
            s_x[xi, pl.ds(2 * ft, 1)] = s[0:1, :128]
            s_x[xi, pl.ds(2 * ft + 1, 1)] = s[0:1, 128:]
            return 0

        lax.fori_loop(lo, hi, win_tile, 0)

    def grad_out_tiles(k, lo, hi):
        def wout_tile(j, _):
            lanes = pl.ds(pl.multiple_of(j * 256, 256), 256)
            b = gg[k, :, :, :, lanes].reshape(1024, 256)
            raw = dot_tn(act[...].reshape(1024, 512), b)
            cols = pl.ds(pl.multiple_of(k * 1024 + j * 256, 256), 256)
            for h in range(2):
                gw2[h * 256 : (h + 1) * 256, cols] = (
                    raw[h * 256 : (h + 1) * 256] * mout_ref[h : h + 1, cols]
                ).astype(BF)
            return 0

        lax.fori_loop(lo, hi, wout_tile, 0)

    drain(gen_x, 1)
    c0g += column_in(
        lambda qq: og_ref.at[:, pl.ds(pl.multiple_of((qq // 2) * 2048, 2048), 2048)], s0g
    )
    w_in_copy.wait()
    for t in range(8):
        win[t * 256 : (t + 1) * 256] = win[t * 256 : (t + 1) * 256] * min_ref[t : t + 1].astype(BF)
    w_out_copy.wait()
    for t in range(2):
        wout[t * 256 : (t + 1) * 256] = wout[t * 256 : (t + 1) * 256] * mout_ref[t : t + 1].astype(BF)
    drain(gen_x, 7)
    drain(gen_g, 1)
    drain(gen_x, 2)
    ca0 = row_other(0, 0)
    row_mine(0, 0)
    drain(gen_g, 2)
    cb0 = row_add(0, 0, ca0)
    drain(gen_x, 2)
    ca1 = row_other(0, 1)
    drain(gen_g, 1)
    row_mine(0, 1)
    cb1 = row_add(0, 1, ca1)
    drain(gen_g, 2)
    cc0 = row_act(0, cb0)
    drain(gen_g, 1)
    cc1 = row_act(1, cb1)
    drain(gen_g, 1)
    cc0.wait_recv()
    cc1.wait_recv()
    gen_o = scatter(0)
    drain(gen_o, 1)
    drain(gen_g, 2)
    da0 = row_other(1, 0)
    drain(gen_o, 1)
    row_mine(1, 0)
    db0 = row_add(1, 0, da0)
    drain(gen_g, 2)
    da1 = row_other(1, 1)
    row_mine(1, 1)
    db1 = row_add(1, 1, da1)
    drain(gen_o, 2)
    grad_out_tiles(0, 0, 2)
    dc0 = row_dpre(0, db0)
    drain(gen_o, 1)
    grad_out_tiles(0, 2, 4)
    drain(gen_o, 1)
    dc1 = row_dpre(1, db1)
    dc0.wait_recv()
    dc1.wait_recv()
    gen_d = scatter(1)
    drain(gen_d, 1)
    drain(gen_o, 1)
    drain(gen_d, 1)
    grad_out_tiles(1, 0, 2)
    drain(gen_d, 1)
    grad_out_tiles(1, 2, 4)
    drain(gen_d, 1)
    grad_in_tiles(0, 0, 4)
    drain(gen_d, 1)
    grad_in_tiles(1, 0, 4)
    sx = [go(s_x.at[xi], s_x.at[xi], dev(step(xi, n), zi, q)) for n in (1, 2, 3)]
    for c in last[0]:
        c.wait_recv()
    for r in range(4):
        f = slice(r * 2048, (r + 1) * 2048)
        o = e_buf[0, 2 * r].astype(F32) + e_buf[0, 2 * r + 1].astype(F32)
        out_ref[:, f] = (x_ref[:, f].astype(F32) + o).astype(BF)
    drain(gen_d, 1)
    for c in sx:
        c.wait_recv()
    s_z[zi] = (s_x[0] + s_x[1]) + (s_x[2] + s_x[3])
    sz = [go(s_z.at[zi], s_z.at[zi], dev(xi, step(zi, n), q)) for n in (1, 2, 3)]
    drain(gen_d, 1)
    for c in sz:
        c.wait_recv()
    s_c[q] = (s_z[0] + s_z[1]) + (s_z[2] + s_z[3])
    sc = [go(s_c.at[q], s_c.at[q], dev(xi, zi, (q + n) % 8)) for n in range(1, 8)]
    for c in sc:
        c.wait_recv()
    for r in range(4):
        gg_ref[r * 16 : (r + 1) * 16] = (s_c[2 * r] + s_c[2 * r + 1]) / gain64_ref[r * 16 : (r + 1) * 16]
    xf = x_ref[...].astype(F32)
    cen = xf - jnp.mean(xf, axis=1, keepdims=True)
    inv = lax.rsqrt(jnp.mean(cen * cen, axis=1, keepdims=True) + 1e-05)
    hat = cen * inv
    for c in last[1]:
        c.wait_recv()
    parts = [
        e_buf[1, 2 * r].astype(F32) + e_buf[1, 2 * r + 1].astype(F32) for r in range(4)
    ]
    d = jnp.concatenate(parts, axis=1)
    g = d * gain_ref[...]
    back = inv * (
        g - jnp.mean(g, axis=1, keepdims=True) - hat * jnp.mean(g * hat, axis=1, keepdims=True)
    )
    gin_ref[...] = (og_ref[...].astype(F32) + back).astype(BF)
    finish()


def hand_over(n, *refs):
    ins, outs, sem = refs[:n], refs[n : 2 * n], refs[2 * n]
    moves = [pltpu.make_async_copy(a, o, sem.at[i]) for i, (a, o) in enumerate(zip(ins, outs))]
    for m in moves:
        m.start()
    for m in moves:
        m.wait()


def shards(inputs, layer_norm_gain, w_in, w_out, pattern_in, pattern_out, out_grad):
    vm = functools.partial(pl.BlockSpec, memory_space=pltpu.VMEM)
    hbm = functools.partial(pl.BlockSpec, memory_space=pl.ANY)
    V = pltpu.VMEM
    out = pl.pallas_call(
        kernel,
        out_shape=(
            jax.ShapeDtypeStruct((8, 8192), BF),
            jax.ShapeDtypeStruct((8, 8192), BF),
            jax.ShapeDtypeStruct((2048, 512), BF),
            jax.ShapeDtypeStruct((512, 2048), BF),
            jax.ShapeDtypeStruct((64, 128), F32),
        ),
        in_specs=[vm(), vm(), vm(), vm(), hbm(), hbm(), vm(), vm()],
        out_specs=(vm(),) * 5,
        scratch_shapes=[
            V((2048, 512), BF),
            V((512, 2048), BF),
            V((8, 512), F32),
            V((2, 2048), F32),
            V((4, 8, 2048), BF),
            V((8, 8, 2048), BF),
            V((8, 8, 2048), BF),
            V((2, 4, 4, 64, 1024), BF),
            V((2, 4, 4, 64, 1024), BF),
            V((2, 2, 256, 512), BF),
            V((2, 2, 256, 512), BF),
            V((2, 2, 256, 512), BF),
            V((2, 2, 256, 512), BF),
            V((2, 2, 256, 512), F32),
            V((4, 4, 64, 512), BF),
            V((4, 4, 64, 512), BF),
            V((2, 2, 4, 64, 1024), BF),
            V((2, 2, 4, 64, 1024), BF),
            V((2, 2, 2, 4, 64, 1024), BF),
            V((2, 2, 2, 4, 64, 1024), BF),
            V((2, 3, 4, 64, 1024), F32),
            V((2, 2, 64, 1024), BF),
            V((2, 2, 2, 32, 1024), BF),
            V((2, 2, 2, 64, 1024), BF),
            V((2, 2, 2, 64, 1024), BF),
            V((2, 8, 8, 2048), BF),
            V((2, 8, 8, 2048), BF),
            V((4, 16, 128), F32),
            V((4, 16, 128), F32),
            V((8, 16, 128), F32),
            pltpu.SemaphoreType.DMA((N_COPIES,)),
            pltpu.SemaphoreType.DMA((N_COPIES,)),
            pltpu.SemaphoreType.DMA((2,)),
        ],
        compiler_params=pltpu.CompilerParams(
            collective_id=0, has_side_effects=True, vmem_limit_bytes=48 << 20
        ),
        name="ffn",
    )(
        inputs, layer_norm_gain.reshape(1, 8192), layer_norm_gain.reshape(64, 128), out_grad,
        w_in, w_out, pattern_in.T, pattern_out,
    )
    output, grad_inputs, g_in, g_out, g_gain = pl.pallas_call(
        functools.partial(hand_over, len(out)),
        out_shape=tuple(jax.ShapeDtypeStruct(o.shape, o.dtype) for o in out),
        in_specs=[vm()] * len(out),
        out_specs=(hbm(),) * len(out),
        scratch_shapes=[pltpu.SemaphoreType.DMA((len(out),))],
        compiler_params=pltpu.CompilerParams(vmem_limit_bytes=8 << 20),
        name="hand_over",
    )(*out)
    return output, grad_inputs, g_in, g_out, g_gain.reshape(8192)


def solution(mesh):
    in_specs = (
        P(("row", "col"), None),
        P(),
        P("row", "col"),
        P("col", "row"),
        P(),
        P(),
        P(("row", "col"), None),
    )
    out_specs = (
        P(("row", "col"), None),
        P(("row", "col"), None),
        P("row", "col"),
        P("col", "row"),
        P(),
    )
    return jax.shard_map(shards, mesh=mesh, in_specs=in_specs, out_specs=out_specs, check_vma=False)
```

```python
import functools

import jax
import jax.numpy as jnp
from jax import lax
from jax.experimental import pallas as pl
from jax.experimental.pallas import tpu as pltpu
from jax.sharding import PartitionSpec as P

BF = jnp.bfloat16
F32 = jnp.float32
N_COPIES = 256
SLICES = tuple((r, k) for r in range(4) for k in range(2))
FAR_FIRST = ((1, 0, 0), (1, 1, 0), (0, 0, 1), (0, 1, 1), (1, 0, 1), (1, 1, 1), (0, 1, 0))


def gelu_value(h):
    inner = 0.7978845608 * (h + 0.044715 * h * h * h)
    return 0.5 * h * (1.0 + jnp.tanh(inner))


def gelu_slope(h):
    tanh_v = jnp.tanh(0.7978845608 * (h + 0.044715 * h * h * h))
    return 0.5 * (1.0 + tanh_v) + 0.5 * h * (1.0 - tanh_v * tanh_v) * 0.7978845608 * (
        1.0 + 0.134145 * h * h
    )


def dot_nn(a, b):
    return lax.dot_general(a, b, (((1,), (0,)), ((), ())), preferred_element_type=F32)


def dot_nt(a, b):
    return lax.dot_general(a, b, (((1,), (1,)), ((), ())), preferred_element_type=F32)


def dot_tn(a, b):
    return lax.dot_general(a, b, (((0,), (0,)), ((), ())), preferred_element_type=F32)


class Sent:
    def __init__(self, c):
        self.c, self.got = c, False
        c.start()

    def wait_recv(self):
        self.got = True
        self.c.wait_recv()


def kernel(
    x_hbm, gain_hbm, gain64_hbm, og_hbm, win_hbm, wout_hbm, pin_hbm, pout_hbm,
    out_ref, gin_ref, gw1, gw2, gg_ref,
    x_ref, gain_ref, gain64_ref, og_ref, pin_ref, pout_ref,
    win, wout, min_ref, mout_ref, normed, s0x, s0g, gx, gg,
    ar_send, ar_recv, ay_send, ay_recv, acc, act, dpre,
    rs_far, rs_half, rs_full, rs_in, rs_p,
    ru_far, ru_half, ru_full, ru_in,
    rfin, e_buf, s_x, s_z, s_c,
    send_sem, recv_sem, w_sem,
):
    row = lax.axis_index("row")
    col = lax.axis_index("col")
    xi, zi, yl = col // 8, (col // 2) % 4, col % 2
    yh, core = row // 2, row % 2
    q = row * 2 + yl

    def dev(x, z, qq):
        return (qq // 2, (x * 4 + z) * 2 + qq % 2)

    sent = []

    def go(src, dst, to):
        i = len(sent)
        c = Sent(
            pltpu.make_async_remote_copy(
                src_ref=src, dst_ref=dst, send_sem=send_sem.at[i], recv_sem=recv_sem.at[i],
                device_id=to, device_id_type=pl.DeviceIdType.MESH,
            )
        )
        sent.append(c)
        return c

    def finish():
        for c in sent:
            if not c.got:
                c.wait_recv()
        for c in sent:
            c.c.wait_send()

    def step(i, n):
        return (i + n + 4) % 4

    def flip(h, c, y):
        return (yh + h) % 2 * 4 + (core + c) % 2 * 2 + (yl + y) % 2

    sibling = (yh * 2 + (1 - core), col)
    partner = ((1 - yh) * 2 + core, col)

    far_first = [flip(h, c, y) for h, c, y in FAR_FIRST]

    loads = [
        pltpu.make_async_copy(a, b, w_sem.at[i])
        for i, (a, b) in enumerate(
            (
                (x_hbm, x_ref),
                (gain_hbm, gain_ref),
                (og_hbm, og_ref),
                (pin_hbm, pin_ref),
                (pout_hbm, pout_ref),
                (gain64_hbm, gain64_ref),
                (win_hbm, win),
                (wout_hbm, wout),
            )
        )
    ]
    for c in loads:
        c.start()
    w_in_copy, w_out_copy = loads[6:]

    barrier = pltpu.get_barrier_semaphore()
    peers = [dev(xi, zi, (q + n) % 8) for n in range(1, 8)]
    peers += [dev(step(xi, n), zi, q) for n in (1, 2, 3)]
    peers += [dev(xi, step(zi, n), q) for n in (1, 2, 3)]
    for p in peers:
        pl.semaphore_signal(barrier, inc=1, device_id=p, device_id_type=pl.DeviceIdType.MESH)


    for c in loads[:2]:
        c.wait()
    xf = x_ref[...].astype(F32)
    cen = xf - jnp.mean(xf, axis=1, keepdims=True)
    inv = lax.rsqrt(jnp.mean(cen * cen, axis=1, keepdims=True) + 1e-05)
    nrm = (cen * inv * gain_ref[...]).astype(BF)
    for r in range(8):
        normed[r] = nrm[:, r * 1024 : (r + 1) * 1024]
    for c in loads[2:6]:
        c.wait()
    pl.semaphore_wait(barrier, len(peers))

    def column_in(src_of, dst):
        return [
            [go(src_of(qq // 2 * 2 + k), dst.at[k, q], dev(xi, zi, qq)) for qq in far_first]
            for k in range(2)
        ]

    c0x = column_in(lambda i: normed.at[i], s0x)
    for k in range(2):
        s0x[k, q] = normed[row * 2 + k]
        s0g[k, q] = og_ref[:, pl.ds(pl.multiple_of((row * 2 + k) * 1024, 1024), 1024)]

    lane = lax.broadcasted_iota(jnp.int32, (16, 64), 1)
    tile = lax.broadcasted_iota(jnp.int32, (16, 128), 1) + row * 8
    for h in range(2):
        rows = jnp.max(jnp.where(lane == col * 2 + h, pin_ref[...], -1), axis=1, keepdims=True)
        kept = jnp.max(jnp.where(rows == tile, 1.0, 0.0), axis=0, keepdims=True)
        for t in range(8):
            min_ref[t : t + 1, h * 256 : (h + 1) * 256] = jnp.broadcast_to(
                kept[:, t : t + 1], (1, 256)
            )
    pout = pout_ref[pl.ds(pl.multiple_of(row * 8, 8), 8), :]
    for h in range(2):
        kept = jnp.max(jnp.where(pout == col * 2 + h, 1.0, 0.0), axis=1, keepdims=True)
        for t in range(8):
            mout_ref[h : h + 1, t * 256 : (t + 1) * 256] = jnp.broadcast_to(
                kept[t : t + 1], (1, 256)
            )

    def blk(g, k, u, v):
        return g.at[0, v, u] if k == 0 else g.at[1, u, v]

    def colours():
        st = []
        for k in range(2):
            u0, v0 = (zi, xi) if k == 0 else (xi, zi)

            def to_z(n):
                return dev(xi, step(zi, n), q)

            def to_x(n):
                return dev(step(xi, n), zi, q)

            st.append(
                dict(
                    k=k, u0=u0, v0=v0, to_u=to_z if k == 0 else to_x, to_v=to_x if k == 0 else to_z
                )
            )
        return st

    def gather(s0, g, arrived):
        st = colours()

        def one(s, off, n, v=None):
            b = blk(g, s["k"], step(s["u0"], off), s["v0"] if v is None else v)
            return go(b, b, s["to_v"](n))

        def both(s, off):
            s["s", off] = {n: one(s, off, n) for n in (1, -1)}

        for s in st:
            for c in arrived[s["k"]]:
                c.wait_recv()
            g[s["k"], xi, zi] = s0[s["k"]].reshape(64, 1024)
            b = blk(g, s["k"], s["u0"], s["v0"])
            s["f"] = {n: go(b, b, s["to_u"](n)) for n in (1, -1)}
            both(s, 0)
            s["f2"], s["s2"] = {}, {}
        yield
        for n in (1, -1):
            for s in st:
                s["f"][n].wait_recv()
                b = blk(g, s["k"], step(s["u0"], -n), s["v0"])
                part = b.at[pl.ds(0, 32)] if n == 1 else b.at[pl.ds(32, 32)]
                s["f2"][n] = go(part, part, s["to_u"](n))
                both(s, -n)
            yield

        def relay(s, off, n):
            s["s", off][n].wait_recv()
            s["s2"][off] = one(s, off, n, step(s["v0"], -n))

        for s in st:
            relay(s, 0, 1)
        yield
        for s in st:
            s["f2"][1].wait_recv()
            s["f2"][-1].wait_recv()
            both(s, 2)
        for s in st:
            s["s", 0][-1].wait_recv()
        yield
        for off in (-1, 1, 2):
            n = 1 if off == 1 else -1
            for s in st:
                relay(s, off, n)
            for s in st:
                s["s", off][-n].wait_recv()
            yield
        for off in (0, -1, 1, 2):
            for s in st:
                s["s2"][off].wait_recv()
            yield

    def drain(g, n):
        for _ in range(n):
            next(g, None)

    gen_x = gather(s0x, gx, c0x)
    c0g = []
    gen_g = gather(s0g, gg, c0g)

    def partial(g, w, nt, xx):
        a = g[0, xx].reshape(256, 1024)
        b = g[1, xx].reshape(256, 1024)
        if nt:
            return dot_nt(a, w[:, :1024]) + dot_nt(b, w[:, 1024:])
        return dot_nn(a, w[:1024]) + dot_nn(b, w[1024:])

    def x_of(p, mine):
        c = core if mine else 1 - core
        return (xi + (4 - c if p == 0 else 1 + c)) % 4

    side = ((gx, win, False), (gg, wout, True))

    def row_other(i, p):
        ar_send[i, p] = partial(*side[i], x_of(p, False)).astype(BF)
        return go(ar_send.at[i, p], ar_recv.at[i, p], sibling)

    def row_mine(i, p):
        acc[i, p] = partial(*side[i], x_of(p, True))

    def row_add(i, p, c):
        c.wait_recv()
        v = acc[i, p] + ar_recv[i, p].astype(F32)
        acc[i, p] = v
        ay_send[i, p] = v.astype(BF)
        return go(ay_send.at[i, p], ay_recv.at[i, p], partner)

    def rows_loop(f):
        def body(m, _):
            f(m, pl.ds(pl.multiple_of(m * 64, 64), 64))
            return 0

        lax.fori_loop(0, 4, body, 0)

    def row_act(p, c):
        c.wait_recv()
        xx = x_of(p, True)

        def rows_of(m, rows):
            pre = acc[0, p, rows] + ay_recv[0, p, rows].astype(F32)
            acc[0, p, rows] = pre
            act[xx, m] = gelu_value(pre).astype(BF)

        rows_loop(rows_of)
        return go(act.at[xx], act.at[xx], sibling)

    def row_dpre(p, c):
        c.wait_recv()
        xx = x_of(p, True)

        def rows_of(m, rows):
            d = acc[1, p, rows] + ay_recv[1, p, rows].astype(F32)
            dpre[xx, m] = (d * gelu_slope(acc[0, p, rows])).astype(BF)

        rows_loop(rows_of)
        return go(dpre.at[xx], dpre.at[xx], sibling)

    def term(t, k, v):
        if t == 0:
            a = act[v] if k == 0 else act[:, v]
            r = dot_nn(a.reshape(256, 512), wout[:, k * 1024 : (k + 1) * 1024])
        else:
            a = dpre[v] if k == 0 else dpre[:, v]
            r = dot_nt(a.reshape(256, 512), win[k * 1024 : (k + 1) * 1024, :])
        return r.reshape(4, 64, 1024)

    last = {}

    def scatter(t):
        st = colours()
        with_half = {1: (2, -1), -1: (1, 0)}
        for s in st:
            k = s["k"]
            rs_far[t, k] = term(t, k, step(s["v0"], 2)).astype(BF)
            s["h"], s["w"], s["uw"] = {}, {}, {}
            for i in range(2):
                for n in (1, -1):
                    off = with_half[n][i]
                    u = step(s["u0"], off)
                    s["h"][off] = go(rs_far.at[t, k, u], rs_half.at[t, k, u], s["to_v"](n))
        yield

        def piece(s, n, off):
            k, u, j = s["k"], step(s["u0"], off), 0 if n == 1 else 1
            p = rs_p[k, j, u]
            if off in with_half[n]:
                s["h"][off].wait_recv()
                p = p + rs_half[t, k, u].astype(F32)
            rs_full[t, k, j, u] = p.astype(BF)
            s["w"][n, off] = go(rs_full.at[t, k, j, u], rs_in.at[t, k, j, u], s["to_v"](n))

        for n, off in ((-1, 2), (1, 1)):
            for s in st:
                rs_p[s["k"], 0 if n == 1 else 1] = term(t, s["k"], step(s["v0"], n))
                piece(s, n, off)
        yield
        for n, off in ((-1, -1), (1, 2)):
            for s in st:
                piece(s, n, off)
        yield
        for n, off in ((-1, 1), (1, -1)):
            for s in st:
                piece(s, n, off)
        for s in st:
            rs_p[s["k"], 2] = term(t, s["k"], s["v0"])
        yield

        def summed(s, off):
            k, u = s["k"], step(s["u0"], off)
            s["w"][1, off].wait_recv()
            s["w"][-1, off].wait_recv()
            return rs_p[k, 2, u] + rs_in[t, k, 0, u].astype(F32) + rs_in[t, k, 1, u].astype(F32)

        for s in st:
            k = s["k"]
            ru_far[t, k] = summed(s, 2).astype(BF)
            s["uh"] = {
                n: go(
                    ru_far.at[t, k, pl.ds(0 if n == 1 else 32, 32)],
                    ru_half.at[t, k, 0 if n == 1 else 1],
                    s["to_u"](n),
                )
                for n in (1, -1)
            }
        for s in st:
            for n in (1, -1):
                piece(s, n, 0)
        yield
        for n in (-1, 1):
            for s in st:
                k, j = s["k"], 0 if n == 1 else 1
                p = summed(s, n)
                s["uh"][n].wait_recv()
                extra = ru_half[t, k, j].astype(F32)
                lo, hi = p[0:32], p[32:64]
                if n == 1:
                    lo = lo + extra
                else:
                    hi = hi + extra
                ru_full[t, k, j, 0:32] = lo.astype(BF)
                ru_full[t, k, j, 32:64] = hi.astype(BF)
                s["uw"][n] = go(ru_full.at[t, k, j], ru_in.at[t, k, j], s["to_u"](n))
        yield
        for s in st:
            k = s["k"]
            r = summed(s, 0)
            s["uw"][1].wait_recv()
            s["uw"][-1].wait_recv()
            r = r + ru_in[t, k, 0].astype(F32) + ru_in[t, k, 1].astype(F32)
            rfin[t, k] = r.astype(BF).reshape(8, 8, 1024)
            last[t] = last.get(t, []) + [
                go(rfin.at[t, k, qq], e_buf.at[t, k, q], dev(xi, zi, qq)) for qq in far_first
            ]
        for k in range(2):
            e_buf[t, k, q] = rfin[t, k, q]
        yield

    ones = jnp.ones((8, 512), BF)

    def grad_in_tiles(k, lo, hi):
        def win_tile(j, _):
            lanes = pl.ds(pl.multiple_of(j * 256, 256), 256)
            ft = k * 4 + j
            a = gx[k, :, :, :, lanes].reshape(1024, 256)
            raw = dot_tn(a, dpre[...].reshape(1024, 512))
            rows = pl.ds(pl.multiple_of(ft * 256, 256), 256)
            gw1[rows] = (raw * min_ref[pl.ds(ft, 1)]).astype(BF)
            p = raw * win[rows].astype(F32)
            hi = p.astype(BF)
            lo = (p - hi.astype(F32)).astype(BF)
            s = dot_nt(ones, hi) + dot_nt(ones, lo)
            s_x[xi, pl.ds(2 * ft, 1)] = s[0:1, :128]
            s_x[xi, pl.ds(2 * ft + 1, 1)] = s[0:1, 128:]
            return 0

        lax.fori_loop(lo, hi, win_tile, 0)

    def grad_out_tiles(k, lo, hi):
        def wout_tile(j, _):
            lanes = pl.ds(pl.multiple_of(j * 256, 256), 256)
            b = gg[k, :, :, :, lanes].reshape(1024, 256)
            raw = dot_tn(act[...].reshape(1024, 512), b)
            cols = pl.ds(pl.multiple_of(k * 1024 + j * 256, 256), 256)
            for h in range(2):
                gw2[h * 256 : (h + 1) * 256, cols] = (
                    raw[h * 256 : (h + 1) * 256] * mout_ref[h : h + 1, cols]
                ).astype(BF)
            return 0

        lax.fori_loop(lo, hi, wout_tile, 0)

    drain(gen_x, 1)
    c0g += column_in(
        lambda i: og_ref.at[:, pl.ds(pl.multiple_of(i * 1024, 1024), 1024)], s0g
    )
    w_in_copy.wait()
    for t in range(8):
        win[t * 256 : (t + 1) * 256] = win[t * 256 : (t + 1) * 256] * min_ref[t : t + 1].astype(BF)
    w_out_copy.wait()
    for t in range(2):
        wout[t * 256 : (t + 1) * 256] = wout[t * 256 : (t + 1) * 256] * mout_ref[t : t + 1].astype(BF)
    drain(gen_x, 7)
    drain(gen_g, 1)
    drain(gen_x, 2)
    ca0 = row_other(0, 0)
    row_mine(0, 0)
    drain(gen_g, 2)
    cb0 = row_add(0, 0, ca0)
    drain(gen_x, 2)
    ca1 = row_other(0, 1)
    drain(gen_g, 1)
    row_mine(0, 1)
    cb1 = row_add(0, 1, ca1)
    drain(gen_g, 2)
    cc0 = row_act(0, cb0)
    drain(gen_g, 1)
    cc1 = row_act(1, cb1)
    drain(gen_g, 1)
    cc0.wait_recv()
    cc1.wait_recv()
    gen_o = scatter(0)
    drain(gen_o, 1)
    drain(gen_g, 2)
    da0 = row_other(1, 0)
    drain(gen_o, 1)
    row_mine(1, 0)
    db0 = row_add(1, 0, da0)
    drain(gen_g, 2)
    da1 = row_other(1, 1)
    row_mine(1, 1)
    db1 = row_add(1, 1, da1)
    drain(gen_o, 2)
    grad_out_tiles(0, 0, 2)
    dc0 = row_dpre(0, db0)
    drain(gen_o, 1)
    grad_out_tiles(0, 2, 4)
    drain(gen_o, 1)
    dc1 = row_dpre(1, db1)
    dc0.wait_recv()
    dc1.wait_recv()
    gen_d = scatter(1)
    drain(gen_d, 1)
    drain(gen_o, 1)
    drain(gen_d, 1)
    grad_out_tiles(1, 0, 2)
    drain(gen_d, 1)
    grad_out_tiles(1, 2, 4)
    drain(gen_d, 1)
    grad_in_tiles(0, 0, 4)
    drain(gen_d, 1)
    grad_in_tiles(1, 0, 4)
    sx = [go(s_x.at[xi], s_x.at[xi], dev(step(xi, n), zi, q)) for n in (1, 2, 3)]
    for c in last[0]:
        c.wait_recv()
    for r, k in SLICES:
        f = slice(r * 2048 + k * 1024, r * 2048 + (k + 1) * 1024)
        o = e_buf[0, k, 2 * r].astype(F32) + e_buf[0, k, 2 * r + 1].astype(F32)
        out_ref[:, f] = (x_ref[:, f].astype(F32) + o).astype(BF)
    drain(gen_d, 1)
    for c in sx:
        c.wait_recv()
    s_z[zi] = (s_x[0] + s_x[1]) + (s_x[2] + s_x[3])
    sz = [go(s_z.at[zi], s_z.at[zi], dev(xi, step(zi, n), q)) for n in (1, 2, 3)]
    drain(gen_d, 1)
    for c in sz:
        c.wait_recv()
    s_c[q] = (s_z[0] + s_z[1]) + (s_z[2] + s_z[3])
    sc = [go(s_c.at[q], s_c.at[q], dev(xi, zi, (q + n) % 8)) for n in range(1, 8)]
    for c in sc:
        c.wait_recv()
    for r in range(4):
        gg_ref[r * 16 : (r + 1) * 16] = (s_c[2 * r] + s_c[2 * r + 1]) / gain64_ref[r * 16 : (r + 1) * 16]
    xf = x_ref[...].astype(F32)
    cen = xf - jnp.mean(xf, axis=1, keepdims=True)
    inv = lax.rsqrt(jnp.mean(cen * cen, axis=1, keepdims=True) + 1e-05)
    hat = cen * inv
    for c in last[1]:
        c.wait_recv()
    parts = [
        e_buf[1, k, 2 * r].astype(F32) + e_buf[1, k, 2 * r + 1].astype(F32) for r, k in SLICES
    ]
    d = jnp.concatenate(parts, axis=1)
    g = d * gain_ref[...]
    back = inv * (
        g - jnp.mean(g, axis=1, keepdims=True) - hat * jnp.mean(g * hat, axis=1, keepdims=True)
    )
    gin_ref[...] = (og_ref[...].astype(F32) + back).astype(BF)
    finish()


def hand_over(n, *refs):
    ins, outs, sem = refs[:n], refs[n : 2 * n], refs[2 * n]
    moves = [pltpu.make_async_copy(a, o, sem.at[i]) for i, (a, o) in enumerate(zip(ins, outs))]
    for m in moves:
        m.start()
    for m in moves:
        m.wait()


def shards(inputs, layer_norm_gain, w_in, w_out, pattern_in, pattern_out, out_grad):
    vm = functools.partial(pl.BlockSpec, memory_space=pltpu.VMEM)
    hbm = functools.partial(pl.BlockSpec, memory_space=pl.ANY)
    V = pltpu.VMEM
    out = pl.pallas_call(
        kernel,
        out_shape=(
            jax.ShapeDtypeStruct((8, 8192), BF),
            jax.ShapeDtypeStruct((8, 8192), BF),
            jax.ShapeDtypeStruct((2048, 512), BF),
            jax.ShapeDtypeStruct((512, 2048), BF),
            jax.ShapeDtypeStruct((64, 128), F32),
        ),
        in_specs=[pl.BlockSpec(memory_space=pltpu.HBM)] * 8,
        out_specs=(vm(),) * 5,
        scratch_shapes=[
            V((8, 8192), BF),
            V((1, 8192), F32),
            V((64, 128), F32),
            V((8, 8192), BF),
            V((16, 64), jnp.int32),
            V((32, 32), jnp.int32),
            V((2048, 512), BF),
            V((512, 2048), BF),
            V((8, 512), F32),
            V((2, 2048), F32),
            V((8, 8, 1024), BF),
            V((2, 8, 8, 1024), BF),
            V((2, 8, 8, 1024), BF),
            V((2, 4, 4, 64, 1024), BF),
            V((2, 4, 4, 64, 1024), BF),
            V((2, 2, 256, 512), BF),
            V((2, 2, 256, 512), BF),
            V((2, 2, 256, 512), BF),
            V((2, 2, 256, 512), BF),
            V((2, 2, 256, 512), F32),
            V((4, 4, 64, 512), BF),
            V((4, 4, 64, 512), BF),
            V((2, 2, 4, 64, 1024), BF),
            V((2, 2, 4, 64, 1024), BF),
            V((2, 2, 2, 4, 64, 1024), BF),
            V((2, 2, 2, 4, 64, 1024), BF),
            V((2, 3, 4, 64, 1024), F32),
            V((2, 2, 64, 1024), BF),
            V((2, 2, 2, 32, 1024), BF),
            V((2, 2, 2, 64, 1024), BF),
            V((2, 2, 2, 64, 1024), BF),
            V((2, 2, 8, 8, 1024), BF),
            V((2, 2, 8, 8, 1024), BF),
            V((4, 16, 128), F32),
            V((4, 16, 128), F32),
            V((8, 16, 128), F32),
            pltpu.SemaphoreType.DMA((N_COPIES,)),
            pltpu.SemaphoreType.DMA((N_COPIES,)),
            pltpu.SemaphoreType.DMA((8,)),
        ],
        compiler_params=pltpu.CompilerParams(
            collective_id=0, has_side_effects=True, vmem_limit_bytes=48 << 20
        ),
        name="ffn",
    )(
        *(
            pltpu.with_memory_space_constraint(a, pltpu.HBM)
            for a in (
                inputs, layer_norm_gain.reshape(1, 8192), layer_norm_gain.reshape(64, 128),
                out_grad, w_in, w_out, pattern_in.T, pattern_out,
            )
        )
    )
    output, grad_inputs, g_in, g_out, g_gain = pl.pallas_call(
        functools.partial(hand_over, len(out)),
        out_shape=tuple(jax.ShapeDtypeStruct(o.shape, o.dtype) for o in out),
        in_specs=[vm()] * len(out),
        out_specs=(hbm(),) * len(out),
        scratch_shapes=[pltpu.SemaphoreType.DMA((len(out),))],
        compiler_params=pltpu.CompilerParams(vmem_limit_bytes=8 << 20),
        name="hand_over",
    )(*out)
    return output, grad_inputs, g_in, g_out, g_gain.reshape(8192)


def solution(mesh):
    in_specs = (
        P(("row", "col"), None),
        P(),
        P("row", "col"),
        P("col", "row"),
        P(),
        P(),
        P(("row", "col"), None),
    )
    out_specs = (
        P(("row", "col"), None),
        P(("row", "col"), None),
        P("row", "col"),
        P("col", "row"),
        P(),
    )
    return jax.shard_map(shards, mesh=mesh, in_specs=in_specs, out_specs=out_specs, check_vma=False)
```

```python
import functools

import jax
import jax.numpy as jnp
from jax import lax
from jax.experimental import pallas as pl
from jax.experimental.pallas import tpu as pltpu
from jax.sharding import PartitionSpec as P

BF = jnp.bfloat16
F32 = jnp.float32
N_COPIES = 256
SLICES = tuple((r, k) for r in range(4) for k in range(2))
FAR_FIRST = ((1, 0, 0), (1, 1, 0), (0, 0, 1), (0, 1, 1), (1, 0, 1), (1, 1, 1), (0, 1, 0))


def gelu_value(h):
    inner = 0.7978845608 * (h + 0.044715 * h * h * h)
    return 0.5 * h * (1.0 + jnp.tanh(inner))


def gelu_slope(h):
    tanh_v = jnp.tanh(0.7978845608 * (h + 0.044715 * h * h * h))
    return 0.5 * (1.0 + tanh_v) + 0.5 * h * (1.0 - tanh_v * tanh_v) * 0.7978845608 * (
        1.0 + 0.134145 * h * h
    )


def dot_nn(a, b):
    return lax.dot_general(a, b, (((1,), (0,)), ((), ())), preferred_element_type=F32)


def dot_nt(a, b):
    return lax.dot_general(a, b, (((1,), (1,)), ((), ())), preferred_element_type=F32)


def dot_tn(a, b):
    return lax.dot_general(a, b, (((0,), (0,)), ((), ())), preferred_element_type=F32)


class Sent:
    def __init__(self, c):
        self.c, self.got = c, False
        c.start()

    def wait_recv(self):
        self.got = True
        self.c.wait_recv()


def kernel(
    x_hbm, gain_hbm, gain64_hbm, og_hbm, win_hbm, wout_hbm, pin_hbm, pout_hbm,
    out_ref, gin_ref, gw1, gw2, gg_ref,
    x_ref, gain_ref, gain64_ref, og_ref, pin_ref, pout_ref,
    win, wout, min_ref, mout_ref, normed, s0x, s0g, gx, gg,
    ar_send, ar_recv, ay_send, ay_recv, acc, act, dpre,
    rs_far, rs_half, rs_full, rs_in, rs_p,
    ru_far, ru_half, ru_full, ru_in,
    rfin, e_buf, s_x, s_z, s_c,
    send_sem, recv_sem, w_sem,
):
    row = lax.axis_index("row")
    col = lax.axis_index("col")
    xi, zi, yl = col // 8, (col // 2) % 4, col % 2
    yh, core = row // 2, row % 2
    q = row * 2 + yl

    def dev(x, z, qq):
        return (qq // 2, (x * 4 + z) * 2 + qq % 2)

    sent = []

    def go(src, dst, to):
        i = len(sent)
        c = Sent(
            pltpu.make_async_remote_copy(
                src_ref=src, dst_ref=dst, send_sem=send_sem.at[i], recv_sem=recv_sem.at[i],
                device_id=to, device_id_type=pl.DeviceIdType.MESH,
            )
        )
        sent.append(c)
        return c

    def finish():
        for c in sent:
            if not c.got:
                c.wait_recv()
        for c in sent:
            c.c.wait_send()

    def step(i, n):
        return (i + n + 4) % 4

    def flip(h, c, y):
        return (yh + h) % 2 * 4 + (core + c) % 2 * 2 + (yl + y) % 2

    sibling = (yh * 2 + (1 - core), col)
    partner = ((1 - yh) * 2 + core, col)

    far_first = [flip(h, c, y) for h, c, y in FAR_FIRST]

    loads = [
        pltpu.make_async_copy(a, b, w_sem.at[i])
        for i, (a, b) in enumerate(
            (
                (x_hbm, x_ref),
                (gain_hbm, gain_ref),
                (og_hbm, og_ref),
                (pin_hbm, pin_ref),
                (pout_hbm, pout_ref),
                (gain64_hbm, gain64_ref),
                (win_hbm, win),
                (wout_hbm, wout),
            )
        )
    ]
    for c in loads:
        c.start()
    w_in_copy, w_out_copy = loads[6:]

    barrier = pltpu.get_barrier_semaphore()
    peers = [dev(xi, zi, (q + n) % 8) for n in range(1, 8)]
    peers += [dev(step(xi, n), zi, q) for n in (1, 2, 3)]
    peers += [dev(xi, step(zi, n), q) for n in (1, 2, 3)]
    for p in peers:
        pl.semaphore_signal(barrier, inc=1, device_id=p, device_id_type=pl.DeviceIdType.MESH)


    for c in loads[:2]:
        c.wait()
    xf = x_ref[...].astype(F32)
    cen = xf - jnp.mean(xf, axis=1, keepdims=True)
    inv = lax.rsqrt(jnp.mean(cen * cen, axis=1, keepdims=True) + 1e-05)
    nrm = (cen * inv * gain_ref[...]).astype(BF)
    for r in range(8):
        normed[r] = nrm[:, r * 1024 : (r + 1) * 1024]
    for c in loads[2:6]:
        c.wait()
    pl.semaphore_wait(barrier, len(peers))

    def column_in(src_of, dst):
        return [
            [go(src_of(qq // 2 * 2 + k), dst.at[k, q], dev(xi, zi, qq)) for qq in far_first]
            for k in range(2)
        ]

    c0x = column_in(lambda i: normed.at[i], s0x)
    for k in range(2):
        s0x[k, q] = normed[row * 2 + k]
        s0g[k, q] = og_ref[:, pl.ds(pl.multiple_of((row * 2 + k) * 1024, 1024), 1024)]

    lane = lax.broadcasted_iota(jnp.int32, (16, 64), 1)
    tile = lax.broadcasted_iota(jnp.int32, (16, 128), 1) + row * 8
    for h in range(2):
        rows = jnp.max(jnp.where(lane == col * 2 + h, pin_ref[...], -1), axis=1, keepdims=True)
        kept = jnp.max(jnp.where(rows == tile, 1.0, 0.0), axis=0, keepdims=True)
        for t in range(8):
            min_ref[t : t + 1, h * 256 : (h + 1) * 256] = jnp.broadcast_to(
                kept[:, t : t + 1], (1, 256)
            )
    pout = pout_ref[pl.ds(pl.multiple_of(row * 8, 8), 8), :]
    for h in range(2):
        kept = jnp.max(jnp.where(pout == col * 2 + h, 1.0, 0.0), axis=1, keepdims=True)
        for t in range(8):
            mout_ref[h : h + 1, t * 256 : (t + 1) * 256] = jnp.broadcast_to(
                kept[t : t + 1], (1, 256)
            )

    def blk(g, k, u, v):
        return g.at[0, v, u] if k == 0 else g.at[1, u, v]

    def colours():
        st = []
        for k in range(2):
            u0, v0 = (zi, xi) if k == 0 else (xi, zi)

            def to_z(n):
                return dev(xi, step(zi, n), q)

            def to_x(n):
                return dev(step(xi, n), zi, q)

            st.append(
                dict(
                    k=k, u0=u0, v0=v0, to_u=to_z if k == 0 else to_x, to_v=to_x if k == 0 else to_z
                )
            )
        return st

    def gather(s0, g, arrived, lean):
        st = colours()

        def view(s, u_off, v_off, rows=pl.ds(0, 64), lanes=None):
            b = blk(g, s["k"], step(s["u0"], u_off), step(s["v0"], v_off))
            if not lean:
                return b.at[rows]
            return b.at[rows, pl.ds(pl.multiple_of(yl * 128, 128), 896) if lanes is None else lanes]

        def push(s, u_off, v_off):
            if lean:
                b = view(s, u_off, v_off, lanes=pl.ds(pl.multiple_of(yl * 896, 128), 128))
                s["p"][u_off, v_off] = go(b, b, dev(xi, zi, flip(0, 0, 1)))

        def pushed(offs):
            if lean:
                for s in st:
                    for key, c in s["p"].items():
                        if key[1 - s["k"]] in offs:
                            c.wait_recv()

        def one(s, off, n, v_off=0):
            b = view(s, off, v_off)
            return go(b, b, s["to_v"](n))

        def both(s, off):
            s["s", off] = {n: one(s, off, n) for n in (1, -1)}

        for s in st:
            for c in arrived[s["k"]]:
                c.wait_recv()
            g[s["k"], xi, zi] = s0[s["k"]].reshape(64, 1024)
            b = view(s, 0, 0)
            s["p"] = {}
            s["f"] = {n: go(b, b, s["to_u"](n)) for n in (1, -1)}
            both(s, 0)
            s["f2"], s["s2"] = {}, {}
        yield
        for n in (1, -1):
            for s in st:
                s["f"][n].wait_recv()
                part = view(s, -n, 0, pl.ds(0 if n == 1 else 32, 32))
                s["f2"][n] = go(part, part, s["to_u"](n))
                both(s, -n)
                push(s, -n, 0)
            yield

        def relay(s, off, n):
            s["s", off][n].wait_recv()
            s["s2"][off] = one(s, off, n, -n)
            push(s, off, -n)

        for s in st:
            relay(s, 0, 1)
        yield
        for s in st:
            s["f2"][1].wait_recv()
            s["f2"][-1].wait_recv()
            both(s, 2)
            push(s, 2, 0)
        for s in st:
            s["s", 0][-1].wait_recv()
            push(s, 0, 1)
        yield
        for off in (-1, 1, 2):
            n = 1 if off == 1 else -1
            for s in st:
                relay(s, off, n)
            for s in st:
                s["s", off][-n].wait_recv()
                push(s, off, n)
            yield
        for off in (0, -1, 1, 2):
            for s in st:
                s["s2"][off].wait_recv()
                push(s, off, 2)
            if off == -1:
                pushed((0, -1))
            if off == 2:
                pushed((1, 2))
            yield

    def drain(g, n):
        for _ in range(n):
            next(g, None)

    gen_x = gather(s0x, gx, c0x, True)
    c0g = []
    gen_g = gather(s0g, gg, c0g, False)

    def partial(g, w, nt, xx):
        a = g[0, xx].reshape(256, 1024)
        b = g[1, xx].reshape(256, 1024)
        if nt:
            return dot_nt(a, w[:, :1024]) + dot_nt(b, w[:, 1024:])
        return dot_nn(a, w[:1024]) + dot_nn(b, w[1024:])

    def x_of(p, mine):
        c = core if mine else 1 - core
        return (xi + (4 - c if p == 0 else 1 + c)) % 4

    side = ((gx, win, False), (gg, wout, True))

    def row_other(i, p):
        ar_send[i, p] = partial(*side[i], x_of(p, False)).astype(BF)
        return go(ar_send.at[i, p], ar_recv.at[i, p], sibling)

    def row_mine(i, p):
        acc[i, p] = partial(*side[i], x_of(p, True))

    def row_add(i, p, c):
        c.wait_recv()
        v = acc[i, p] + ar_recv[i, p].astype(F32)
        acc[i, p] = v
        ay_send[i, p] = v.astype(BF)
        return go(ay_send.at[i, p], ay_recv.at[i, p], partner)

    def rows_loop(f):
        def body(m, _):
            f(m, pl.ds(pl.multiple_of(m * 64, 64), 64))
            return 0

        lax.fori_loop(0, 4, body, 0)

    def row_act(p, c):
        c.wait_recv()
        xx = x_of(p, True)

        def rows_of(m, rows):
            pre = acc[0, p, rows] + ay_recv[0, p, rows].astype(F32)
            acc[0, p, rows] = pre
            act[xx, m] = gelu_value(pre).astype(BF)

        rows_loop(rows_of)
        return go(act.at[xx], act.at[xx], sibling)

    def row_dpre(p, c):
        c.wait_recv()
        xx = x_of(p, True)

        def rows_of(m, rows):
            d = acc[1, p, rows] + ay_recv[1, p, rows].astype(F32)
            dpre[xx, m] = (d * gelu_slope(acc[0, p, rows])).astype(BF)

        rows_loop(rows_of)
        return go(dpre.at[xx], dpre.at[xx], sibling)

    def term(t, k, v):
        if t == 0:
            a = act[v] if k == 0 else act[:, v]
            r = dot_nn(a.reshape(256, 512), wout[:, k * 1024 : (k + 1) * 1024])
        else:
            a = dpre[v] if k == 0 else dpre[:, v]
            r = dot_nt(a.reshape(256, 512), win[k * 1024 : (k + 1) * 1024, :])
        return r.reshape(4, 64, 1024)

    last = {}

    def scatter(t):
        st = colours()
        with_half = {1: (2, -1), -1: (1, 0)}
        for s in st:
            k = s["k"]
            rs_far[t, k] = term(t, k, step(s["v0"], 2)).astype(BF)
            s["h"], s["w"], s["uw"] = {}, {}, {}
            for i in range(2):
                for n in (1, -1):
                    off = with_half[n][i]
                    u = step(s["u0"], off)
                    s["h"][off] = go(rs_far.at[t, k, u], rs_half.at[t, k, u], s["to_v"](n))
        yield

        def piece(s, n, off):
            k, u, j = s["k"], step(s["u0"], off), 0 if n == 1 else 1
            p = rs_p[k, j, u]
            if off in with_half[n]:
                s["h"][off].wait_recv()
                p = p + rs_half[t, k, u].astype(F32)
            rs_full[t, k, j, u] = p.astype(BF)
            s["w"][n, off] = go(rs_full.at[t, k, j, u], rs_in.at[t, k, j, u], s["to_v"](n))

        for n, off in ((-1, 2), (1, 1)):
            for s in st:
                rs_p[s["k"], 0 if n == 1 else 1] = term(t, s["k"], step(s["v0"], n))
                piece(s, n, off)
        yield
        for n, off in ((-1, -1), (1, 2)):
            for s in st:
                piece(s, n, off)
        yield
        for n, off in ((-1, 1), (1, -1)):
            for s in st:
                piece(s, n, off)
        for s in st:
            rs_p[s["k"], 2] = term(t, s["k"], s["v0"])
        yield

        def summed(s, off):
            k, u = s["k"], step(s["u0"], off)
            s["w"][1, off].wait_recv()
            s["w"][-1, off].wait_recv()
            return rs_p[k, 2, u] + rs_in[t, k, 0, u].astype(F32) + rs_in[t, k, 1, u].astype(F32)

        for s in st:
            k = s["k"]
            ru_far[t, k] = summed(s, 2).astype(BF)
            s["uh"] = {
                n: go(
                    ru_far.at[t, k, pl.ds(0 if n == 1 else 32, 32)],
                    ru_half.at[t, k, 0 if n == 1 else 1],
                    s["to_u"](n),
                )
                for n in (1, -1)
            }
        for s in st:
            for n in (1, -1):
                piece(s, n, 0)
        yield
        for n in (-1, 1):
            for s in st:
                k, j = s["k"], 0 if n == 1 else 1
                p = summed(s, n)
                s["uh"][n].wait_recv()
                extra = ru_half[t, k, j].astype(F32)
                lo, hi = p[0:32], p[32:64]
                if n == 1:
                    lo = lo + extra
                else:
                    hi = hi + extra
                ru_full[t, k, j, 0:32] = lo.astype(BF)
                ru_full[t, k, j, 32:64] = hi.astype(BF)
                s["uw"][n] = go(ru_full.at[t, k, j], ru_in.at[t, k, j], s["to_u"](n))
        yield
        for s in st:
            k = s["k"]
            r = summed(s, 0)
            s["uw"][1].wait_recv()
            s["uw"][-1].wait_recv()
            r = r + ru_in[t, k, 0].astype(F32) + ru_in[t, k, 1].astype(F32)
            rfin[t, k] = r.astype(BF).reshape(8, 8, 1024)
            last[t] = last.get(t, []) + [
                go(rfin.at[t, k, qq], e_buf.at[t, k, q], dev(xi, zi, qq)) for qq in far_first
            ]
        for k in range(2):
            e_buf[t, k, q] = rfin[t, k, q]
        yield

    ones = jnp.ones((8, 512), BF)

    def grad_in_tiles(k, lo, hi):
        def win_tile(j, _):
            lanes = pl.ds(pl.multiple_of(j * 256, 256), 256)
            ft = k * 4 + j
            a = gx[k, :, :, :, lanes].reshape(1024, 256)
            raw = dot_tn(a, dpre[...].reshape(1024, 512))
            rows = pl.ds(pl.multiple_of(ft * 256, 256), 256)
            gw1[rows] = (raw * min_ref[pl.ds(ft, 1)]).astype(BF)
            p = raw * win[rows].astype(F32)
            hi = p.astype(BF)
            lo = (p - hi.astype(F32)).astype(BF)
            s = dot_nt(ones, hi) + dot_nt(ones, lo)
            s_x[xi, pl.ds(2 * ft, 1)] = s[0:1, :128]
            s_x[xi, pl.ds(2 * ft + 1, 1)] = s[0:1, 128:]
            return 0

        lax.fori_loop(lo, hi, win_tile, 0)

    def grad_out_tiles(k, lo, hi):
        def wout_tile(j, _):
            lanes = pl.ds(pl.multiple_of(j * 256, 256), 256)
            b = gg[k, :, :, :, lanes].reshape(1024, 256)
            raw = dot_tn(act[...].reshape(1024, 512), b)
            cols = pl.ds(pl.multiple_of(k * 1024 + j * 256, 256), 256)
            for h in range(2):
                gw2[h * 256 : (h + 1) * 256, cols] = (
                    raw[h * 256 : (h + 1) * 256] * mout_ref[h : h + 1, cols]
                ).astype(BF)
            return 0

        lax.fori_loop(lo, hi, wout_tile, 0)

    drain(gen_x, 1)
    c0g += column_in(
        lambda i: og_ref.at[:, pl.ds(pl.multiple_of(i * 1024, 1024), 1024)], s0g
    )
    w_in_copy.wait()
    for t in range(8):
        win[t * 256 : (t + 1) * 256] = win[t * 256 : (t + 1) * 256] * min_ref[t : t + 1].astype(BF)
    w_out_copy.wait()
    for t in range(2):
        wout[t * 256 : (t + 1) * 256] = wout[t * 256 : (t + 1) * 256] * mout_ref[t : t + 1].astype(BF)
    drain(gen_x, 7)
    drain(gen_g, 1)
    drain(gen_x, 2)
    ca0 = row_other(0, 0)
    row_mine(0, 0)
    drain(gen_g, 2)
    cb0 = row_add(0, 0, ca0)
    drain(gen_x, 2)
    ca1 = row_other(0, 1)
    drain(gen_g, 1)
    row_mine(0, 1)
    cb1 = row_add(0, 1, ca1)
    drain(gen_g, 2)
    cc0 = row_act(0, cb0)
    drain(gen_g, 1)
    cc1 = row_act(1, cb1)
    drain(gen_g, 1)
    cc0.wait_recv()
    cc1.wait_recv()
    gen_o = scatter(0)
    drain(gen_o, 1)
    drain(gen_g, 2)
    da0 = row_other(1, 0)
    row_mine(1, 0)
    db0 = row_add(1, 0, da0)
    drain(gen_o, 1)
    drain(gen_g, 2)
    da1 = row_other(1, 1)
    row_mine(1, 1)
    db1 = row_add(1, 1, da1)
    drain(gen_o, 2)
    grad_out_tiles(0, 0, 2)
    dc0 = row_dpre(0, db0)
    drain(gen_o, 1)
    grad_out_tiles(0, 2, 4)
    grad_out_tiles(1, 0, 2)
    drain(gen_o, 1)
    dc1 = row_dpre(1, db1)
    grad_out_tiles(1, 2, 4)
    dc0.wait_recv()
    dc1.wait_recv()
    gen_d = scatter(1)
    drain(gen_d, 1)
    grad_in_tiles(0, 0, 2)
    drain(gen_o, 1)
    drain(gen_d, 1)
    grad_in_tiles(0, 2, 3)
    drain(gen_d, 1)
    grad_in_tiles(0, 3, 4)
    drain(gen_d, 1)
    grad_in_tiles(1, 0, 4)
    sx = [go(s_x.at[xi], s_x.at[xi], dev(step(xi, n), zi, q)) for n in (1, 2, 3)]
    drain(gen_d, 1)
    for c in last[0]:
        c.wait_recv()
    for r, k in SLICES:
        f = slice(r * 2048 + k * 1024, r * 2048 + (k + 1) * 1024)
        o = e_buf[0, k, 2 * r].astype(F32) + e_buf[0, k, 2 * r + 1].astype(F32)
        out_ref[:, f] = (x_ref[:, f].astype(F32) + o).astype(BF)
    drain(gen_d, 1)
    for c in sx:
        c.wait_recv()
    s_z[zi] = (s_x[0] + s_x[1]) + (s_x[2] + s_x[3])
    sz = [go(s_z.at[zi], s_z.at[zi], dev(xi, step(zi, n), q)) for n in (1, 2, 3)]
    drain(gen_d, 1)
    for c in sz:
        c.wait_recv()
    s_c[q] = (s_z[0] + s_z[1]) + (s_z[2] + s_z[3])
    sc = [go(s_c.at[q], s_c.at[q], dev(xi, zi, (q + n) % 8)) for n in range(1, 8)]
    for c in sc:
        c.wait_recv()
    for r in range(4):
        gg_ref[r * 16 : (r + 1) * 16] = (s_c[2 * r] + s_c[2 * r + 1]) / gain64_ref[r * 16 : (r + 1) * 16]
    xf = x_ref[...].astype(F32)
    cen = xf - jnp.mean(xf, axis=1, keepdims=True)
    inv = lax.rsqrt(jnp.mean(cen * cen, axis=1, keepdims=True) + 1e-05)
    hat = cen * inv
    for c in last[1]:
        c.wait_recv()
    parts = [
        e_buf[1, k, 2 * r].astype(F32) + e_buf[1, k, 2 * r + 1].astype(F32) for r, k in SLICES
    ]
    d = jnp.concatenate(parts, axis=1)
    g = d * gain_ref[...]
    back = inv * (
        g - jnp.mean(g, axis=1, keepdims=True) - hat * jnp.mean(g * hat, axis=1, keepdims=True)
    )
    gin_ref[...] = (og_ref[...].astype(F32) + back).astype(BF)
    finish()


def hand_over(n, *refs):
    ins, outs, sem = refs[:n], refs[n : 2 * n], refs[2 * n]
    moves = [pltpu.make_async_copy(a, o, sem.at[i]) for i, (a, o) in enumerate(zip(ins, outs))]
    for m in moves:
        m.start()
    for m in moves:
        m.wait()


def shards(inputs, layer_norm_gain, w_in, w_out, pattern_in, pattern_out, out_grad):
    vm = functools.partial(pl.BlockSpec, memory_space=pltpu.VMEM)
    hbm = functools.partial(pl.BlockSpec, memory_space=pl.ANY)
    V = pltpu.VMEM
    out = pl.pallas_call(
        kernel,
        out_shape=(
            jax.ShapeDtypeStruct((8, 8192), BF),
            jax.ShapeDtypeStruct((8, 8192), BF),
            jax.ShapeDtypeStruct((2048, 512), BF),
            jax.ShapeDtypeStruct((512, 2048), BF),
            jax.ShapeDtypeStruct((64, 128), F32),
        ),
        in_specs=[pl.BlockSpec(memory_space=pltpu.HBM)] * 8,
        out_specs=(vm(),) * 5,
        scratch_shapes=[
            V((8, 8192), BF),
            V((1, 8192), F32),
            V((64, 128), F32),
            V((8, 8192), BF),
            V((16, 64), jnp.int32),
            V((32, 32), jnp.int32),
            V((2048, 512), BF),
            V((512, 2048), BF),
            V((8, 512), F32),
            V((2, 2048), F32),
            V((8, 8, 1024), BF),
            V((2, 8, 8, 1024), BF),
            V((2, 8, 8, 1024), BF),
            V((2, 4, 4, 64, 1024), BF),
            V((2, 4, 4, 64, 1024), BF),
            V((2, 2, 256, 512), BF),
            V((2, 2, 256, 512), BF),
            V((2, 2, 256, 512), BF),
            V((2, 2, 256, 512), BF),
            V((2, 2, 256, 512), F32),
            V((4, 4, 64, 512), BF),
            V((4, 4, 64, 512), BF),
            V((2, 2, 4, 64, 1024), BF),
            V((2, 2, 4, 64, 1024), BF),
            V((2, 2, 2, 4, 64, 1024), BF),
            V((2, 2, 2, 4, 64, 1024), BF),
            V((2, 3, 4, 64, 1024), F32),
            V((2, 2, 64, 1024), BF),
            V((2, 2, 2, 32, 1024), BF),
            V((2, 2, 2, 64, 1024), BF),
            V((2, 2, 2, 64, 1024), BF),
            V((2, 2, 8, 8, 1024), BF),
            V((2, 2, 8, 8, 1024), BF),
            V((4, 16, 128), F32),
            V((4, 16, 128), F32),
            V((8, 16, 128), F32),
            pltpu.SemaphoreType.DMA((N_COPIES,)),
            pltpu.SemaphoreType.DMA((N_COPIES,)),
            pltpu.SemaphoreType.DMA((8,)),
        ],
        compiler_params=pltpu.CompilerParams(
            collective_id=0, has_side_effects=True, vmem_limit_bytes=48 << 20
        ),
        name="ffn",
    )(
        *(
            pltpu.with_memory_space_constraint(a, pltpu.HBM)
            for a in (
                inputs, layer_norm_gain.reshape(1, 8192), layer_norm_gain.reshape(64, 128),
                out_grad, w_in, w_out, pattern_in.T, pattern_out,
            )
        )
    )
    output, grad_inputs, g_in, g_out, g_gain = pl.pallas_call(
        functools.partial(hand_over, len(out)),
        out_shape=tuple(jax.ShapeDtypeStruct(o.shape, o.dtype) for o in out),
        in_specs=[vm()] * len(out),
        out_specs=(hbm(),) * len(out),
        scratch_shapes=[pltpu.SemaphoreType.DMA((len(out),))],
        compiler_params=pltpu.CompilerParams(vmem_limit_bytes=8 << 20),
        name="hand_over",
    )(*out)
    return output, grad_inputs, g_in, g_out, g_gain.reshape(8192)


def solution(mesh):
    in_specs = (
        P(("row", "col"), None),
        P(),
        P("row", "col"),
        P("col", "row"),
        P(),
        P(),
        P(("row", "col"), None),
    )
    out_specs = (
        P(("row", "col"), None),
        P(("row", "col"), None),
        P("row", "col"),
        P("col", "row"),
        P(),
    )
    return jax.shard_map(shards, mesh=mesh, in_specs=in_specs, out_specs=out_specs, check_vma=False)
```

```python
import functools

import jax
import jax.numpy as jnp
from jax import lax
from jax.experimental import pallas as pl
from jax.experimental.pallas import tpu as pltpu
from jax.sharding import PartitionSpec as P

BF = jnp.bfloat16
F32 = jnp.float32
N_COPIES = 256
SLICES = tuple((r, k) for r in range(4) for k in range(2))
FAR_FIRST = ((1, 0, 0), (1, 1, 0), (0, 0, 1), (0, 1, 1), (1, 0, 1), (1, 1, 1), (0, 1, 0))


def gelu_value(h):
    inner = 0.7978845608 * (h + 0.044715 * h * h * h)
    return 0.5 * h * (1.0 + jnp.tanh(inner))


def gelu_slope(h):
    tanh_v = jnp.tanh(0.7978845608 * (h + 0.044715 * h * h * h))
    return 0.5 * (1.0 + tanh_v) + 0.5 * h * (1.0 - tanh_v * tanh_v) * 0.7978845608 * (
        1.0 + 0.134145 * h * h
    )


def dot_nn(a, b):
    return lax.dot_general(a, b, (((1,), (0,)), ((), ())), preferred_element_type=F32)


def dot_nt(a, b):
    return lax.dot_general(a, b, (((1,), (1,)), ((), ())), preferred_element_type=F32)


def dot_tn(a, b):
    return lax.dot_general(a, b, (((0,), (0,)), ((), ())), preferred_element_type=F32)


class Sent:
    def __init__(self, c):
        self.c, self.got = c, False
        c.start()

    def wait_recv(self):
        self.got = True
        self.c.wait_recv()


def kernel(
    x_hbm, gain_hbm, gain64_hbm, og_hbm, win_hbm, wout_hbm, pin_hbm, pout_hbm,
    out_ref, gin_ref, gw1, gw2, gg_ref,
    x_ref, gain_ref, gain64_ref, og_ref, pin_ref, pout_ref,
    win, wout, min_ref, mout_ref, normed, s0x, s0g, gx, gg,
    ar_send, ar_recv, ay_send, ay_recv, acc, act, dpre,
    rs_far, rs_half, rs_full, rs_in, rs_p,
    ru_far, ru_half, ru_full, ru_in,
    rfin, e_buf, s_x, s_z, s_c,
    send_sem, recv_sem, w_sem,
):
    row = lax.axis_index("row")
    col = lax.axis_index("col")
    xi, zi, yl = col // 8, (col // 2) % 4, col % 2
    yh, core = row // 2, row % 2
    q = row * 2 + yl

    def dev(x, z, qq):
        return (qq // 2, (x * 4 + z) * 2 + qq % 2)

    sent = []

    def go(src, dst, to):
        i = len(sent)
        c = Sent(
            pltpu.make_async_remote_copy(
                src_ref=src, dst_ref=dst, send_sem=send_sem.at[i], recv_sem=recv_sem.at[i],
                device_id=to, device_id_type=pl.DeviceIdType.MESH,
            )
        )
        sent.append(c)
        return c

    def finish():
        for c in sent:
            if not c.got:
                c.wait_recv()
        for c in sent:
            c.c.wait_send()

    def step(i, n):
        return (i + n + 4) % 4

    def flip(h, c, y):
        return (yh + h) % 2 * 4 + (core + c) % 2 * 2 + (yl + y) % 2

    sibling = (yh * 2 + (1 - core), col)
    partner = ((1 - yh) * 2 + core, col)

    far_first = [flip(h, c, y) for h, c, y in FAR_FIRST]

    loads = [
        pltpu.make_async_copy(a, b, w_sem.at[i])
        for i, (a, b) in enumerate(
            (
                (x_hbm, x_ref),
                (gain_hbm, gain_ref),
                (og_hbm, og_ref),
                (pin_hbm, pin_ref),
                (pout_hbm, pout_ref),
                (gain64_hbm, gain64_ref),
                (win_hbm, win),
                (wout_hbm, wout),
            )
        )
    ]
    for c in loads:
        c.start()
    w_in_copy, w_out_copy = loads[6:]

    barrier = pltpu.get_barrier_semaphore()
    peers = [dev(xi, zi, (q + n) % 8) for n in range(1, 8)]
    peers += [dev(step(xi, n), zi, q) for n in (1, 2, 3)]
    peers += [dev(xi, step(zi, n), q) for n in (1, 2, 3)]
    for p in peers:
        pl.semaphore_signal(barrier, inc=1, device_id=p, device_id_type=pl.DeviceIdType.MESH)


    for c in loads[:2]:
        c.wait()
    xf = x_ref[...].astype(F32)
    cen = xf - jnp.mean(xf, axis=1, keepdims=True)
    inv = lax.rsqrt(jnp.mean(cen * cen, axis=1, keepdims=True) + 1e-05)
    nrm = (cen * inv * gain_ref[...]).astype(BF)
    for r in range(8):
        normed[r] = nrm[:, r * 1024 : (r + 1) * 1024]
    for c in loads[2:6]:
        c.wait()
    pl.semaphore_wait(barrier, len(peers))

    def column_in(src_of, dst):
        return [
            [go(src_of(qq // 2 * 2 + k), dst.at[k, q], dev(xi, zi, qq)) for qq in far_first]
            for k in range(2)
        ]

    c0x = column_in(lambda i: normed.at[i], s0x)
    for k in range(2):
        s0x[k, q] = normed[row * 2 + k]

    def blk(g, k, u, v):
        return g.at[0, v, u] if k == 0 else g.at[1, u, v]

    def colours():
        st = []
        for k in range(2):
            u0, v0 = (zi, xi) if k == 0 else (xi, zi)

            def to_z(n):
                return dev(xi, step(zi, n), q)

            def to_x(n):
                return dev(step(xi, n), zi, q)

            st.append(
                dict(
                    k=k, u0=u0, v0=v0, to_u=to_z if k == 0 else to_x, to_v=to_x if k == 0 else to_z
                )
            )
        return st

    def gather(s0, g, arrived):
        st = colours()

        def one(s, off, n, v=None):
            b = blk(g, s["k"], step(s["u0"], off), s["v0"] if v is None else v)
            return go(b, b, s["to_v"](n))

        def both(s, off):
            s["s", off] = {n: one(s, off, n) for n in (1, -1)}

        for s in st:
            for c in arrived[s["k"]]:
                c.wait_recv()
            g[s["k"], xi, zi] = s0[s["k"]].reshape(64, 1024)
            b = blk(g, s["k"], s["u0"], s["v0"])
            s["f"] = {n: go(b, b, s["to_u"](n)) for n in (1, -1)}
            both(s, 0)
            s["f2"], s["s2"] = {}, {}
        yield
        for n in (1, -1):
            for s in st:
                s["f"][n].wait_recv()
                b = blk(g, s["k"], step(s["u0"], -n), s["v0"])
                part = b.at[pl.ds(0, 32)] if n == 1 else b.at[pl.ds(32, 32)]
                s["f2"][n] = go(part, part, s["to_u"](n))
                both(s, -n)
            yield

        def relay(s, off, n):
            s["s", off][n].wait_recv()
            s["s2"][off] = one(s, off, n, step(s["v0"], -n))

        for s in st:
            relay(s, 0, 1)
        yield
        for s in st:
            s["f2"][1].wait_recv()
            s["f2"][-1].wait_recv()
            both(s, 2)
        for s in st:
            s["s", 0][-1].wait_recv()
        yield
        for off in (-1, 1, 2):
            n = 1 if off == 1 else -1
            for s in st:
                relay(s, off, n)
            for s in st:
                s["s", off][-n].wait_recv()
            yield
        for off in (0, -1, 1, 2):
            for s in st:
                s["s2"][off].wait_recv()
            yield

    def drain(g, n):
        for _ in range(n):
            next(g, None)

    gen_x = gather(s0x, gx, c0x)
    c0g = []
    gen_g = gather(s0g, gg, c0g)

    def partial(g, w, nt, xx):
        a = g[0, xx].reshape(256, 1024)
        b = g[1, xx].reshape(256, 1024)
        if nt:
            return dot_nt(a, w[:, :1024]) + dot_nt(b, w[:, 1024:])
        return dot_nn(a, w[:1024]) + dot_nn(b, w[1024:])

    def x_of(p, mine):
        c = core if mine else 1 - core
        return (xi + (4 - c if p == 0 else 1 + c)) % 4

    side = ((gx, win, False), (gg, wout, True))

    def row_other(i, p):
        ar_send[i, p] = partial(*side[i], x_of(p, False)).astype(BF)
        return go(ar_send.at[i, p], ar_recv.at[i, p], sibling)

    def row_mine(i, p):
        acc[i, p] = partial(*side[i], x_of(p, True))

    def row_add(i, p, c):
        c.wait_recv()
        v = acc[i, p] + ar_recv[i, p].astype(F32)
        acc[i, p] = v
        ay_send[i, p] = v.astype(BF)
        return go(ay_send.at[i, p], ay_recv.at[i, p], partner)

    def rows_loop(f):
        def body(m, _):
            f(m, pl.ds(pl.multiple_of(m * 64, 64), 64))
            return 0

        lax.fori_loop(0, 4, body, 0)

    def row_act(p, c):
        c.wait_recv()
        xx = x_of(p, True)

        def rows_of(m, rows):
            pre = acc[0, p, rows] + ay_recv[0, p, rows].astype(F32)
            acc[0, p, rows] = pre
            act[xx, m] = gelu_value(pre).astype(BF)

        rows_loop(rows_of)
        return go(act.at[xx], act.at[xx], sibling)

    def row_dpre(p, c):
        c.wait_recv()
        xx = x_of(p, True)

        def rows_of(m, rows):
            d = acc[1, p, rows] + ay_recv[1, p, rows].astype(F32)
            dpre[xx, m] = (d * gelu_slope(acc[0, p, rows])).astype(BF)

        rows_loop(rows_of)
        return go(dpre.at[xx], dpre.at[xx], sibling)

    def term(t, k, v):
        if t == 0:
            a = act[v] if k == 0 else act[:, v]
            r = dot_nn(a.reshape(256, 512), wout[:, k * 1024 : (k + 1) * 1024])
        else:
            a = dpre[v] if k == 0 else dpre[:, v]
            r = dot_nt(a.reshape(256, 512), win[k * 1024 : (k + 1) * 1024, :])
        return r.reshape(4, 64, 1024)

    last = {}

    def scatter(t):
        st = colours()
        with_half = {1: (2, -1), -1: (1, 0)}
        for s in st:
            k = s["k"]
            rs_far[t, k] = term(t, k, step(s["v0"], 2)).astype(BF)
            s["h"], s["w"], s["uw"] = {}, {}, {}
            for i in range(2):
                for n in (1, -1):
                    off = with_half[n][i]
                    u = step(s["u0"], off)
                    s["h"][off] = go(rs_far.at[t, k, u], rs_half.at[t, k, u], s["to_v"](n))
        yield

        def piece(s, n, off):
            k, u, j = s["k"], step(s["u0"], off), 0 if n == 1 else 1
            p = rs_p[k, j, u]
            if off in with_half[n]:
                s["h"][off].wait_recv()
                p = p + rs_half[t, k, u].astype(F32)
            rs_full[t, k, j, u] = p.astype(BF)
            s["w"][n, off] = go(rs_full.at[t, k, j, u], rs_in.at[t, k, j, u], s["to_v"](n))

        for n, off in ((-1, 2), (1, 1)):
            for s in st:
                rs_p[s["k"], 0 if n == 1 else 1] = term(t, s["k"], step(s["v0"], n))
                piece(s, n, off)
        yield
        for n, off in ((-1, -1), (1, 2)):
            for s in st:
                piece(s, n, off)
        yield
        for n, off in ((-1, 1), (1, -1)):
            for s in st:
                piece(s, n, off)
        for s in st:
            rs_p[s["k"], 2] = term(t, s["k"], s["v0"])
        yield

        def summed(s, off):
            k, u = s["k"], step(s["u0"], off)
            s["w"][1, off].wait_recv()
            s["w"][-1, off].wait_recv()
            return rs_p[k, 2, u] + rs_in[t, k, 0, u].astype(F32) + rs_in[t, k, 1, u].astype(F32)

        for s in st:
            k = s["k"]
            ru_far[t, k] = summed(s, 2).astype(BF)
            s["uh"] = {
                n: go(
                    ru_far.at[t, k, pl.ds(0 if n == 1 else 32, 32)],
                    ru_half.at[t, k, 0 if n == 1 else 1],
                    s["to_u"](n),
                )
                for n in (1, -1)
            }
        for s in st:
            for n in (1, -1):
                piece(s, n, 0)
        yield
        for n in (-1, 1):
            for s in st:
                k, j = s["k"], 0 if n == 1 else 1
                p = summed(s, n)
                s["uh"][n].wait_recv()
                extra = ru_half[t, k, j].astype(F32)
                lo, hi = p[0:32], p[32:64]
                if n == 1:
                    lo = lo + extra
                else:
                    hi = hi + extra
                ru_full[t, k, j, 0:32] = lo.astype(BF)
                ru_full[t, k, j, 32:64] = hi.astype(BF)
                s["uw"][n] = go(ru_full.at[t, k, j], ru_in.at[t, k, j], s["to_u"](n))
        yield
        for s in st:
            k = s["k"]
            r = summed(s, 0)
            s["uw"][1].wait_recv()
            s["uw"][-1].wait_recv()
            r = r + ru_in[t, k, 0].astype(F32) + ru_in[t, k, 1].astype(F32)
            rfin[t, k] = r.astype(BF).reshape(8, 8, 1024)
            last[t] = last.get(t, []) + [
                go(rfin.at[t, k, qq], e_buf.at[t, k, q], dev(xi, zi, qq)) for qq in far_first
            ]
        for k in range(2):
            e_buf[t, k, q] = rfin[t, k, q]
        yield

    ones = jnp.ones((8, 512), BF)

    def grad_in_tiles(k, lo, hi):
        def win_tile(j, _):
            lanes = pl.ds(pl.multiple_of(j * 256, 256), 256)
            ft = k * 4 + j
            a = gx[k, :, :, :, lanes].reshape(1024, 256)
            raw = dot_tn(a, dpre[...].reshape(1024, 512))
            rows = pl.ds(pl.multiple_of(ft * 256, 256), 256)
            gw1[rows] = (raw * min_ref[pl.ds(ft, 1)]).astype(BF)
            p = raw * win[rows].astype(F32)
            hi = p.astype(BF)
            lo = (p - hi.astype(F32)).astype(BF)
            s = dot_nt(ones, hi) + dot_nt(ones, lo)
            s_x[xi, pl.ds(2 * ft, 1)] = s[0:1, :128]
            s_x[xi, pl.ds(2 * ft + 1, 1)] = s[0:1, 128:]
            return 0

        lax.fori_loop(lo, hi, win_tile, 0)

    def grad_out_tiles(k, lo, hi):
        def wout_tile(j, _):
            lanes = pl.ds(pl.multiple_of(j * 256, 256), 256)
            b = gg[k, :, :, :, lanes].reshape(1024, 256)
            raw = dot_tn(act[...].reshape(1024, 512), b)
            cols = pl.ds(pl.multiple_of(k * 1024 + j * 256, 256), 256)
            for h in range(2):
                gw2[h * 256 : (h + 1) * 256, cols] = (
                    raw[h * 256 : (h + 1) * 256] * mout_ref[h : h + 1, cols]
                ).astype(BF)
            return 0

        lax.fori_loop(lo, hi, wout_tile, 0)

    drain(gen_x, 1)
    c0g += column_in(
        lambda i: og_ref.at[:, pl.ds(pl.multiple_of(i * 1024, 1024), 1024)], s0g
    )
    for k in range(2):
        s0g[k, q] = og_ref[:, pl.ds(pl.multiple_of((row * 2 + k) * 1024, 1024), 1024)]
    lane = lax.broadcasted_iota(jnp.int32, (16, 64), 1)
    tile = lax.broadcasted_iota(jnp.int32, (16, 128), 1) + row * 8
    for h in range(2):
        rows = jnp.max(jnp.where(lane == col * 2 + h, pin_ref[...], -1), axis=1, keepdims=True)
        kept = jnp.max(jnp.where(rows == tile, 1.0, 0.0), axis=0, keepdims=True)
        for t in range(8):
            min_ref[t : t + 1, h * 256 : (h + 1) * 256] = jnp.broadcast_to(
                kept[:, t : t + 1], (1, 256)
            )
    w_in_copy.wait()
    for t in range(8):
        win[t * 256 : (t + 1) * 256] = win[t * 256 : (t + 1) * 256] * min_ref[t : t + 1].astype(BF)
    drain(gen_x, 7)
    drain(gen_g, 1)
    pout = pout_ref[pl.ds(pl.multiple_of(row * 8, 8), 8), :]
    for h in range(2):
        kept = jnp.max(jnp.where(pout == col * 2 + h, 1.0, 0.0), axis=1, keepdims=True)
        for t in range(8):
            mout_ref[h : h + 1, t * 256 : (t + 1) * 256] = jnp.broadcast_to(
                kept[t : t + 1], (1, 256)
            )
    w_out_copy.wait()
    for t in range(2):
        wout[t * 256 : (t + 1) * 256] = wout[t * 256 : (t + 1) * 256] * mout_ref[t : t + 1].astype(BF)
    drain(gen_x, 2)
    ca0 = row_other(0, 0)
    row_mine(0, 0)
    drain(gen_g, 2)
    cb0 = row_add(0, 0, ca0)
    drain(gen_x, 2)
    ca1 = row_other(0, 1)
    drain(gen_g, 1)
    row_mine(0, 1)
    cb1 = row_add(0, 1, ca1)
    drain(gen_g, 2)
    cc0 = row_act(0, cb0)
    drain(gen_g, 1)
    cc1 = row_act(1, cb1)
    drain(gen_g, 1)
    cc0.wait_recv()
    cc1.wait_recv()
    gen_o = scatter(0)
    drain(gen_o, 1)
    drain(gen_g, 2)
    da0 = row_other(1, 0)
    row_mine(1, 0)
    db0 = row_add(1, 0, da0)
    drain(gen_o, 1)
    drain(gen_g, 2)
    da1 = row_other(1, 1)
    row_mine(1, 1)
    db1 = row_add(1, 1, da1)
    drain(gen_o, 2)
    grad_out_tiles(0, 0, 2)
    dc0 = row_dpre(0, db0)
    drain(gen_o, 1)
    grad_out_tiles(0, 2, 4)
    grad_out_tiles(1, 0, 2)
    drain(gen_o, 1)
    dc1 = row_dpre(1, db1)
    grad_out_tiles(1, 2, 4)
    dc0.wait_recv()
    dc1.wait_recv()
    gen_d = scatter(1)
    drain(gen_d, 1)
    grad_in_tiles(0, 0, 2)
    drain(gen_o, 1)
    drain(gen_d, 1)
    grad_in_tiles(0, 2, 3)
    drain(gen_d, 1)
    grad_in_tiles(0, 3, 4)
    drain(gen_d, 1)
    grad_in_tiles(1, 0, 4)
    sx = [go(s_x.at[xi], s_x.at[xi], dev(step(xi, n), zi, q)) for n in (1, 2, 3)]
    drain(gen_d, 1)
    for c in last[0]:
        c.wait_recv()
    for r, k in SLICES:
        f = slice(r * 2048 + k * 1024, r * 2048 + (k + 1) * 1024)
        o = e_buf[0, k, 2 * r].astype(F32) + e_buf[0, k, 2 * r + 1].astype(F32)
        out_ref[:, f] = (x_ref[:, f].astype(F32) + o).astype(BF)
    drain(gen_d, 1)
    for c in sx:
        c.wait_recv()
    s_z[zi] = (s_x[0] + s_x[1]) + (s_x[2] + s_x[3])
    sz = [go(s_z.at[zi], s_z.at[zi], dev(xi, step(zi, n), q)) for n in (1, 2, 3)]
    for c in sz:
        c.wait_recv()
    s_c[q] = (s_z[0] + s_z[1]) + (s_z[2] + s_z[3])
    sc = [go(s_c.at[q], s_c.at[q], dev(xi, zi, qq)) for qq in far_first]
    xf = x_ref[...].astype(F32)
    cen = xf - jnp.mean(xf, axis=1, keepdims=True)
    inv = lax.rsqrt(jnp.mean(cen * cen, axis=1, keepdims=True) + 1e-05)
    hat = cen * inv
    drain(gen_d, 1)
    for c in sc:
        c.wait_recv()
    for r in range(4):
        gg_ref[r * 16 : (r + 1) * 16] = (s_c[2 * r] + s_c[2 * r + 1]) / gain64_ref[r * 16 : (r + 1) * 16]
    for c in last[1]:
        c.wait_recv()
    parts = [
        e_buf[1, k, 2 * r].astype(F32) + e_buf[1, k, 2 * r + 1].astype(F32) for r, k in SLICES
    ]
    d = jnp.concatenate(parts, axis=1)
    g = d * gain_ref[...]
    back = inv * (
        g - jnp.mean(g, axis=1, keepdims=True) - hat * jnp.mean(g * hat, axis=1, keepdims=True)
    )
    gin_ref[...] = (og_ref[...].astype(F32) + back).astype(BF)
    finish()


def hand_over(n, *refs):
    ins, outs, sem = refs[:n], refs[n : 2 * n], refs[2 * n]
    moves = [pltpu.make_async_copy(a, o, sem.at[i]) for i, (a, o) in enumerate(zip(ins, outs))]
    for m in moves:
        m.start()
    for m in moves:
        m.wait()


def shards(inputs, layer_norm_gain, w_in, w_out, pattern_in, pattern_out, out_grad):
    vm = functools.partial(pl.BlockSpec, memory_space=pltpu.VMEM)
    hbm = functools.partial(pl.BlockSpec, memory_space=pl.ANY)
    V = pltpu.VMEM
    out = pl.pallas_call(
        kernel,
        out_shape=(
            jax.ShapeDtypeStruct((8, 8192), BF),
            jax.ShapeDtypeStruct((8, 8192), BF),
            jax.ShapeDtypeStruct((2048, 512), BF),
            jax.ShapeDtypeStruct((512, 2048), BF),
            jax.ShapeDtypeStruct((64, 128), F32),
        ),
        in_specs=[pl.BlockSpec(memory_space=pltpu.HBM)] * 8,
        out_specs=(vm(),) * 5,
        scratch_shapes=[
            V((8, 8192), BF),
            V((1, 8192), F32),
            V((64, 128), F32),
            V((8, 8192), BF),
            V((16, 64), jnp.int32),
            V((32, 32), jnp.int32),
            V((2048, 512), BF),
            V((512, 2048), BF),
            V((8, 512), F32),
            V((2, 2048), F32),
            V((8, 8, 1024), BF),
            V((2, 8, 8, 1024), BF),
            V((2, 8, 8, 1024), BF),
            V((2, 4, 4, 64, 1024), BF),
            V((2, 4, 4, 64, 1024), BF),
            V((2, 2, 256, 512), BF),
            V((2, 2, 256, 512), BF),
            V((2, 2, 256, 512), BF),
            V((2, 2, 256, 512), BF),
            V((2, 2, 256, 512), F32),
            V((4, 4, 64, 512), BF),
            V((4, 4, 64, 512), BF),
            V((2, 2, 4, 64, 1024), BF),
            V((2, 2, 4, 64, 1024), BF),
            V((2, 2, 2, 4, 64, 1024), BF),
            V((2, 2, 2, 4, 64, 1024), BF),
            V((2, 3, 4, 64, 1024), F32),
            V((2, 2, 64, 1024), BF),
            V((2, 2, 2, 32, 1024), BF),
            V((2, 2, 2, 64, 1024), BF),
            V((2, 2, 2, 64, 1024), BF),
            V((2, 2, 8, 8, 1024), BF),
            V((2, 2, 8, 8, 1024), BF),
            V((4, 16, 128), F32),
            V((4, 16, 128), F32),
            V((8, 16, 128), F32),
            pltpu.SemaphoreType.DMA((N_COPIES,)),
            pltpu.SemaphoreType.DMA((N_COPIES,)),
            pltpu.SemaphoreType.DMA((8,)),
        ],
        compiler_params=pltpu.CompilerParams(
            collective_id=0, has_side_effects=True, vmem_limit_bytes=48 << 20
        ),
        name="ffn",
    )(
        *(
            pltpu.with_memory_space_constraint(a, pltpu.HBM)
            for a in (
                inputs, layer_norm_gain.reshape(1, 8192), layer_norm_gain.reshape(64, 128),
                out_grad, w_in, w_out, pattern_in.T, pattern_out,
            )
        )
    )
    output, grad_inputs, g_in, g_out, g_gain = pl.pallas_call(
        functools.partial(hand_over, len(out)),
        out_shape=tuple(jax.ShapeDtypeStruct(o.shape, o.dtype) for o in out),
        in_specs=[vm()] * len(out),
        out_specs=(hbm(),) * len(out),
        scratch_shapes=[pltpu.SemaphoreType.DMA((len(out),))],
        compiler_params=pltpu.CompilerParams(vmem_limit_bytes=8 << 20),
        name="hand_over",
    )(*out)
    return output, grad_inputs, g_in, g_out, g_gain.reshape(8192)


def solution(mesh):
    in_specs = (
        P(("row", "col"), None),
        P(),
        P("row", "col"),
        P("col", "row"),
        P(),
        P(),
        P(("row", "col"), None),
    )
    out_specs = (
        P(("row", "col"), None),
        P(("row", "col"), None),
        P("row", "col"),
        P("col", "row"),
        P(),
    )
    return jax.shard_map(shards, mesh=mesh, in_specs=in_specs, out_specs=out_specs, check_vma=False)
```

```python
import functools

import jax
import jax.numpy as jnp
from jax import lax
from jax.experimental import pallas as pl
from jax.experimental.pallas import tpu as pltpu
from jax.sharding import PartitionSpec as P

BF = jnp.bfloat16
F32 = jnp.float32
N_COPIES = 256
SLICES = tuple((r, k) for r in range(4) for k in range(2))
FAR_FIRST = ((1, 0, 0), (1, 1, 0), (0, 0, 1), (0, 1, 1), (1, 0, 1), (1, 1, 1), (0, 1, 0))


def gelu_value(h):
    inner = 0.7978845608 * (h + 0.044715 * h * h * h)
    return 0.5 * h * (1.0 + jnp.tanh(inner))


def gelu_slope(h):
    tanh_v = jnp.tanh(0.7978845608 * (h + 0.044715 * h * h * h))
    return 0.5 * (1.0 + tanh_v) + 0.5 * h * (1.0 - tanh_v * tanh_v) * 0.7978845608 * (
        1.0 + 0.134145 * h * h
    )


def dot_nn(a, b):
    return lax.dot_general(a, b, (((1,), (0,)), ((), ())), preferred_element_type=F32)


def dot_nt(a, b):
    return lax.dot_general(a, b, (((1,), (1,)), ((), ())), preferred_element_type=F32)


def dot_tn(a, b):
    return lax.dot_general(a, b, (((0,), (0,)), ((), ())), preferred_element_type=F32)


class Sent:
    def __init__(self, c):
        self.c, self.got = c, False
        c.start()

    def wait_recv(self):
        self.got = True
        self.c.wait_recv()


def kernel(
    x_hbm, gain_hbm, gain64_hbm, og_hbm, win_hbm, wout_hbm, pin_hbm, pout_hbm,
    out_ref, gin_ref, gw1, gw2, gg_ref,
    x_ref, gain_ref, gain64_ref, og_ref, pin_ref, pout_ref,
    win, wout, min_ref, mout_ref, normed, s0x, s0g, gx, gg,
    ar_send, ar_recv, ay_send, ay_recv, acc, act, dpre,
    rs_far, rs_half, rs_full, rs_in, rs_p,
    ru_far, ru_half, ru_full, ru_in,
    rfin, e_buf, s_x, s_z, s_c,
    send_sem, recv_sem, w_sem,
):
    row = lax.axis_index("row")
    col = lax.axis_index("col")
    xi, zi, yl = col // 8, (col // 2) % 4, col % 2
    yh, core = row // 2, row % 2
    q = row * 2 + yl

    def dev(x, z, qq):
        return (qq // 2, (x * 4 + z) * 2 + qq % 2)

    sent = []

    def go(src, dst, to):
        i = len(sent)
        c = Sent(
            pltpu.make_async_remote_copy(
                src_ref=src, dst_ref=dst, send_sem=send_sem.at[i], recv_sem=recv_sem.at[i],
                device_id=to, device_id_type=pl.DeviceIdType.MESH,
            )
        )
        sent.append(c)
        return c

    def finish():
        for c in sent:
            if not c.got:
                c.wait_recv()
        for c in sent:
            c.c.wait_send()

    def step(i, n):
        return (i + n + 4) % 4

    def flip(h, c, y):
        return (yh + h) % 2 * 4 + (core + c) % 2 * 2 + (yl + y) % 2

    sibling = (yh * 2 + (1 - core), col)
    partner = ((1 - yh) * 2 + core, col)

    far_first = [flip(h, c, y) for h, c, y in FAR_FIRST]

    loads = [
        pltpu.make_async_copy(a, b, w_sem.at[i])
        for i, (a, b) in enumerate(
            (
                (x_hbm, x_ref),
                (gain_hbm, gain_ref),
                (og_hbm, og_ref),
                (pin_hbm, pin_ref),
                (pout_hbm, pout_ref),
                (gain64_hbm, gain64_ref),
                (win_hbm, win),
                (wout_hbm, wout),
            )
        )
    ]
    for c in loads:
        c.start()
    w_in_copy, w_out_copy = loads[6:]

    barrier = pltpu.get_barrier_semaphore()
    peers = [dev(xi, zi, (q + n) % 8) for n in range(1, 8)]
    peers += [dev(step(xi, n), zi, q) for n in (1, 2, 3)]
    peers += [dev(xi, step(zi, n), q) for n in (1, 2, 3)]
    for p in peers:
        pl.semaphore_signal(barrier, inc=1, device_id=p, device_id_type=pl.DeviceIdType.MESH)


    for c in loads[:2]:
        c.wait()
    xf = x_ref[...].astype(F32)
    cen = xf - jnp.mean(xf, axis=1, keepdims=True)
    inv = lax.rsqrt(jnp.mean(cen * cen, axis=1, keepdims=True) + 1e-05)
    nrm = (cen * inv * gain_ref[...]).astype(BF)
    for r in range(8):
        normed[r] = nrm[:, r * 1024 : (r + 1) * 1024]
    pl.semaphore_wait(barrier, len(peers))

    def column_in(src_of, dst):
        return [
            [go(src_of(qq // 2 * 2 + k), dst.at[k, q], dev(xi, zi, qq)) for qq in far_first]
            for k in range(2)
        ]

    c0x = column_in(lambda i: normed.at[i], s0x)
    for k in range(2):
        s0x[k, q] = normed[row * 2 + k]
    for c in loads[2:6]:
        c.wait()

    def blk(g, k, u, v):
        return g.at[0, v, u] if k == 0 else g.at[1, u, v]

    def colours():
        st = []
        for k in range(2):
            u0, v0 = (zi, xi) if k == 0 else (xi, zi)

            def to_z(n):
                return dev(xi, step(zi, n), q)

            def to_x(n):
                return dev(step(xi, n), zi, q)

            st.append(
                dict(
                    k=k, u0=u0, v0=v0, to_u=to_z if k == 0 else to_x, to_v=to_x if k == 0 else to_z
                )
            )
        return st

    def gather(s0, g, arrived):
        st = colours()

        def one(s, off, n, v=None):
            b = blk(g, s["k"], step(s["u0"], off), s["v0"] if v is None else v)
            return go(b, b, s["to_v"](n))

        def both(s, off):
            s["s", off] = {n: one(s, off, n) for n in (1, -1)}

        for s in st:
            for c in arrived[s["k"]]:
                c.wait_recv()
            g[s["k"], xi, zi] = s0[s["k"]].reshape(64, 1024)
            b = blk(g, s["k"], s["u0"], s["v0"])
            s["f"] = {n: go(b, b, s["to_u"](n)) for n in (1, -1)}
            s["f2"], s["s2"] = {}, {}
        for s in st:
            both(s, 0)
        yield
        for n in (1, -1):
            for s in st:
                s["f"][n].wait_recv()
                b = blk(g, s["k"], step(s["u0"], -n), s["v0"])
                part = b.at[pl.ds(0, 32)] if n == 1 else b.at[pl.ds(32, 32)]
                s["f2"][n] = go(part, part, s["to_u"](n))
                both(s, -n)
            yield

        def relay(s, off, n):
            s["s", off][n].wait_recv()
            s["s2"][off] = one(s, off, n, step(s["v0"], -n))

        for s in st:
            relay(s, 0, 1)
        yield
        for s in st:
            s["f2"][1].wait_recv()
            s["f2"][-1].wait_recv()
            both(s, 2)
        for s in st:
            s["s", 0][-1].wait_recv()
        yield
        for off in (-1, 1, 2):
            n = 1 if off == 1 else -1
            for s in st:
                relay(s, off, n)
            for s in st:
                s["s", off][-n].wait_recv()
            yield
        for off in (0, -1, 1, 2):
            for s in st:
                s["s2"][off].wait_recv()
            yield

    def drain(g, n):
        for _ in range(n):
            next(g, None)

    gen_x = gather(s0x, gx, c0x)
    c0g = []
    gen_g = gather(s0g, gg, c0g)

    def partial(g, w, nt, xx):
        a = g[0, xx].reshape(256, 1024)
        b = g[1, xx].reshape(256, 1024)
        if nt:
            return dot_nt(a, w[:, :1024]) + dot_nt(b, w[:, 1024:])
        return dot_nn(a, w[:1024]) + dot_nn(b, w[1024:])

    def x_of(p, mine):
        c = core if mine else 1 - core
        return (xi + (4 - c if p == 0 else 1 + c)) % 4

    side = ((gx, win, False), (gg, wout, True))

    def row_other(i, p):
        ar_send[i, p] = partial(*side[i], x_of(p, False)).astype(BF)
        return go(ar_send.at[i, p], ar_recv.at[i, p], sibling)

    def row_mine(i, p):
        acc[i, p] = partial(*side[i], x_of(p, True))

    def row_add(i, p, c):
        c.wait_recv()
        v = acc[i, p] + ar_recv[i, p].astype(F32)
        acc[i, p] = v
        ay_send[i, p] = v.astype(BF)
        return go(ay_send.at[i, p], ay_recv.at[i, p], partner)

    def rows_loop(f):
        def body(m, _):
            f(m, pl.ds(pl.multiple_of(m * 64, 64), 64))
            return 0

        lax.fori_loop(0, 4, body, 0)

    def row_act(p, c):
        c.wait_recv()
        xx = x_of(p, True)

        def rows_of(m, rows):
            pre = acc[0, p, rows] + ay_recv[0, p, rows].astype(F32)
            acc[0, p, rows] = pre
            act[xx, m] = gelu_value(pre).astype(BF)

        rows_loop(rows_of)
        return go(act.at[xx], act.at[xx], sibling)

    def row_dpre(p, c):
        c.wait_recv()
        xx = x_of(p, True)

        def rows_of(m, rows):
            d = acc[1, p, rows] + ay_recv[1, p, rows].astype(F32)
            dpre[xx, m] = (d * gelu_slope(acc[0, p, rows])).astype(BF)

        rows_loop(rows_of)
        return go(dpre.at[xx], dpre.at[xx], sibling)

    def term(t, k, v):
        if t == 0:
            a = act[v] if k == 0 else act[:, v]
            r = dot_nn(a.reshape(256, 512), wout[:, k * 1024 : (k + 1) * 1024])
        else:
            a = dpre[v] if k == 0 else dpre[:, v]
            r = dot_nt(a.reshape(256, 512), win[k * 1024 : (k + 1) * 1024, :])
        return r.reshape(4, 64, 1024)

    last = {}

    def scatter(t):
        st = colours()
        with_half = {1: (2, -1), -1: (1, 0)}
        for s in st:
            k = s["k"]
            rs_far[t, k] = term(t, k, step(s["v0"], 2)).astype(BF)
            s["h"], s["w"], s["uw"] = {}, {}, {}
            for i in range(2):
                for n in (1, -1):
                    off = with_half[n][i]
                    u = step(s["u0"], off)
                    s["h"][off] = go(rs_far.at[t, k, u], rs_half.at[t, k, u], s["to_v"](n))
        yield

        def piece(s, n, off):
            k, u, j = s["k"], step(s["u0"], off), 0 if n == 1 else 1
            p = rs_p[k, j, u]
            if off in with_half[n]:
                s["h"][off].wait_recv()
                p = p + rs_half[t, k, u].astype(F32)
            rs_full[t, k, j, u] = p.astype(BF)
            s["w"][n, off] = go(rs_full.at[t, k, j, u], rs_in.at[t, k, j, u], s["to_v"](n))

        for n, off in ((-1, 2), (1, 1)):
            for s in st:
                rs_p[s["k"], 0 if n == 1 else 1] = term(t, s["k"], step(s["v0"], n))
                piece(s, n, off)
        yield
        for n, off in ((-1, -1), (1, 2)):
            for s in st:
                piece(s, n, off)
        yield
        for n, off in ((-1, 1), (1, -1)):
            for s in st:
                piece(s, n, off)
        for s in st:
            rs_p[s["k"], 2] = term(t, s["k"], s["v0"])
        yield

        def summed(s, off):
            k, u = s["k"], step(s["u0"], off)
            s["w"][1, off].wait_recv()
            s["w"][-1, off].wait_recv()
            return rs_p[k, 2, u] + rs_in[t, k, 0, u].astype(F32) + rs_in[t, k, 1, u].astype(F32)

        for s in st:
            k = s["k"]
            ru_far[t, k] = summed(s, 2).astype(BF)
            s["uh"] = {
                n: go(
                    ru_far.at[t, k, pl.ds(0 if n == 1 else 32, 32)],
                    ru_half.at[t, k, 0 if n == 1 else 1],
                    s["to_u"](n),
                )
                for n in (1, -1)
            }
        for s in st:
            for n in (1, -1):
                piece(s, n, 0)
        yield
        for n in (-1, 1):
            for s in st:
                k, j = s["k"], 0 if n == 1 else 1
                p = summed(s, n)
                s["uh"][n].wait_recv()
                extra = ru_half[t, k, j].astype(F32)
                lo, hi = p[0:32], p[32:64]
                if n == 1:
                    lo = lo + extra
                else:
                    hi = hi + extra
                ru_full[t, k, j, 0:32] = lo.astype(BF)
                ru_full[t, k, j, 32:64] = hi.astype(BF)
                s["uw"][n] = go(ru_full.at[t, k, j], ru_in.at[t, k, j], s["to_u"](n))
        yield
        for s in st:
            k = s["k"]
            r = summed(s, 0)
            s["uw"][1].wait_recv()
            s["uw"][-1].wait_recv()
            r = r + ru_in[t, k, 0].astype(F32) + ru_in[t, k, 1].astype(F32)
            rfin[t, k] = r.astype(BF).reshape(8, 8, 1024)
            last[t] = last.get(t, []) + [
                go(rfin.at[t, k, qq], e_buf.at[t, k, q], dev(xi, zi, qq)) for qq in far_first
            ]
        for k in range(2):
            e_buf[t, k, q] = rfin[t, k, q]
        yield

    ones = jnp.ones((8, 512), BF)

    def grad_in_tiles(k, lo, hi):
        def win_tile(j, _):
            lanes = pl.ds(pl.multiple_of(j * 256, 256), 256)
            ft = k * 4 + j
            a = gx[k, :, :, :, lanes].reshape(1024, 256)
            raw = dot_tn(a, dpre[...].reshape(1024, 512))
            rows = pl.ds(pl.multiple_of(ft * 256, 256), 256)
            gw1[rows] = (raw * min_ref[pl.ds(ft, 1)]).astype(BF)
            p = raw * win[rows].astype(F32)
            hi = p.astype(BF)
            lo = (p - hi.astype(F32)).astype(BF)
            s = dot_nt(ones, hi) + dot_nt(ones, lo)
            s_x[xi, pl.ds(2 * ft, 1)] = s[0:1, :128]
            s_x[xi, pl.ds(2 * ft + 1, 1)] = s[0:1, 128:]
            return 0

        lax.fori_loop(lo, hi, win_tile, 0)

    def grad_out_tiles(k, lo, hi):
        def wout_tile(j, _):
            lanes = pl.ds(pl.multiple_of(j * 256, 256), 256)
            b = gg[k, :, :, :, lanes].reshape(1024, 256)
            raw = dot_tn(act[...].reshape(1024, 512), b)
            cols = pl.ds(pl.multiple_of(k * 1024 + j * 256, 256), 256)
            for h in range(2):
                gw2[h * 256 : (h + 1) * 256, cols] = (
                    raw[h * 256 : (h + 1) * 256] * mout_ref[h : h + 1, cols]
                ).astype(BF)
            return 0

        lax.fori_loop(lo, hi, wout_tile, 0)

    drain(gen_x, 1)
    c0g += column_in(
        lambda i: og_ref.at[:, pl.ds(pl.multiple_of(i * 1024, 1024), 1024)], s0g
    )
    for k in range(2):
        s0g[k, q] = og_ref[:, pl.ds(pl.multiple_of((row * 2 + k) * 1024, 1024), 1024)]
    lane = lax.broadcasted_iota(jnp.int32, (16, 64), 1)
    tile = lax.broadcasted_iota(jnp.int32, (16, 128), 1) + row * 8
    for h in range(2):
        rows = jnp.max(jnp.where(lane == col * 2 + h, pin_ref[...], -1), axis=1, keepdims=True)
        kept = jnp.max(jnp.where(rows == tile, 1.0, 0.0), axis=0, keepdims=True)
        for t in range(8):
            min_ref[t : t + 1, h * 256 : (h + 1) * 256] = jnp.broadcast_to(
                kept[:, t : t + 1], (1, 256)
            )
    w_in_copy.wait()
    for t in range(8):
        win[t * 256 : (t + 1) * 256] = win[t * 256 : (t + 1) * 256] * min_ref[t : t + 1].astype(BF)
    drain(gen_x, 7)
    drain(gen_g, 1)
    pout = pout_ref[pl.ds(pl.multiple_of(row * 8, 8), 8), :]
    for h in range(2):
        kept = jnp.max(jnp.where(pout == col * 2 + h, 1.0, 0.0), axis=1, keepdims=True)
        for t in range(8):
            mout_ref[h : h + 1, t * 256 : (t + 1) * 256] = jnp.broadcast_to(
                kept[t : t + 1], (1, 256)
            )
    w_out_copy.wait()
    for t in range(2):
        wout[t * 256 : (t + 1) * 256] = wout[t * 256 : (t + 1) * 256] * mout_ref[t : t + 1].astype(BF)
    drain(gen_x, 2)
    ca0 = row_other(0, 0)
    row_mine(0, 0)
    drain(gen_g, 2)
    cb0 = row_add(0, 0, ca0)
    drain(gen_x, 2)
    ca1 = row_other(0, 1)
    drain(gen_g, 1)
    row_mine(0, 1)
    cb1 = row_add(0, 1, ca1)
    drain(gen_g, 2)
    cc0 = row_act(0, cb0)
    drain(gen_g, 1)
    cc1 = row_act(1, cb1)
    drain(gen_g, 1)
    cc0.wait_recv()
    cc1.wait_recv()
    gen_o = scatter(0)
    drain(gen_o, 1)
    drain(gen_g, 2)
    da0 = row_other(1, 0)
    row_mine(1, 0)
    db0 = row_add(1, 0, da0)
    drain(gen_o, 1)
    drain(gen_g, 2)
    da1 = row_other(1, 1)
    row_mine(1, 1)
    db1 = row_add(1, 1, da1)
    drain(gen_o, 2)
    grad_out_tiles(0, 0, 2)
    dc0 = row_dpre(0, db0)
    drain(gen_o, 1)
    grad_out_tiles(0, 2, 4)
    grad_out_tiles(1, 0, 2)
    drain(gen_o, 1)
    dc1 = row_dpre(1, db1)
    grad_out_tiles(1, 2, 4)
    dc0.wait_recv()
    dc1.wait_recv()
    gen_d = scatter(1)
    drain(gen_d, 1)
    grad_in_tiles(0, 0, 2)
    drain(gen_o, 1)
    drain(gen_d, 1)
    grad_in_tiles(0, 2, 3)
    drain(gen_d, 1)
    grad_in_tiles(0, 3, 4)
    drain(gen_d, 1)
    grad_in_tiles(1, 0, 4)
    sx = [go(s_x.at[xi], s_x.at[xi], dev(step(xi, n), zi, q)) for n in (1, 2, 3)]
    drain(gen_d, 1)
    for c in last[0]:
        c.wait_recv()
    for r, k in SLICES:
        f = slice(r * 2048 + k * 1024, r * 2048 + (k + 1) * 1024)
        o = e_buf[0, k, 2 * r].astype(F32) + e_buf[0, k, 2 * r + 1].astype(F32)
        out_ref[:, f] = (x_ref[:, f].astype(F32) + o).astype(BF)
    drain(gen_d, 1)
    for c in sx:
        c.wait_recv()
    s_z[zi] = (s_x[0] + s_x[1]) + (s_x[2] + s_x[3])
    sz = [go(s_z.at[zi], s_z.at[zi], dev(xi, step(zi, n), q)) for n in (1, 2, 3)]
    for c in sz:
        c.wait_recv()
    s_c[q] = (s_z[0] + s_z[1]) + (s_z[2] + s_z[3])
    sc = [go(s_c.at[q], s_c.at[q], dev(xi, zi, qq)) for qq in far_first]
    xf = x_ref[...].astype(F32)
    cen = xf - jnp.mean(xf, axis=1, keepdims=True)
    inv = lax.rsqrt(jnp.mean(cen * cen, axis=1, keepdims=True) + 1e-05)
    hat = cen * inv
    drain(gen_d, 1)
    for c in sc:
        c.wait_recv()
    for r in range(4):
        gg_ref[r * 16 : (r + 1) * 16] = (s_c[2 * r] + s_c[2 * r + 1]) / gain64_ref[r * 16 : (r + 1) * 16]
    for c in last[1]:
        c.wait_recv()
    parts = [
        e_buf[1, k, 2 * r].astype(F32) + e_buf[1, k, 2 * r + 1].astype(F32) for r, k in SLICES
    ]
    d = jnp.concatenate(parts, axis=1)
    g = d * gain_ref[...]
    back = inv * (
        g - jnp.mean(g, axis=1, keepdims=True) - hat * jnp.mean(g * hat, axis=1, keepdims=True)
    )
    gin_ref[...] = (og_ref[...].astype(F32) + back).astype(BF)
    finish()


def hand_over(n, *refs):
    ins, outs, sem = refs[:n], refs[n : 2 * n], refs[2 * n]
    moves = [pltpu.make_async_copy(a, o, sem.at[i]) for i, (a, o) in enumerate(zip(ins, outs))]
    for m in moves:
        m.start()
    for m in moves:
        m.wait()


def shards(inputs, layer_norm_gain, w_in, w_out, pattern_in, pattern_out, out_grad):
    vm = functools.partial(pl.BlockSpec, memory_space=pltpu.VMEM)
    hbm = functools.partial(pl.BlockSpec, memory_space=pl.ANY)
    V = pltpu.VMEM
    out = pl.pallas_call(
        kernel,
        out_shape=(
            jax.ShapeDtypeStruct((8, 8192), BF),
            jax.ShapeDtypeStruct((8, 8192), BF),
            jax.ShapeDtypeStruct((2048, 512), BF),
            jax.ShapeDtypeStruct((512, 2048), BF),
            jax.ShapeDtypeStruct((64, 128), F32),
        ),
        in_specs=[pl.BlockSpec(memory_space=pltpu.HBM)] * 8,
        out_specs=(vm(),) * 5,
        scratch_shapes=[
            V((8, 8192), BF),
            V((1, 8192), F32),
            V((64, 128), F32),
            V((8, 8192), BF),
            V((16, 64), jnp.int32),
            V((32, 32), jnp.int32),
            V((2048, 512), BF),
            V((512, 2048), BF),
            V((8, 512), F32),
            V((2, 2048), F32),
            V((8, 8, 1024), BF),
            V((2, 8, 8, 1024), BF),
            V((2, 8, 8, 1024), BF),
            V((2, 4, 4, 64, 1024), BF),
            V((2, 4, 4, 64, 1024), BF),
            V((2, 2, 256, 512), BF),
            V((2, 2, 256, 512), BF),
            V((2, 2, 256, 512), BF),
            V((2, 2, 256, 512), BF),
            V((2, 2, 256, 512), F32),
            V((4, 4, 64, 512), BF),
            V((4, 4, 64, 512), BF),
            V((2, 2, 4, 64, 1024), BF),
            V((2, 2, 4, 64, 1024), BF),
            V((2, 2, 2, 4, 64, 1024), BF),
            V((2, 2, 2, 4, 64, 1024), BF),
            V((2, 3, 4, 64, 1024), F32),
            V((2, 2, 64, 1024), BF),
            V((2, 2, 2, 32, 1024), BF),
            V((2, 2, 2, 64, 1024), BF),
            V((2, 2, 2, 64, 1024), BF),
            V((2, 2, 8, 8, 1024), BF),
            V((2, 2, 8, 8, 1024), BF),
            V((4, 16, 128), F32),
            V((4, 16, 128), F32),
            V((8, 16, 128), F32),
            pltpu.SemaphoreType.DMA((N_COPIES,)),
            pltpu.SemaphoreType.DMA((N_COPIES,)),
            pltpu.SemaphoreType.DMA((8,)),
        ],
        compiler_params=pltpu.CompilerParams(
            collective_id=0, has_side_effects=True, vmem_limit_bytes=48 << 20
        ),
        name="ffn",
    )(
        *(
            pltpu.with_memory_space_constraint(a, pltpu.HBM)
            for a in (
                inputs, layer_norm_gain.reshape(1, 8192), layer_norm_gain.reshape(64, 128),
                out_grad, w_in, w_out, pattern_in.T, pattern_out,
            )
        )
    )
    output, grad_inputs, g_in, g_out, g_gain = pl.pallas_call(
        functools.partial(hand_over, len(out)),
        out_shape=tuple(jax.ShapeDtypeStruct(o.shape, o.dtype) for o in out),
        in_specs=[vm()] * len(out),
        out_specs=(hbm(),) * len(out),
        scratch_shapes=[pltpu.SemaphoreType.DMA((len(out),))],
        compiler_params=pltpu.CompilerParams(vmem_limit_bytes=8 << 20),
        name="hand_over",
    )(*out)
    return output, grad_inputs, g_in, g_out, g_gain.reshape(8192)


def solution(mesh):
    in_specs = (
        P(("row", "col"), None),
        P(),
        P("row", "col"),
        P("col", "row"),
        P(),
        P(),
        P(("row", "col"), None),
    )
    out_specs = (
        P(("row", "col"), None),
        P(("row", "col"), None),
        P("row", "col"),
        P("col", "row"),
        P(),
    )
    return jax.shard_map(shards, mesh=mesh, in_specs=in_specs, out_specs=out_specs, check_vma=False)
```
